32 devices in a mesh: grp: 2 (over core), ty: 4 (over y, x), tx: 4 (over z).
Axes of the slice: x: 2, y: 2, z: 4, core: 2. Of those that a mesh axis runs over, the one named last changes fastest.
Arguments:
- coupled_state: float32 [2, 23, 32, 8, 512], P('grp', None, None, 'ty', 'tx'), may hold values from -4 to 4, as said below
- land_mask: int32 [8, 512], P('ty', 'tx'), may hold values 0 or 1
- bottom_level: int32 [8, 512], P('ty', 'tx'), may hold values from 1 to 32
- shortwave: float32 [8, 512], P('ty', 'tx'), may hold values from 0.5 to 1.5
- absorb: float32 [19], replicated, may hold values from 0.01 to 0.1
- reaction: float32 [19, 19], replicated, may hold values from -1.25 to 1.25
Outputs:
- new_state: float32 [2, 23, 32, 8, 512], P('grp', None, None, 'ty', 'tx')
The draws below stay inside these ranges and needn't reach their ends.
Inputs may be any that keep to these rules, and one draw needn't show every extreme that they name: `coupled_state`: fields 0 and 1 lie in -2 to 2, fields 2 and 3 in -4 to 4, the tracers in 0.1 to 2.
All inputs are finite; a program needn't handle non-finite values. No bound on the sum of `land_mask` on one device may be relied on, other than what follows from the above.
Results may differ from the reference program's by a relative error of at most 0.0003.
Values sent between devices are 32-bit elements; how exact they have to be, the bound alone decides.
No kernel may reach another device: no remote copies, remote signals or barrier semaphores. Data moves between devices by JAX's collectives and lax.ppermute only.
A program may use at most 192 MiB of HBM per device.

```python
import math
import jax
import jax.numpy as jnp
from jax import lax

NTR = 19
NZ = 32
STEPS = 2
NX = 8
NY = 512


def draw_coupled_state(key, part):
    flow_key, scalar_key, tracer_key = jax.random.split(jax.random.fold_in(key, 17), 3)
    pair_shape = (2, 2, NZ, NX, NY)
    tracer_shape = (2, NTR, NZ, NX, NY)
    flow = jnp.clip(0.8 * jax.random.normal(flow_key, pair_shape, jnp.float32), -2.0, 2.0)
    scalars = jnp.clip(jax.random.normal(scalar_key, pair_shape, jnp.float32), -4.0, 4.0)
    tracers = jnp.exp(jax.random.uniform(tracer_key, tracer_shape, jnp.float32, math.log(0.1), math.log(2.0)))
    return jnp.concatenate([flow, scalars, tracers], axis=1)


def set_ends(values, own_key, low, high):
    extent = values.shape
    spot = [jax.random.randint(jax.random.fold_in(own_key, axis), (), 0, extent[axis]) for axis in range(len(extent))]
    values = values.at[tuple(spot)].set(low)
    longest = extent.index(max(extent))
    spot[longest] = (spot[longest] + 1) % extent[longest]
    return values.at[tuple(spot)].set(high)


def block_levels(key, extent, cuts, low, high):
    def one(axis_at, blocks):
        draws = jax.random.uniform(jax.random.fold_in(jax.random.fold_in(key, 6), axis_at), (blocks,), jnp.float32, low / len(cuts), high / len(cuts))
        return jnp.repeat(jnp.exp(draws), extent[axis_at] // blocks).reshape((-1,) + (1,) * (len(extent) - axis_at - 1))

    level = one(*cuts[0])
    for cut in cuts[1:]:
        level = level * one(*cut)
    return level


def bell_draw(rng, dims, width, bound, kind=jnp.bfloat16):
    return jnp.clip(width * jax.random.normal(rng, dims, jnp.float32), -bound, bound).astype(kind)


def setup_inputs(seed: int = 0) -> dict:
    splits = jax.random.split(jax.random.key(seed), 7)
    coupled_state = draw_coupled_state(jax.random.fold_in(splits[6], 71), 0)
    land_mask = set_ends((jax.random.randint(splits[1], (NX, NY), 0, 6) < 5).astype(jnp.int32), jax.random.fold_in(splits[1], 1), 0, 1)
    bottom_level = set_ends(jax.random.randint(splits[2], (NX, NY), 1, NZ + 1), jax.random.fold_in(splits[2], 1), 1, NZ).astype(jnp.int32)
    shortwave = jnp.clip(0.5 + 1.0 * jax.random.uniform(splits[3], (NX, NY), jnp.float32) ** block_levels(splits[3], (NX, NY), ((0, 4), (1, 4)), -0.2, 0.2), 0.5, 1.5)
    absorb = jnp.clip(jnp.exp(jax.random.uniform(splits[4], (NTR,), jnp.float32, math.log(0.01), math.log(0.1))), 0.01, 0.1)
    reaction = bell_draw(splits[5], (NTR, NTR), NTR ** -0.5, 1.25, jnp.float32)
    return dict(coupled_state=coupled_state, land_mask=land_mask, bottom_level=bottom_level, shortwave=shortwave, absorb=absorb, reaction=reaction)


integration_interval = 0.1
tracer_step = 0.08
coriolis = 0.8
barotropic_gradient_coefficient = 0.1
water_extinction = 0.04
layer_depth = 0.05
growth_peak = 2.0
half_light = 0.5
ratio_floor = 0.01


def east_of(values):
    zero_rim = jnp.zeros_like(values[..., :1, :])
    return jnp.concatenate([values[..., 1:, :], zero_rim], axis=-2)


def west_of(values):
    zero_rim = jnp.zeros_like(values[..., :1, :])
    return jnp.concatenate([zero_rim, values[..., :-1, :]], axis=-2)


def north_of(values):
    zero_rim = jnp.zeros_like(values[..., :1])
    return jnp.concatenate([values[..., 1:], zero_rim], axis=-1)


def south_of(values):
    zero_rim = jnp.zeros_like(values[..., :1])
    return jnp.concatenate([zero_rim, values[..., :-1]], axis=-1)


def diffusion_stencil(values):
    return east_of(values) + west_of(values) + north_of(values) + south_of(values) - 4.0 * values


def light_field(tracers, absorb, shortwave):
    extinction = water_extinction + jnp.einsum("t,tkxy->kxy", absorb, tracers, precision=lax.Precision.HIGHEST)
    optical = jnp.cumsum(extinction, axis=0) * layer_depth
    light_below = shortwave * jnp.exp(-optical)
    light_above = light_below * jnp.exp(layer_depth * extinction)
    return light_below, light_above


def ocean_update(gridded_quantities, marine_indicator, absorb, shortwave):
    zonal_current, meridional_current, thermal_state, brine_content = gridded_quantities[0], gridded_quantities[1], gridded_quantities[2], gridded_quantities[3]
    hydrostatic_load = jnp.cumsum(-0.2 * thermal_state + 0.8 * brine_content, axis=0) * barotropic_gradient_coefficient
    grad_east = 0.5 * (east_of(hydrostatic_load) - west_of(hydrostatic_load))
    grad_north = 0.5 * (north_of(hydrostatic_load) - south_of(hydrostatic_load))
    zonal_current_later = marine_indicator * (zonal_current + integration_interval * (coriolis * meridional_current - grad_east + diffusion_stencil(zonal_current)))
    meridional_current_later = marine_indicator * (meridional_current + integration_interval * (-coriolis * zonal_current - grad_north + diffusion_stencil(meridional_current)))
    light_below, light_above = light_field(gridded_quantities[4:], absorb, shortwave)
    thermal_forcing = (light_above - light_below) / layer_depth
    thermal_state_later = marine_indicator * (thermal_state + integration_interval * (diffusion_stencil(thermal_state) + thermal_forcing))
    brine_content_later = marine_indicator * (brine_content + integration_interval * diffusion_stencil(brine_content))
    return jnp.stack([zonal_current_later, meridional_current_later, thermal_state_later, brine_content_later])


def tracer_fluxes(gridded_quantities, inside):
    tracers = gridded_quantities[4:]
    face_east = 0.5 * (gridded_quantities[0] + east_of(gridded_quantities[0])) * inside * east_of(inside)
    face_north = 0.5 * (gridded_quantities[1] + north_of(gridded_quantities[1])) * inside * north_of(inside)
    tracer_east = east_of(tracers)
    tracer_north = north_of(tracers)
    low_east = jnp.maximum(face_east, 0.0) * tracers + jnp.minimum(face_east, 0.0) * tracer_east
    low_north = jnp.maximum(face_north, 0.0) * tracers + jnp.minimum(face_north, 0.0) * tracer_north
    anti_east = 0.5 * face_east * (tracers + tracer_east) - low_east
    anti_north = 0.5 * face_north * (tracers + tracer_north) - low_north
    lowered = tracers - tracer_step * (low_east - west_of(low_east) + low_north - south_of(low_north))
    tracer_west = west_of(tracers)
    tracer_south = south_of(tracers)
    bound_up = jnp.maximum(jnp.maximum(jnp.maximum(tracers, tracer_east), jnp.maximum(tracer_west, tracer_north)), tracer_south)
    bound_down = jnp.minimum(jnp.minimum(jnp.minimum(tracers, tracer_east), jnp.minimum(tracer_west, tracer_north)), tracer_south)
    west_anti = west_of(anti_east)
    south_anti = south_of(anti_north)
    gain_in = jnp.maximum(west_anti, 0.0) - jnp.minimum(anti_east, 0.0) + jnp.maximum(south_anti, 0.0) - jnp.minimum(anti_north, 0.0)
    gain_out = jnp.maximum(anti_east, 0.0) - jnp.minimum(west_anti, 0.0) + jnp.maximum(anti_north, 0.0) - jnp.minimum(south_anti, 0.0)
    room_up = jnp.maximum(bound_up - lowered, 0.0) / tracer_step
    room_down = jnp.maximum(lowered - bound_down, 0.0) / tracer_step
    ratio_in = jnp.minimum(gain_in, room_up) / jnp.maximum(gain_in, ratio_floor)
    ratio_out = jnp.minimum(gain_out, room_down) / jnp.maximum(gain_out, ratio_floor)
    return lowered, anti_east, anti_north, jnp.stack([ratio_in, ratio_out])


def tracer_finish(gridded_quantities, lowered, anti_east, anti_north, ratios, marine_indicator, absorb, shortwave, reaction):
    ratio_in, ratio_out = ratios[0], ratios[1]
    limit_east = jnp.where(anti_east >= 0.0, jnp.minimum(east_of(ratio_in), ratio_out), jnp.minimum(ratio_in, east_of(ratio_out)))
    limit_north = jnp.where(anti_north >= 0.0, jnp.minimum(north_of(ratio_in), ratio_out), jnp.minimum(ratio_in, north_of(ratio_out)))
    flux_east = limit_east * anti_east
    flux_north = limit_north * anti_north
    advected = lowered - tracer_step * (flux_east - west_of(flux_east) + flux_north - south_of(flux_north))
    light_below, light_above = light_field(advected, absorb, shortwave)
    growth = growth_peak * jnp.exp(0.063 * gridded_quantities[2]) * light_below / (light_below + half_light) * (1.0 + 0.2 * jnp.tanh(gridded_quantities[3]))
    mixed_terms = jnp.einsum("st,tkxy->skxy", reaction, advected, precision=lax.Precision.HIGHEST)
    return marine_indicator * (advected + tracer_step * growth * mixed_terms)


def reference(coupled_state, land_mask, bottom_level, shortwave, absorb, reaction):
    levels = jnp.arange(NZ, dtype=jnp.int32)[:, None, None]
    marine_indicator = ((land_mask[None] == 1) & (levels < bottom_level[None])).astype(jnp.float32)
    inside = jnp.ones((NX, NY), jnp.float32)
    ocean_view = coupled_state[0]
    tracer_view = coupled_state[1]
    for step_index in range(STEPS):
        dynamics = ocean_update(ocean_view, marine_indicator, absorb, shortwave)
        lowered, anti_east, anti_north, ratios = tracer_fluxes(tracer_view, inside)
        tracers = tracer_finish(tracer_view, lowered, anti_east, anti_north, ratios, marine_indicator, absorb, shortwave, reaction)
        if step_index + 1 < STEPS:
            ocean_view = jnp.concatenate([dynamics, tracers], axis=0)
            tracer_view = ocean_view
        else:
            ocean_view = jnp.concatenate([dynamics, ocean_view[4:]], axis=0)
            tracer_view = jnp.concatenate([tracer_view[:4], tracers], axis=0)
    return jnp.stack([ocean_view, tracer_view])
```

```python
import functools

import jax
import jax.numpy as jnp
from jax import lax
from jax.experimental import pallas as pl
from jax.experimental.pallas import tpu as pltpu
from jax.sharding import PartitionSpec as P

STEPS = 2
HALO = 2 * STEPS
LANES = 128
PAD = 8
DYN = 4

integration_interval = 0.1
tracer_interval = 0.08
coriolis = 0.8
barotropic_gradient_coefficient = 0.1
water_extinction = 0.04
layer_depth = 0.05
growth_peak = 2.0
half_light = 0.5
ratio_floor = 0.01

F32 = jnp.float32
BF16 = jnp.bfloat16
HIGHEST = lax.Precision.HIGHEST
VMEM = pl.BlockSpec(memory_space=pltpu.VMEM)
SMEM = pl.BlockSpec(memory_space=pltpu.SMEM)
ANY = pl.BlockSpec(memory_space=pl.ANY)


def dot(a, b):
    return jnp.dot(a, b, precision=HIGHEST, preferred_element_type=F32)


def iota(shape, dim):
    return lax.broadcasted_iota(jnp.int32, shape, dim)


class Plan:
    def __init__(self, mesh, nf, nz, rows, cols):
        self.n, self.m = mesh.shape["ty"], mesh.shape["tx"]
        self.nf, self.nz, self.rows, self.cols = nf, nz, rows, cols
        assert cols == LANES and LANES % nz == 0 and LANES // nz == DYN
        assert self.n & (self.n - 1) == 0 and self.n > 1
        self.per = LANES // nz
        self.groups = -(-(nf + 1) // self.per)
        self.tg = self.groups - 1
        self.chunk = cols // self.n
        self.width = self.chunk + 2 * HALO
        assert self.width % 8 == 0 and self.chunk % 8 == 0 and self.chunk >= HALO
        self.R = self.n * rows
        self.padded = self.width + 2 * PAD
        self.depth_lane = LANES - nz
        self.sw_lane = LANES - nz // 2

    def ty(self):
        return lax.axis_index("ty")

    def is_ocean(self):
        return lax.axis_index("grp") == 0

    def chunk_of(self, ty):
        odd = lax.rem(lax.axis_index("tx"), 2)
        return jnp.where(odd == 0, ty, self.n - 1 - ty)

    def xor(self, mask):
        ty, out, bit = self.ty(), 0, 1
        while bit < self.n:
            here = lax.rem(lax.div(ty, bit), 2)
            out = out + bit * ((1 - here) if mask & bit else here)
            bit *= 2
        return out


def pack_kernel(p, view, land, bottom, sw, absorb, *rest):
    outs_t, outs_o, t_ref = rest[: p.n], rest[p.n : 2 * p.n], rest[2 * p.n]
    nz, rows, step = p.nz, p.rows, p.per * p.nz
    half = nz // 2
    ocean = p.is_ocean()

    def aux(r, upper):
        depth = jnp.where(land[r : r + 1, :] == 1, bottom[r : r + 1, :], 0).astype(F32)
        return jnp.concatenate(
            [
                upper,
                jnp.broadcast_to(depth, (half, LANES)),
                jnp.broadcast_to(sw[r : r + 1, :], (half, LANES)),
            ],
            axis=0,
        )

    def field(r, g, count):
        return view[pl.ds(g * step * rows + r, count, stride=rows), :]

    def put(r, g, block):
        t_ref[g, r, HALO : HALO + LANES, :] = block.T

    def send(outs, count):
        for mask in range(p.n):
            start = pl.multiple_of(p.chunk_of(p.xor(mask)) * p.chunk, 8)
            for g in range(count):
                for r in range(rows):
                    outs[mask][g, r] = t_ref[g, r, pl.ds(start, p.width), :]

    zero = jnp.zeros((HALO, LANES), F32)
    for g in range(p.groups):
        for r in range(rows):
            t_ref[g, r, :HALO, :] = zero
            t_ref[g, r, HALO + LANES :, :] = zero

    @pl.when(jnp.logical_not(ocean))
    def _():
        for r in range(rows):
            for g in range(p.groups - 1):
                put(r, g, field(r, g, step))
            have = (p.nf - p.tg * p.per) * nz
            block = field(r, p.tg, have)
            if have < LANES - nz:
                block = jnp.concatenate([block, jnp.zeros((LANES - nz - have, LANES), F32)], axis=0)
            put(r, p.tg, aux(r, block))
        send(outs_t, p.groups)

    @pl.when(ocean)
    def _():
        lower = (iota((nz, nz), 0) >= iota((nz, nz), 1)).astype(F32)
        for r in range(rows):
            put(r, 0, field(r, 0, step))
            kd = jnp.full((nz, LANES), water_extinction, F32)
            for t in range(p.nf - DYN):
                kd = kd + absorb[t] * view[pl.ds((DYN + t) * nz * rows + r, nz, stride=rows), :]
            below = sw[r : r + 1, :] * jnp.exp(-layer_depth * dot(lower, kd))
            above = below * jnp.exp(layer_depth * kd)
            forcing = (above - below) / layer_depth
            put(r, 1, aux(r, jnp.concatenate([jnp.zeros((2 * nz, LANES), F32), forcing], axis=0)))
        send(outs_o, 2)


def edge_kernel(p, *refs):
    src_t, src_o, z_t, z_o = refs[: p.n], refs[p.n : 2 * p.n], refs[2 * p.n], refs[2 * p.n + 1]
    left = p.chunk_of(p.ty()) == 0
    ocean = p.is_ocean()

    def copy(src, dst, count, lo):
        for mask in range(p.n):
            base = p.xor(mask) * p.rows
            for g in range(count):
                for r in range(p.rows):
                    dst[g, base + r] = src[mask][g, r, lo : lo + HALO, :]

    for cond, src, dst, count in (
        (ocean, src_o, z_o, 2),
        (jnp.logical_not(ocean), src_t, z_t, p.groups),
    ):

        @pl.when(cond & left)
        def _():
            copy(src, dst, count, HALO)

        @pl.when(cond & jnp.logical_not(left))
        def _():
            copy(src, dst, count, p.chunk)


def assemble(p, src, z, g, dst):
    for mask in range(p.n):
        base = p.xor(mask) * p.rows
        for r in range(p.rows):
            dst[1 + base + r, PAD : PAD + p.width, :] = src[mask][g, r]
    chunk = p.chunk_of(p.ty())

    @pl.when(chunk == 0)
    def _():
        dst[1 : 1 + p.R, PAD : PAD + HALO, :] = z[g]

    @pl.when(chunk == p.n - 1)
    def _():
        dst[1 : 1 + p.R, PAD + p.width - HALO : PAD + p.width, :] = z[g]


def aux_fields(p, aux_ref, wet_ref, sw_ref):
    level = (iota((p.width, LANES), 1) % p.nz).astype(F32)
    for r in range(p.R):
        x = aux_ref[1 + r, PAD : PAD + p.width, :]
        wet_ref[r] = (level < x[:, p.depth_lane : p.depth_lane + 1]).astype(F32)
        sw_ref[r] = jnp.broadcast_to(x[:, p.sw_lane : p.sw_lane + 1], (p.width, LANES))


def lanes_of(p, shape, dim):
    i = iota(shape, dim)
    return i // p.nz, i % p.nz


def copy_matrix(p, slot):
    f0, k0 = lanes_of(p, (LANES, LANES), 0)
    _, k1 = lanes_of(p, (LANES, LANES), 1)
    return ((f0 == slot) & (k0 == k1)).astype(F32)


def cumsum_matrix(p):
    _, k0 = lanes_of(p, (LANES, LANES), 0)
    _, k1 = lanes_of(p, (LANES, LANES), 1)
    return (k0 <= k1).astype(F32)


def sum_matrix(p):
    _, k0 = lanes_of(p, (LANES, LANES), 0)
    _, k1 = lanes_of(p, (LANES, LANES), 1)
    return (k0 == k1).astype(F32)


def optical_depth(p, attenuation):
    _, level = lanes_of(p, attenuation.shape, 1)
    plain = (water_extinction * layer_depth) * (level + 1).astype(F32)
    return layer_depth * dot(attenuation, cumsum_matrix(p)) + plain


def ocean_step(p, d, forcing, wet, out, pp):
    f0, k0 = lanes_of(p, (LANES, LANES), 0)
    _, k1 = lanes_of(p, (LANES, LANES), 1)
    weight = jnp.where(f0 == 2, -0.2, jnp.where(f0 == 3, 0.8, 0.0)) * barotropic_gradient_coefficient
    press = jnp.where(k0 <= k1, weight, 0.0)
    mid = slice(PAD, PAD + p.width)
    for r in range(p.R):
        pp[1 + r, mid, :] = dot(d[1 + r, mid, :], press)
    f, _ = lanes_of(p, (p.width, LANES), 1)
    for r in range(p.R):
        x = d[1 + r, mid, :]
        lap = d[2 + r, mid, :] + d[r, mid, :] + d[1 + r, PAD + 1 : PAD + 1 + p.width, :]
        lap = lap + d[1 + r, PAD - 1 : PAD - 1 + p.width, :] - 4.0 * x
        grad_e = 0.5 * (pp[2 + r, mid, :] - pp[r, mid, :])
        grad_n = 0.5 * (
            pp[1 + r, PAD + 1 : PAD + 1 + p.width, :] - pp[1 + r, PAD - 1 : PAD - 1 + p.width, :]
        )
        of_u = coriolis * pltpu.roll(x, LANES - p.nz, 1) - grad_e
        of_v = -coriolis * pltpu.roll(x, p.nz, 1) - grad_n
        other = jnp.where(f == 2, forcing(r), 0.0)
        extra = jnp.where(f == 0, of_u, jnp.where(f == 1, of_v, other))
        out[r] = wet[r] * (x + integration_interval * (lap + extra))


def clear_pads(p, *refs):
    side = jnp.zeros((PAD, LANES), F32)
    for ref in refs:
        count = ref.shape[0]
        for r in range(count):
            ref[r, :PAD, :] = side
            ref[r, PAD + p.width :, :] = side
        row = jnp.zeros((p.padded, LANES), F32)
        ref[0] = row
        ref[count - 1] = row


def tracer_step(p, d, load_group, wet, sw, absorb, r_hi, r_lo, store, scratch):
    c, feh, fnh, va, ae, le, an, ln, low, rin, rout, adv = scratch
    R, W = p.R, p.width
    mid = slice(PAD, PAD + W)
    up = slice(PAD + 1, PAD + 1 + W)
    down = slice(PAD - 1, PAD - 1 + W)
    clear_pads(p, c, va, ae, le, an, ln, rin, rout)

    flat = jnp.concatenate([d[1 + r, mid, :] for r in range(R)], axis=0)
    ua = dot(flat, copy_matrix(p, 0))
    vv = dot(flat, copy_matrix(p, 1))
    for r in range(R):
        va[1 + r, mid, :] = vv[r * W : (r + 1) * W]
    first = lax.axis_index("tx") * p.cols + p.chunk_of(p.ty()) * p.chunk - HALO
    col = first + iota((W, LANES), 0)
    inside = ((col >= 0) & (col + 1 < p.m * p.cols)).astype(F32)
    half = 0.25 * tracer_interval
    for r in range(R):
        if r + 1 < R:
            feh[r] = half * (ua[r * W : (r + 1) * W] + ua[(r + 1) * W : (r + 2) * W])
        else:
            feh[r] = jnp.zeros((W, LANES), F32)
        fnh[r] = half * (va[1 + r, mid, :] + va[1 + r, up, :]) * inside

    def group(g, _):
        load_group(g, c)
        for r in range(R):
            c0 = c[1 + r, mid, :]
            cn = c[1 + r, up, :]
            ce = c[2 + r, mid, :]
            f = feh[r]
            a = jnp.abs(f) * (ce - c0)
            ae[1 + r, mid, :] = a
            le[1 + r, mid, :] = f * (ce + c0) - a
            f = fnh[r]
            a = jnp.abs(f) * (cn - c0)
            an[1 + r, mid, :] = a
            ln[1 + r, mid, :] = f * (cn + c0) - a
        for r in range(R):
            c0 = c[1 + r, mid, :]
            cn = c[1 + r, up, :]
            cs = c[1 + r, down, :]
            ce = c[2 + r, mid, :]
            cw = c[r, mid, :]
            lw = c0 - (le[1 + r, mid, :] - le[r, mid, :] + ln[1 + r, mid, :] - ln[1 + r, down, :])
            low[r] = lw
            hi = jnp.maximum(jnp.maximum(jnp.maximum(c0, ce), jnp.maximum(cw, cn)), cs)
            lo = jnp.minimum(jnp.minimum(jnp.minimum(c0, ce), jnp.minimum(cw, cn)), cs)
            e, w = ae[1 + r, mid, :], ae[r, mid, :]
            nn, s = an[1 + r, mid, :], an[1 + r, down, :]
            ep, wp, np_, sp = (jnp.maximum(x, 0.0) for x in (e, w, nn, s))
            em, wm, nm, sm = (jnp.minimum(x, 0.0) for x in (e, w, nn, s))
            gain_in = wp - em + sp - nm
            gain_out = ep - wm + np_ - sm
            floor = ratio_floor * tracer_interval
            rin[1 + r, mid, :] = jnp.minimum(gain_in, jnp.maximum(hi - lw, 0.0)) / jnp.maximum(
                gain_in, floor
            )
            rout[1 + r, mid, :] = jnp.minimum(gain_out, jnp.maximum(lw - lo, 0.0)) / jnp.maximum(
                gain_out, floor
            )
        before = jnp.zeros((W, LANES), F32)
        for r in range(R):
            ri, ro = rin[1 + r, mid, :], rout[1 + r, mid, :]
            a = ae[1 + r, mid, :]
            east = a * jnp.where(
                a >= 0.0,
                jnp.minimum(rin[2 + r, mid, :], ro),
                jnp.minimum(ri, rout[2 + r, mid, :]),
            )
            a = an[1 + r, mid, :]
            north = a * jnp.where(
                a >= 0.0,
                jnp.minimum(rin[1 + r, up, :], ro),
                jnp.minimum(ri, rout[1 + r, up, :]),
            )
            ln[1 + r, mid, :] = north
            adv[g, r] = low[r] - (east - before + north - ln[1 + r, down, :])
            before = east
        return 0

    lax.fori_loop(0, p.tg, group, 0)

    whole = [adv[g].reshape(R * W, LANES) for g in range(p.tg)]
    att = whole[0] * absorb[0:1, :]
    for g in range(1, p.tg):
        att = att + whole[g] * absorb[g : g + 1, :]
    light = sw[...].reshape(R * W, LANES) * jnp.exp(-optical_depth(p, att))
    warm = jnp.exp(0.063 * flat) * pltpu.roll(1.0 + 0.2 * jnp.tanh(flat), LANES - p.nz, 1)
    growth = (
        (growth_peak * tracer_interval) * dot(warm, copy_matrix(p, 2)) * light / (light + half_light)
    )
    every = jnp.concatenate(whole, axis=1)
    hi = every.astype(BF16)
    lo = (every - hi.astype(F32)).astype(BF16)

    def mm(a, b):
        return jnp.dot(a, b, preferred_element_type=F32)

    mixed = mm(hi, r_hi[...]) + mm(lo, r_hi[...]) + mm(hi, r_lo[...])
    wets = wet[...].reshape(R * W, LANES)
    for g in range(p.tg):
        new = wets * (whole[g] + growth * mixed[:, g * LANES : (g + 1) * LANES])
        store(g, new.reshape(R, W, LANES))


def ocean_first_kernel(p, *refs):
    src, z, dyn, wet, sw, d, aux, pp = (refs[: p.n],) + refs[p.n :]

    @pl.when(p.is_ocean())
    def _():
        clear_pads(p, d, aux, pp)
        assemble(p, src, z, 0, d)
        assemble(p, src, z, 1, aux)
        aux_fields(p, aux, wet, sw)
        ocean_step(p, d, lambda r: aux[1 + r, PAD : PAD + p.width, :], wet, dyn, pp)


def tracer_first_kernel(p, *refs):
    src, (z, absorb, r_hi, r_lo, c1, wet, sw, d), scratch = refs[: p.n], refs[p.n : p.n + 8], refs[p.n + 8 :]

    @pl.when(jnp.logical_not(p.is_ocean()))
    def _():
        c = scratch[0]
        clear_pads(p, d)
        assemble(p, src, z, p.groups - 1, c)
        aux_fields(p, c, wet, sw)
        assemble(p, src, z, 0, d)

        def load(g, dst):
            assemble(p, src, z, g + 1, dst)

        def store(g, value):
            c1[g] = value

        tracer_step(p, d, load, wet, sw, absorb, r_hi, r_lo, store, scratch)


def load_dyn(p, dyn, d):
    clear_pads(p, d)
    for r in range(p.R):
        d[1 + r, PAD : PAD + p.width, :] = dyn[r]


def put_back(p, outs, group, value):
    for mask in range(p.n):
        outs[mask][group] = value(p.xor(mask) * p.rows)


def tracer_second_kernel(p, *refs):
    dyn, c1, wet, sw, absorb, r_hi, r_lo = refs[:7]
    outs, (d, c2), scratch = refs[7 : 7 + p.n], refs[7 + p.n : 9 + p.n], refs[9 + p.n :]
    core = slice(HALO, HALO + p.chunk)

    @pl.when(jnp.logical_not(p.is_ocean()))
    def _():
        load_dyn(p, dyn, d)

        def load(g, dst):
            for r in range(p.R):
                dst[1 + r, PAD : PAD + p.width, :] = c1[g, r]

        def store(g, value):
            c2[...] = value
            put_back(p, outs, g + 1, lambda row: c2[pl.ds(row, p.rows), core, :])

        tracer_step(p, d, load, wet, sw, absorb, r_hi, r_lo, store, scratch)
        put_back(p, outs, 0, lambda row: dyn[pl.ds(row, p.rows), core, :])


def ocean_second_kernel(p, *refs):
    dyn, c1, wet, sw, absorb = refs[:5]
    same, outs, (d, pp, heat, dyn2) = refs[5 : 5 + p.n], refs[5 + p.n : 5 + 2 * p.n], refs[5 + 2 * p.n :]
    core = slice(HALO, HALO + p.chunk)

    @pl.when(jnp.logical_not(p.is_ocean()))
    def _():
        for mask in range(p.n):
            outs[mask][...] = same[mask][...]

    @pl.when(p.is_ocean())
    def _():
        load_dyn(p, dyn, d)
        clear_pads(p, pp)
        flat = (p.R * p.width, LANES)
        att = c1[0].reshape(flat) * absorb[0:1, :]
        for g in range(1, p.tg):
            att = att + c1[g].reshape(flat) * absorb[g : g + 1, :]
        below = sw[...].reshape(flat) * jnp.exp(-optical_depth(p, att))
        kd = dot(att, sum_matrix(p)) + water_extinction
        above = below * jnp.exp(layer_depth * kd)
        heat[...] = ((above - below) / layer_depth).reshape(heat.shape)
        ocean_step(p, d, lambda r: heat[r], wet, dyn2, pp)
        put_back(p, outs, 0, lambda row: dyn2[pl.ds(row, p.rows), core, :])
        for g in range(p.tg):
            put_back(p, outs, g + 1, lambda row: c1[g, pl.ds(row, p.rows), core, :])


def unpack_kernel(p, *refs):
    src, out, t_ref = refs[: p.n], refs[p.n], refs[p.n + 1]
    step = p.per * p.nz
    for g in range(p.groups):
        count = min(step, (p.nf - g * p.per) * p.nz)
        for r in range(p.rows):
            for mask in range(p.n):
                start = pl.multiple_of(p.chunk_of(p.xor(mask)) * p.chunk, 8)
                t_ref[pl.ds(start, p.chunk), :] = src[mask][g, r]
            out[pl.ds(g * step * p.rows + r, count, stride=p.rows), :] = t_ref[...].T[:count]


def mix_kernel(p, reaction, r_hi, r_lo):
    size = p.tg * LANES
    spread = (iota((size, LANES), 0) // p.nz == iota((size, LANES), 1)).astype(F32)
    rows = lax.dot_general(
        spread, reaction[...], (((1,), (1,)), ((), ())), precision=HIGHEST, preferred_element_type=F32
    )
    full = lax.dot_general(
        rows, spread, (((1,), (1,)), ((), ())), precision=HIGHEST, preferred_element_type=F32
    )
    same = iota((size, size), 0) % p.nz == iota((size, size), 1) % p.nz
    full = jnp.where(same, full, 0.0)
    hi = full.astype(BF16)
    r_hi[...] = hi
    r_lo[...] = (full - hi.astype(F32)).astype(BF16)


def solution(mesh):
    def local(coupled_state, land_mask, bottom_level, shortwave, absorb, reaction):
        view = coupled_state[0]
        p = Plan(mesh, *view.shape)
        n, G, R, W = p.n, p.groups, p.R, p.width

        def sds(*shape, dtype=F32):
            return jax.ShapeDtypeStruct(shape, dtype)

        def call(kernel, name, outs, ins, scratch=(), in_specs=None, aliases=None):
            return pl.pallas_call(
                functools.partial(kernel, p),
                name=name,
                out_shape=outs,
                in_specs=in_specs or [VMEM] * len(ins),
                out_specs=jax.tree.map(lambda _: VMEM, outs),
                scratch_shapes=[pltpu.VMEM(s, F32) for s in scratch],
                input_output_aliases=aliases or {},
                compiler_params=pltpu.CompilerParams(vmem_limit_bytes=56 * 2**20),
            )(*ins)

        def swap(value, mask, grp):
            pairs = [(grp * n + i, grp * n + (i ^ mask)) for i in range(n)]
            return lax.ppermute(value, ("grp", "ty"), pairs)

        def edges(value, grp):
            pairs = []
            size = lax.axis_size("tx")
            for tx in range(size - 1):
                end = n - 1 if tx % 2 == 0 else 0
                a = (grp * n + end) * size + tx
                pairs += [(a, a + 1), (a + 1, a)]
            return lax.ppermute(value, ("grp", "ty", "tx"), pairs)

        flat = view.reshape(p.nf * p.nz * p.rows, p.cols)
        packed = call(
            pack_kernel,
            "pack",
            [sds(G, p.rows, W, LANES)] * n + [sds(2, p.rows, W, LANES)] * n,
            [flat, land_mask, bottom_level, shortwave, absorb],
            [(G, p.rows, LANES + 2 * HALO, LANES)],
            [VMEM] * 4 + [SMEM],
        )
        got_t = [packed[0]] + [swap(packed[k], k, 1) for k in range(1, n)]
        got_o = [packed[n]] + [swap(packed[n + k], k, 0) for k in range(1, n)]

        react = jnp.pad(reaction, ((0, LANES - reaction.shape[0]), (0, LANES - reaction.shape[1])))
        size = p.tg * LANES
        r_hi, r_lo = call(
            mix_kernel, "mix", [sds(size, size, dtype=BF16), sds(size, size, dtype=BF16)], [react]
        )
        weights = jnp.pad(absorb, (0, p.tg * p.per - absorb.shape[0])).reshape(p.tg, p.per)
        weights = jnp.repeat(weights, p.nz, axis=1)

        z_t, z_o = call(
            edge_kernel, "edge", [sds(G, R, HALO, LANES), sds(2, R, HALO, LANES)], got_t + got_o
        )
        z_t, z_o = edges(z_t, 1), edges(z_o, 0)

        padded = (R + 2, p.padded, LANES)
        block = (R, W, LANES)
        scratch = [padded, block, block] + [padded] * 5 + [block] + [padded] * 2 + [(p.tg,) + block]
        dyn1, wet_o, sw_o = call(
            ocean_first_kernel, "ocean_first", [sds(*block)] * 3, got_o + [z_o], [padded] * 3
        )

        def across(value, source):
            other = [
                ((source * n + i) , ((1 - source) * n + i)) for i in range(n)
            ]
            return lax.ppermute(value, ("grp", "ty"), other)

        dyn1_t = across(dyn1, 0)
        c1, wet_t, sw_t = call(
            tracer_first_kernel,
            "tracer_first",
            [sds(p.tg, *block), sds(*block), sds(*block)],
            got_t + [z_t, weights, r_hi, r_lo],
            [padded] + scratch,
        )
        c1_o = across(c1, 1)
        back = [sds(G, p.rows, p.chunk, LANES)] * n
        outs = call(
            tracer_second_kernel,
            "tracer_second",
            back,
            [dyn1_t, c1, wet_t, sw_t, weights, r_hi, r_lo],
            [padded, block] + scratch,
        )
        outs = call(
            ocean_second_kernel,
            "ocean_second",
            back,
            [dyn1, c1_o, wet_o, sw_o, weights] + list(outs),
            [padded, padded, block, block],
            aliases={5 + k: k for k in range(n)},
        )
        home = [outs[0]] + [
            lax.ppermute(outs[k], "ty", [(i, i ^ k) for i in range(n)]) for k in range(1, n)
        ]
        out = call(
            unpack_kernel, "unpack", [sds(p.nf * p.nz * p.rows, p.cols)], home, [(LANES, LANES)]
        )[0]
        return out.reshape((1,) + view.shape)

    in_specs = (
        P("grp", None, None, "ty", "tx"),
        P("ty", "tx"),
        P("ty", "tx"),
        P("ty", "tx"),
        P(),
        P(),
    )
    out_specs = P("grp", None, None, "ty", "tx")
    return jax.shard_map(local, mesh=mesh, in_specs=in_specs, out_specs=out_specs, check_vma=False)
```

```python
import functools

import jax
import jax.numpy as jnp
from jax import lax
from jax.experimental import pallas as pl
from jax.experimental.pallas import tpu as pltpu
from jax.sharding import PartitionSpec as P

STEPS = 2
HALO = 2 * STEPS
LANES = 128
PAD = 8
DYN = 4

integration_interval = 0.1
tracer_interval = 0.08
coriolis = 0.8
barotropic_gradient_coefficient = 0.1
water_extinction = 0.04
layer_depth = 0.05
growth_peak = 2.0
half_light = 0.5
ratio_floor = 0.01

F32 = jnp.float32
BF16 = jnp.bfloat16
HIGHEST = lax.Precision.HIGHEST
VMEM = pl.BlockSpec(memory_space=pltpu.VMEM)
SMEM = pl.BlockSpec(memory_space=pltpu.SMEM)
ANY = pl.BlockSpec(memory_space=pl.ANY)


def dot(a, b):
    return jnp.dot(a, b, precision=HIGHEST, preferred_element_type=F32)


def iota(shape, dim):
    return lax.broadcasted_iota(jnp.int32, shape, dim)


class Plan:
    def __init__(self, mesh, nf, nz, rows, cols):
        self.n, self.m = mesh.shape["ty"], mesh.shape["tx"]
        self.nf, self.nz, self.rows, self.cols = nf, nz, rows, cols
        assert cols == LANES and LANES % nz == 0 and LANES // nz == DYN
        assert self.n & (self.n - 1) == 0 and self.n > 1
        self.per = LANES // nz
        self.groups = -(-(nf + 1) // self.per)
        self.tg = self.groups - 1
        self.chunk = cols // self.n
        self.width = self.chunk + 2 * HALO
        assert self.width % 8 == 0 and self.chunk % 8 == 0 and self.chunk >= HALO
        self.R = self.n * rows
        self.padded = self.width + 2 * PAD
        self.depth_lane = LANES - nz
        self.sw_lane = LANES - nz // 2

    def ty(self):
        return lax.axis_index("ty")

    def is_ocean(self):
        return lax.axis_index("grp") == 0

    def chunk_of(self, ty):
        odd = lax.rem(lax.axis_index("tx"), 2)
        return jnp.where(odd == 0, ty, self.n - 1 - ty)

    def xor(self, mask):
        ty, out, bit = self.ty(), 0, 1
        while bit < self.n:
            here = lax.rem(lax.div(ty, bit), 2)
            out = out + bit * ((1 - here) if mask & bit else here)
            bit *= 2
        return out


def pack_kernel(p, view, land, bottom, sw, absorb, *rest):
    outs_t, outs_o, t_ref = rest[: p.n], rest[p.n : 2 * p.n], rest[2 * p.n]
    nz, rows, step = p.nz, p.rows, p.per * p.nz
    half = nz // 2
    ocean = p.is_ocean()

    def aux(r, upper):
        depth = jnp.where(land[r : r + 1, :] == 1, bottom[r : r + 1, :], 0).astype(F32)
        return jnp.concatenate(
            [
                upper,
                jnp.broadcast_to(depth, (half, LANES)),
                jnp.broadcast_to(sw[r : r + 1, :], (half, LANES)),
            ],
            axis=0,
        )

    def field(r, g, count):
        return view[pl.ds(g * step * rows + r, count, stride=rows), :]

    def put(r, g, block):
        t_ref[g, r, HALO : HALO + LANES, :] = block.T

    def send(outs, count):
        for mask in range(p.n):
            start = pl.multiple_of(p.chunk_of(p.xor(mask)) * p.chunk, 8)
            for g in range(count):
                for r in range(rows):
                    outs[mask][g, r] = t_ref[g, r, pl.ds(start, p.width), :]

    zero = jnp.zeros((HALO, LANES), F32)
    for g in range(p.groups):
        for r in range(rows):
            t_ref[g, r, :HALO, :] = zero
            t_ref[g, r, HALO + LANES :, :] = zero

    @pl.when(jnp.logical_not(ocean))
    def _():
        for r in range(rows):
            for g in range(p.groups - 1):
                put(r, g, field(r, g, step))
            have = (p.nf - p.tg * p.per) * nz
            block = field(r, p.tg, have)
            if have < LANES - nz:
                block = jnp.concatenate([block, jnp.zeros((LANES - nz - have, LANES), F32)], axis=0)
            put(r, p.tg, aux(r, block))
        send(outs_t, p.groups)

    @pl.when(ocean)
    def _():
        lower = (iota((nz, nz), 0) >= iota((nz, nz), 1)).astype(F32)
        for r in range(rows):
            put(r, 0, field(r, 0, step))
            kd = jnp.full((nz, LANES), water_extinction, F32)
            for t in range(p.nf - DYN):
                kd = kd + absorb[t] * view[pl.ds((DYN + t) * nz * rows + r, nz, stride=rows), :]
            below = sw[r : r + 1, :] * jnp.exp(-layer_depth * dot(lower, kd))
            above = below * jnp.exp(layer_depth * kd)
            forcing = (above - below) / layer_depth
            put(r, 1, aux(r, jnp.concatenate([jnp.zeros((2 * nz, LANES), F32), forcing], axis=0)))
        send(outs_o, 2)


def edge_kernel(p, *refs):
    src_t, src_o, z_t, z_o = refs[: p.n], refs[p.n : 2 * p.n], refs[2 * p.n], refs[2 * p.n + 1]
    left = p.chunk_of(p.ty()) == 0
    ocean = p.is_ocean()

    def copy(src, dst, count, lo):
        for mask in range(p.n):
            base = p.xor(mask) * p.rows
            for g in range(count):
                for r in range(p.rows):
                    dst[g, base + r] = src[mask][g, r, lo : lo + HALO, :]

    for cond, src, dst, count in (
        (ocean, src_o, z_o, 2),
        (jnp.logical_not(ocean), src_t, z_t, p.groups),
    ):

        @pl.when(cond & left)
        def _():
            copy(src, dst, count, HALO)

        @pl.when(cond & jnp.logical_not(left))
        def _():
            copy(src, dst, count, p.chunk)


def assemble(p, src, z, g, dst):
    for mask in range(p.n):
        base = p.xor(mask) * p.rows
        for r in range(p.rows):
            dst[1 + base + r, PAD : PAD + p.width, :] = src[mask][g, r]
    chunk = p.chunk_of(p.ty())

    @pl.when(chunk == 0)
    def _():
        dst[1 : 1 + p.R, PAD : PAD + HALO, :] = z[g]

    @pl.when(chunk == p.n - 1)
    def _():
        dst[1 : 1 + p.R, PAD + p.width - HALO : PAD + p.width, :] = z[g]


def aux_fields(p, aux_ref, wet_ref, sw_ref):
    level = (iota((p.width, LANES), 1) % p.nz).astype(F32)
    for r in range(p.R):
        x = aux_ref[1 + r, PAD : PAD + p.width, :]
        wet_ref[r] = (level < x[:, p.depth_lane : p.depth_lane + 1]).astype(F32)
        sw_ref[r] = jnp.broadcast_to(x[:, p.sw_lane : p.sw_lane + 1], (p.width, LANES))


def lanes_of(p, shape, dim):
    i = iota(shape, dim)
    return i // p.nz, i % p.nz


def copy_matrix(p, slot):
    f0, k0 = lanes_of(p, (LANES, LANES), 0)
    _, k1 = lanes_of(p, (LANES, LANES), 1)
    return ((f0 == slot) & (k0 == k1)).astype(F32)


def cumsum_matrix(p):
    _, k0 = lanes_of(p, (LANES, LANES), 0)
    _, k1 = lanes_of(p, (LANES, LANES), 1)
    return (k0 <= k1).astype(F32)


def sum_matrix(p):
    _, k0 = lanes_of(p, (LANES, LANES), 0)
    _, k1 = lanes_of(p, (LANES, LANES), 1)
    return (k0 == k1).astype(F32)


def optical_depth(p, attenuation):
    _, level = lanes_of(p, attenuation.shape, 1)
    plain = (water_extinction * layer_depth) * (level + 1).astype(F32)
    return layer_depth * dot(attenuation, cumsum_matrix(p)) + plain


def ocean_step(p, d, forcing, wet, out, pp):
    f0, k0 = lanes_of(p, (LANES, LANES), 0)
    _, k1 = lanes_of(p, (LANES, LANES), 1)
    weight = jnp.where(f0 == 2, -0.2, jnp.where(f0 == 3, 0.8, 0.0)) * barotropic_gradient_coefficient
    press = jnp.where(k0 <= k1, weight, 0.0)
    mid = slice(PAD, PAD + p.width)
    for r in range(p.R):
        pp[1 + r, mid, :] = dot(d[1 + r, mid, :], press)
    f, _ = lanes_of(p, (p.width, LANES), 1)
    for r in range(p.R):
        x = d[1 + r, mid, :]
        lap = d[2 + r, mid, :] + d[r, mid, :] + d[1 + r, PAD + 1 : PAD + 1 + p.width, :]
        lap = lap + d[1 + r, PAD - 1 : PAD - 1 + p.width, :] - 4.0 * x
        grad_e = 0.5 * (pp[2 + r, mid, :] - pp[r, mid, :])
        grad_n = 0.5 * (
            pp[1 + r, PAD + 1 : PAD + 1 + p.width, :] - pp[1 + r, PAD - 1 : PAD - 1 + p.width, :]
        )
        of_u = coriolis * pltpu.roll(x, LANES - p.nz, 1) - grad_e
        of_v = -coriolis * pltpu.roll(x, p.nz, 1) - grad_n
        other = jnp.where(f == 2, forcing(r), 0.0)
        extra = jnp.where(f == 0, of_u, jnp.where(f == 1, of_v, other))
        out[r] = wet[r] * (x + integration_interval * (lap + extra))


def clear_pads(p, *refs):
    side = jnp.zeros((PAD, LANES), F32)
    for ref in refs:
        count = ref.shape[0]
        for r in range(count):
            ref[r, :PAD, :] = side
            ref[r, PAD + p.width :, :] = side
        row = jnp.zeros((p.padded, LANES), F32)
        ref[0] = row
        ref[count - 1] = row


def tracer_step(p, d, load_group, wet, sw, absorb, r_hi, r_lo, store, scratch):
    c, feh, fnh, va, ae, le, an, ln, low, rin, rout, adv = scratch
    R, W = p.R, p.width
    mid = slice(PAD, PAD + W)
    up = slice(PAD + 1, PAD + 1 + W)
    down = slice(PAD - 1, PAD - 1 + W)
    clear_pads(p, c, va, ae, le, an, ln, rin, rout)

    flat = jnp.concatenate([d[1 + r, mid, :] for r in range(R)], axis=0)
    ua = dot(flat, copy_matrix(p, 0))
    vv = dot(flat, copy_matrix(p, 1))
    for r in range(R):
        va[1 + r, mid, :] = vv[r * W : (r + 1) * W]
    first = lax.axis_index("tx") * p.cols + p.chunk_of(p.ty()) * p.chunk - HALO
    col = first + iota((W, LANES), 0)
    inside = ((col >= 0) & (col + 1 < p.m * p.cols)).astype(F32)
    half = 0.25 * tracer_interval
    for r in range(R):
        if r + 1 < R:
            feh[r] = half * (ua[r * W : (r + 1) * W] + ua[(r + 1) * W : (r + 2) * W])
        else:
            feh[r] = jnp.zeros((W, LANES), F32)
        fnh[r] = half * (va[1 + r, mid, :] + va[1 + r, up, :]) * inside

    def group(g, _):
        load_group(g, c)
        for r in range(R):
            c0 = c[1 + r, mid, :]
            cn = c[1 + r, up, :]
            ce = c[2 + r, mid, :]
            f = feh[r]
            a = jnp.abs(f) * (ce - c0)
            ae[1 + r, mid, :] = a
            le[1 + r, mid, :] = f * (ce + c0) - a
            f = fnh[r]
            a = jnp.abs(f) * (cn - c0)
            an[1 + r, mid, :] = a
            ln[1 + r, mid, :] = f * (cn + c0) - a
        for r in range(R):
            c0 = c[1 + r, mid, :]
            cn = c[1 + r, up, :]
            cs = c[1 + r, down, :]
            ce = c[2 + r, mid, :]
            cw = c[r, mid, :]
            lw = c0 - (le[1 + r, mid, :] - le[r, mid, :] + ln[1 + r, mid, :] - ln[1 + r, down, :])
            low[r] = lw
            hi = jnp.maximum(jnp.maximum(jnp.maximum(c0, ce), jnp.maximum(cw, cn)), cs)
            lo = jnp.minimum(jnp.minimum(jnp.minimum(c0, ce), jnp.minimum(cw, cn)), cs)
            e, w = ae[1 + r, mid, :], ae[r, mid, :]
            nn, s = an[1 + r, mid, :], an[1 + r, down, :]
            ep, wp, np_, sp = (jnp.maximum(x, 0.0) for x in (e, w, nn, s))
            em, wm, nm, sm = (jnp.minimum(x, 0.0) for x in (e, w, nn, s))
            gain_in = wp - em + sp - nm
            gain_out = ep - wm + np_ - sm
            floor = ratio_floor * tracer_interval
            rin[1 + r, mid, :] = jnp.minimum(gain_in, jnp.maximum(hi - lw, 0.0)) / jnp.maximum(
                gain_in, floor
            )
            rout[1 + r, mid, :] = jnp.minimum(gain_out, jnp.maximum(lw - lo, 0.0)) / jnp.maximum(
                gain_out, floor
            )
        before = jnp.zeros((W, LANES), F32)
        for r in range(R):
            ri, ro = rin[1 + r, mid, :], rout[1 + r, mid, :]
            a = ae[1 + r, mid, :]
            east = a * jnp.where(
                a >= 0.0,
                jnp.minimum(rin[2 + r, mid, :], ro),
                jnp.minimum(ri, rout[2 + r, mid, :]),
            )
            a = an[1 + r, mid, :]
            north = a * jnp.where(
                a >= 0.0,
                jnp.minimum(rin[1 + r, up, :], ro),
                jnp.minimum(ri, rout[1 + r, up, :]),
            )
            ln[1 + r, mid, :] = north
            adv[g, r] = low[r] - (east - before + north - ln[1 + r, down, :])
            before = east
        return 0

    lax.fori_loop(0, p.tg, group, 0)

    whole = [adv[g].reshape(R * W, LANES) for g in range(p.tg)]
    att = whole[0] * absorb[0:1, :]
    for g in range(1, p.tg):
        att = att + whole[g] * absorb[g : g + 1, :]
    light = sw[...].reshape(R * W, LANES) * jnp.exp(-optical_depth(p, att))
    warm = jnp.exp(0.063 * flat) * pltpu.roll(1.0 + 0.2 * jnp.tanh(flat), LANES - p.nz, 1)
    growth = (
        (growth_peak * tracer_interval) * dot(warm, copy_matrix(p, 2)) * light / (light + half_light)
    )
    every = jnp.concatenate(whole, axis=1)
    hi = every.astype(BF16)
    lo = (every - hi.astype(F32)).astype(BF16)

    def mm(a, b):
        return jnp.dot(a, b, preferred_element_type=F32)

    mixed = mm(hi, r_hi[...]) + mm(lo, r_hi[...]) + mm(hi, r_lo[...])
    wets = wet[...].reshape(R * W, LANES)
    for g in range(p.tg):
        new = wets * (whole[g] + growth * mixed[:, g * LANES : (g + 1) * LANES])
        store(g, new.reshape(R, W, LANES))


def ocean_first_kernel(p, *refs):
    src, z, dyn, wet, sw, d, aux, pp = (refs[: p.n],) + refs[p.n :]

    @pl.when(p.is_ocean())
    def _():
        clear_pads(p, d, aux, pp)
        assemble(p, src, z, 0, d)
        assemble(p, src, z, 1, aux)
        aux_fields(p, aux, wet, sw)
        ocean_step(p, d, lambda r: aux[1 + r, PAD : PAD + p.width, :], wet, dyn, pp)


def tracer_first_kernel(p, *refs):
    src, (z, absorb, r_hi, r_lo, c1, wet, sw, d), scratch = refs[: p.n], refs[p.n : p.n + 8], refs[p.n + 8 :]

    @pl.when(jnp.logical_not(p.is_ocean()))
    def _():
        c = scratch[0]
        clear_pads(p, d)
        assemble(p, src, z, p.groups - 1, c)
        aux_fields(p, c, wet, sw)
        assemble(p, src, z, 0, d)

        def load(g, dst):
            assemble(p, src, z, g + 1, dst)

        def store(g, value):
            c1[g] = value

        tracer_step(p, d, load, wet, sw, absorb, r_hi, r_lo, store, scratch)


def load_dyn(p, dyn, d):
    clear_pads(p, d)
    for r in range(p.R):
        d[1 + r, PAD : PAD + p.width, :] = dyn[r]


def put_back(p, outs, group, value):
    for mask in range(p.n):
        outs[mask][group] = value(p.xor(mask) * p.rows)


def tracer_second_kernel(p, *refs):
    dyn, c1, wet, sw, absorb, r_hi, r_lo = refs[:7]
    outs, (d, c2), scratch = refs[7 : 7 + p.n], refs[7 + p.n : 9 + p.n], refs[9 + p.n :]
    core = slice(HALO, HALO + p.chunk)

    @pl.when(jnp.logical_not(p.is_ocean()))
    def _():
        load_dyn(p, dyn, d)

        def load(g, dst):
            for r in range(p.R):
                dst[1 + r, PAD : PAD + p.width, :] = c1[g, r]

        def store(g, value):
            c2[...] = value
            put_back(p, outs, g + 1, lambda row: c2[pl.ds(row, p.rows), core, :])

        tracer_step(p, d, load, wet, sw, absorb, r_hi, r_lo, store, scratch)
        put_back(p, outs, 0, lambda row: dyn[pl.ds(row, p.rows), core, :])


def ocean_second_kernel(p, *refs):
    dyn, c1, wet, sw, absorb = refs[:5]
    same, outs, (d, pp, heat, dyn2) = refs[5 : 5 + p.n], refs[5 + p.n : 5 + 2 * p.n], refs[5 + 2 * p.n :]
    core = slice(HALO, HALO + p.chunk)

    @pl.when(jnp.logical_not(p.is_ocean()))
    def _():
        for mask in range(p.n):
            outs[mask][...] = same[mask][...]

    @pl.when(p.is_ocean())
    def _():
        load_dyn(p, dyn, d)
        clear_pads(p, pp)
        flat = (p.R * p.width, LANES)
        att = c1[0].reshape(flat) * absorb[0:1, :]
        for g in range(1, p.tg):
            att = att + c1[g].reshape(flat) * absorb[g : g + 1, :]
        below = sw[...].reshape(flat) * jnp.exp(-optical_depth(p, att))
        kd = dot(att, sum_matrix(p)) + water_extinction
        above = below * jnp.exp(layer_depth * kd)
        heat[...] = ((above - below) / layer_depth).reshape(heat.shape)
        ocean_step(p, d, lambda r: heat[r], wet, dyn2, pp)
        put_back(p, outs, 0, lambda row: dyn2[pl.ds(row, p.rows), core, :])
        for g in range(p.tg):
            put_back(p, outs, g + 1, lambda row: c1[g, pl.ds(row, p.rows), core, :])


def unpack_kernel(p, *refs):
    src, out, t_ref = refs[: p.n], refs[p.n], refs[p.n + 1]
    step = p.per * p.nz
    for g in range(p.groups):
        count = min(step, (p.nf - g * p.per) * p.nz)
        for r in range(p.rows):
            for mask in range(p.n):
                start = pl.multiple_of(p.chunk_of(p.xor(mask)) * p.chunk, 8)
                t_ref[pl.ds(start, p.chunk), :] = src[mask][g, r]
            out[pl.ds(g * step * p.rows + r, count, stride=p.rows), :] = t_ref[...].T[:count]


def mix_kernel(p, reaction, r_hi, r_lo):
    size = p.tg * LANES
    spread = (iota((size, LANES), 0) // p.nz == iota((size, LANES), 1)).astype(F32)
    rows = lax.dot_general(
        spread, reaction[...], (((1,), (1,)), ((), ())), precision=HIGHEST, preferred_element_type=F32
    )
    full = lax.dot_general(
        rows, spread, (((1,), (1,)), ((), ())), precision=HIGHEST, preferred_element_type=F32
    )
    same = iota((size, size), 0) % p.nz == iota((size, size), 1) % p.nz
    full = jnp.where(same, full, 0.0)
    hi = full.astype(BF16)
    r_hi[...] = hi
    r_lo[...] = (full - hi.astype(F32)).astype(BF16)


def solution(mesh):
    def local(coupled_state, land_mask, bottom_level, shortwave, absorb, reaction):
        view = coupled_state[0]
        p = Plan(mesh, *view.shape)
        n, G, R, W = p.n, p.groups, p.R, p.width

        def sds(*shape, dtype=F32):
            return jax.ShapeDtypeStruct(shape, dtype)

        def call(kernel, name, outs, ins, scratch=(), in_specs=None, aliases=None):
            return pl.pallas_call(
                functools.partial(kernel, p),
                name=name,
                out_shape=outs,
                in_specs=in_specs or [VMEM] * len(ins),
                out_specs=jax.tree.map(lambda _: VMEM, outs),
                scratch_shapes=[pltpu.VMEM(s, F32) for s in scratch],
                input_output_aliases=aliases or {},
                compiler_params=pltpu.CompilerParams(vmem_limit_bytes=20 * 2**20),
            )(*ins)

        def swap(value, mask, grp):
            pairs = [(grp * n + i, grp * n + (i ^ mask)) for i in range(n)]
            return lax.ppermute(value, ("grp", "ty"), pairs)

        def edges(value, grp):
            pairs = []
            size = lax.axis_size("tx")
            for tx in range(size - 1):
                end = n - 1 if tx % 2 == 0 else 0
                a = (grp * n + end) * size + tx
                pairs += [(a, a + 1), (a + 1, a)]
            return lax.ppermute(value, ("grp", "ty", "tx"), pairs)

        flat = view.reshape(p.nf * p.nz * p.rows, p.cols)
        packed = call(
            pack_kernel,
            "pack",
            [sds(G, p.rows, W, LANES)] * n + [sds(2, p.rows, W, LANES)] * n,
            [flat, land_mask, bottom_level, shortwave, absorb],
            [(G, p.rows, LANES + 2 * HALO, LANES)],
            [VMEM] * 4 + [SMEM],
        )
        got_t = [packed[0]] + [swap(packed[k], k, 1) for k in range(1, n)]
        got_o = [packed[n]] + [swap(packed[n + k], k, 0) for k in range(1, n)]

        react = jnp.pad(reaction, ((0, LANES - reaction.shape[0]), (0, LANES - reaction.shape[1])))
        size = p.tg * LANES
        r_hi, r_lo = call(
            mix_kernel, "mix", [sds(size, size, dtype=BF16), sds(size, size, dtype=BF16)], [react]
        )
        weights = jnp.pad(absorb, (0, p.tg * p.per - absorb.shape[0])).reshape(p.tg, p.per)
        weights = jnp.repeat(weights, p.nz, axis=1)

        z_t, z_o = call(
            edge_kernel, "edge", [sds(G, R, HALO, LANES), sds(2, R, HALO, LANES)], got_t + got_o
        )
        z_t, z_o = edges(z_t, 1), edges(z_o, 0)

        padded = (R + 2, p.padded, LANES)
        block = (R, W, LANES)
        scratch = [padded, block, block] + [padded] * 5 + [block] + [padded] * 2 + [(p.tg,) + block]
        dyn1, wet_o, sw_o = call(
            ocean_first_kernel, "ocean_first", [sds(*block)] * 3, got_o + [z_o], [padded] * 3
        )

        def across(value, source):
            other = [
                ((source * n + i) , ((1 - source) * n + i)) for i in range(n)
            ]
            return lax.ppermute(value, ("grp", "ty"), other)

        dyn1_t = across(dyn1, 0)
        c1, wet_t, sw_t = call(
            tracer_first_kernel,
            "tracer_first",
            [sds(p.tg, *block), sds(*block), sds(*block)],
            got_t + [z_t, weights, r_hi, r_lo],
            [padded] + scratch,
        )
        c1_o = across(c1, 1)
        back = [sds(G, p.rows, p.chunk, LANES)] * n
        outs = call(
            tracer_second_kernel,
            "tracer_second",
            back,
            [dyn1_t, c1, wet_t, sw_t, weights, r_hi, r_lo],
            [padded, block] + scratch,
        )
        outs = call(
            ocean_second_kernel,
            "ocean_second",
            back,
            [dyn1, c1_o, wet_o, sw_o, weights] + list(outs),
            [padded, padded, block, block],
            aliases={5 + k: k for k in range(n)},
        )
        home = [outs[0]] + [
            lax.ppermute(outs[k], "ty", [(i, i ^ k) for i in range(n)]) for k in range(1, n)
        ]
        out = call(
            unpack_kernel, "unpack", [sds(p.nf * p.nz * p.rows, p.cols)], home, [(LANES, LANES)]
        )[0]
        return out.reshape((1,) + view.shape)

    in_specs = (
        P("grp", None, None, "ty", "tx"),
        P("ty", "tx"),
        P("ty", "tx"),
        P("ty", "tx"),
        P(),
        P(),
    )
    out_specs = P("grp", None, None, "ty", "tx")
    return jax.shard_map(local, mesh=mesh, in_specs=in_specs, out_specs=out_specs, check_vma=False)
```

```python
import functools

import jax
import jax.numpy as jnp
from jax import lax
from jax.experimental import pallas as pl
from jax.experimental.pallas import tpu as pltpu
from jax.sharding import PartitionSpec as P


STEPS = 2
HALO = 2 * STEPS
LANES = 128
PAD = 8
DYN = 4
SHARED = 2

integration_interval = 0.1
tracer_interval = 0.08
coriolis = 0.8
barotropic_gradient_coefficient = 0.1
water_extinction = 0.04
layer_depth = 0.05
growth_peak = 2.0
half_light = 0.5
ratio_floor = 0.01

F32 = jnp.float32
BF16 = jnp.bfloat16
HIGHEST = lax.Precision.HIGHEST
VMEM = pl.BlockSpec(memory_space=pltpu.VMEM)
SMEM = pl.BlockSpec(memory_space=pltpu.SMEM)
ANY = pl.BlockSpec(memory_space=pl.ANY)
HBM = pl.BlockSpec(memory_space=pltpu.HBM)


def dot(a, b):
    return jnp.dot(a, b, precision=HIGHEST, preferred_element_type=F32)


def iota(shape, dim):
    return lax.broadcasted_iota(jnp.int32, shape, dim)


class Plan:
    def __init__(self, mesh, nf, nz, rows, cols):
        self.n, self.m = mesh.shape["ty"], mesh.shape["tx"]
        self.nf, self.nz, self.rows, self.cols = nf, nz, rows, cols
        assert cols == LANES and LANES % nz == 0 and LANES // nz == DYN
        assert self.n & (self.n - 1) == 0 and self.n > 1
        self.per = LANES // nz
        self.groups = -(-(nf + 1) // self.per)
        self.tg = self.groups - 1
        self.chunk = cols // self.n
        self.width = self.chunk + 2 * HALO
        assert self.width % 8 == 0 and self.chunk % 8 == 0 and self.chunk >= HALO
        self.R = self.n * rows
        self.padded = self.width + 2 * PAD
        self.depth_lane = LANES - nz
        self.sw_lane = LANES - nz // 2

    def ty(self):
        return lax.axis_index("ty")

    def is_ocean(self):
        return lax.axis_index("grp") == 0

    def chunk_of(self, ty):
        odd = lax.rem(lax.axis_index("tx"), 2)
        return jnp.where(odd == 0, ty, self.n - 1 - ty)

    def xor(self, mask):
        ty, out, bit = self.ty(), 0, 1
        while bit < self.n:
            here = lax.rem(lax.div(ty, bit), 2)
            out = out + bit * ((1 - here) if mask & bit else here)
            bit *= 2
        return out


def part(src, mask, g):
    n = len(src) // 2
    return src[mask].at[g] if g < SHARED else src[n + mask].at[g - SHARED]


def pack_kernel(p, *refs):
    given, outs, t_ref, here, sems = refs[:5], refs[5 : 5 + 2 * p.n], refs[5 + 2 * p.n], refs[6 + 2 * p.n : 11 + 2 * p.n], refs[11 + 2 * p.n]
    copies = [pltpu.make_async_copy(a, b, sems.at[i]) for i, (a, b) in enumerate(zip(given, here))]
    for copy in copies:
        copy.start()
    for copy in copies:
        copy.wait()
    view, land, bottom, sw, absorb = here
    nz, rows, step = p.nz, p.rows, p.per * p.nz
    half = nz // 2
    ocean = p.is_ocean()

    def aux(r, upper):
        depth = jnp.where(land[r : r + 1, :] == 1, bottom[r : r + 1, :], 0).astype(F32)
        return jnp.concatenate(
            [
                upper,
                jnp.broadcast_to(depth, (half, LANES)),
                jnp.broadcast_to(sw[r : r + 1, :], (half, LANES)),
            ],
            axis=0,
        )

    def field(r, g, count):
        return view[pl.ds(g * step * rows + r, count, stride=rows), :]

    def put(r, g, block):
        t_ref[g, r, HALO : HALO + LANES, :] = block.T

    def send(count):
        for mask in range(p.n):
            start = pl.multiple_of(p.chunk_of(p.xor(mask)) * p.chunk, 8)
            for g in range(count):
                for r in range(rows):
                    part(outs, mask, g)[r] = t_ref[g, r, pl.ds(start, p.width), :]

    zero = jnp.zeros((HALO, LANES), F32)
    for g in range(p.groups):
        for r in range(rows):
            t_ref[g, r, :HALO, :] = zero
            t_ref[g, r, HALO + LANES :, :] = zero

    @pl.when(jnp.logical_not(ocean))
    def _():
        for r in range(rows):
            for g in range(p.groups - 1):
                put(r, g, field(r, g, step))
            have = (p.nf - p.tg * p.per) * nz
            block = field(r, p.tg, have)
            if have < LANES - nz:
                block = jnp.concatenate([block, jnp.zeros((LANES - nz - have, LANES), F32)], axis=0)
            put(r, p.tg, aux(r, block))
        send(p.groups)

    @pl.when(ocean)
    def _():
        lower = (iota((nz, nz), 0) >= iota((nz, nz), 1)).astype(F32)
        for r in range(rows):
            put(r, 0, field(r, 0, step))
            kd = jnp.full((nz, LANES), water_extinction, F32)
            for t in range(p.nf - DYN):
                kd = kd + absorb[t] * view[pl.ds((DYN + t) * nz * rows + r, nz, stride=rows), :]
            below = sw[r : r + 1, :] * jnp.exp(-layer_depth * dot(lower, kd))
            above = below * jnp.exp(layer_depth * kd)
            forcing = (above - below) / layer_depth
            put(r, 1, aux(r, jnp.concatenate([jnp.zeros((2 * nz, LANES), F32), forcing], axis=0)))
        send(2)


def edge_kernel(p, *refs):
    src, z = refs[: 2 * p.n], refs[2 * p.n + 1]
    left = p.chunk_of(p.ty()) == 0

    def copy(lo):
        for mask in range(p.n):
            base = p.xor(mask) * p.rows
            for g in range(p.groups):
                for r in range(p.rows):
                    z[g, base + r] = part(src, mask, g)[r, lo : lo + HALO, :]

    @pl.when(left)
    def _():
        copy(HALO)

    @pl.when(jnp.logical_not(left))
    def _():
        copy(p.chunk)


def assemble(p, src, z, g, dst):
    for mask in range(p.n):
        base = p.xor(mask) * p.rows
        for r in range(p.rows):
            dst[1 + base + r, PAD : PAD + p.width, :] = part(src, mask, g)[r]
    chunk, tx = p.chunk_of(p.ty()), lax.axis_index("tx")

    @pl.when(chunk == 0)
    def _():
        dst[1 : 1 + p.R, PAD : PAD + HALO, :] = jnp.where(tx > 0, z[g], 0.0)

    @pl.when(chunk == p.n - 1)
    def _():
        dst[1 : 1 + p.R, PAD + p.width - HALO : PAD + p.width, :] = jnp.where(
            tx < p.m - 1, z[g], 0.0
        )


def aux_fields(p, aux_ref, wet_ref, sw_ref):
    level = (iota((p.width, LANES), 1) % p.nz).astype(F32)
    for r in range(p.R):
        x = aux_ref[1 + r, PAD : PAD + p.width, :]
        wet_ref[r] = (level < x[:, p.depth_lane : p.depth_lane + 1]).astype(F32)
        sw_ref[r] = jnp.broadcast_to(x[:, p.sw_lane : p.sw_lane + 1], (p.width, LANES))


def lanes_of(p, shape, dim):
    i = iota(shape, dim)
    return i // p.nz, i % p.nz


def copy_matrix(p, slot):
    f0, k0 = lanes_of(p, (LANES, LANES), 0)
    _, k1 = lanes_of(p, (LANES, LANES), 1)
    return ((f0 == slot) & (k0 == k1)).astype(F32)


def cumsum_matrix(p):
    _, k0 = lanes_of(p, (LANES, LANES), 0)
    _, k1 = lanes_of(p, (LANES, LANES), 1)
    return (k0 <= k1).astype(F32)


def sum_matrix(p):
    _, k0 = lanes_of(p, (LANES, LANES), 0)
    _, k1 = lanes_of(p, (LANES, LANES), 1)
    return (k0 == k1).astype(F32)


def optical_depth(p, attenuation):
    _, level = lanes_of(p, attenuation.shape, 1)
    plain = (water_extinction * layer_depth) * (level + 1).astype(F32)
    return layer_depth * dot(attenuation, cumsum_matrix(p)) + plain


def ocean_step(p, d, forcing, wet, out, pp):
    f0, k0 = lanes_of(p, (LANES, LANES), 0)
    _, k1 = lanes_of(p, (LANES, LANES), 1)
    weight = jnp.where(f0 == 2, -0.2, jnp.where(f0 == 3, 0.8, 0.0)) * barotropic_gradient_coefficient
    press = jnp.where(k0 <= k1, weight, 0.0)
    mid = slice(PAD, PAD + p.width)
    for r in range(p.R):
        pp[1 + r, mid, :] = dot(d[1 + r, mid, :], press)
    f, _ = lanes_of(p, (p.width, LANES), 1)
    for r in range(p.R):
        x = d[1 + r, mid, :]
        lap = d[2 + r, mid, :] + d[r, mid, :] + d[1 + r, PAD + 1 : PAD + 1 + p.width, :]
        lap = lap + d[1 + r, PAD - 1 : PAD - 1 + p.width, :] - 4.0 * x
        grad_e = 0.5 * (pp[2 + r, mid, :] - pp[r, mid, :])
        grad_n = 0.5 * (
            pp[1 + r, PAD + 1 : PAD + 1 + p.width, :] - pp[1 + r, PAD - 1 : PAD - 1 + p.width, :]
        )
        of_u = coriolis * pltpu.roll(x, LANES - p.nz, 1) - grad_e
        of_v = -coriolis * pltpu.roll(x, p.nz, 1) - grad_n
        other = jnp.where(f == 2, forcing(r), 0.0)
        extra = jnp.where(f == 0, of_u, jnp.where(f == 1, of_v, other))
        out[r] = wet[r] * (x + integration_interval * (lap + extra))


def clear_pads(p, *refs):
    side = jnp.zeros((PAD, LANES), F32)
    for ref in refs:
        count = ref.shape[0]
        for r in range(count):
            ref[r, :PAD, :] = side
            ref[r, PAD + p.width :, :] = side
        row = jnp.zeros((p.padded, LANES), F32)
        ref[0] = row
        ref[count - 1] = row


def tracer_step(p, d, load_group, wet, sw, absorb, r_hi, r_lo, store, scratch):
    c, feh, fnh, va, ae, le, an, ln, low, rin, rout, adv = scratch
    R, W = p.R, p.width
    mid = slice(PAD, PAD + W)
    up = slice(PAD + 1, PAD + 1 + W)
    down = slice(PAD - 1, PAD - 1 + W)
    clear_pads(p, c, va, ae, le, an, ln, rin, rout)

    flat = jnp.concatenate([d[1 + r, mid, :] for r in range(R)], axis=0)
    ua = dot(flat, copy_matrix(p, 0))
    vv = dot(flat, copy_matrix(p, 1))
    for r in range(R):
        va[1 + r, mid, :] = vv[r * W : (r + 1) * W]
    first = lax.axis_index("tx") * p.cols + p.chunk_of(p.ty()) * p.chunk - HALO
    col = first + iota((W, LANES), 0)
    inside = ((col >= 0) & (col + 1 < p.m * p.cols)).astype(F32)
    half = 0.25 * tracer_interval
    for r in range(R):
        if r + 1 < R:
            feh[r] = half * (ua[r * W : (r + 1) * W] + ua[(r + 1) * W : (r + 2) * W])
        else:
            feh[r] = jnp.zeros((W, LANES), F32)
        fnh[r] = half * (va[1 + r, mid, :] + va[1 + r, up, :]) * inside

    def group(g):
        load_group(g, c)
        for r in range(R):
            c0 = c[1 + r, mid, :]
            cn = c[1 + r, up, :]
            ce = c[2 + r, mid, :]
            f = feh[r]
            a = jnp.abs(f) * (ce - c0)
            ae[1 + r, mid, :] = a
            le[1 + r, mid, :] = f * (ce + c0) - a
            f = fnh[r]
            a = jnp.abs(f) * (cn - c0)
            an[1 + r, mid, :] = a
            ln[1 + r, mid, :] = f * (cn + c0) - a
        for r in range(R):
            c0 = c[1 + r, mid, :]
            cn = c[1 + r, up, :]
            cs = c[1 + r, down, :]
            ce = c[2 + r, mid, :]
            cw = c[r, mid, :]
            lw = c0 - (le[1 + r, mid, :] - le[r, mid, :] + ln[1 + r, mid, :] - ln[1 + r, down, :])
            low[r] = lw
            hi = jnp.maximum(jnp.maximum(jnp.maximum(c0, ce), jnp.maximum(cw, cn)), cs)
            lo = jnp.minimum(jnp.minimum(jnp.minimum(c0, ce), jnp.minimum(cw, cn)), cs)
            e, w = ae[1 + r, mid, :], ae[r, mid, :]
            nn, s = an[1 + r, mid, :], an[1 + r, down, :]
            ep, wp, np_, sp = (jnp.maximum(x, 0.0) for x in (e, w, nn, s))
            em, wm, nm, sm = (jnp.minimum(x, 0.0) for x in (e, w, nn, s))
            gain_in = wp - em + sp - nm
            gain_out = ep - wm + np_ - sm
            floor = ratio_floor * tracer_interval
            rin[1 + r, mid, :] = jnp.minimum(gain_in, jnp.maximum(hi - lw, 0.0)) / jnp.maximum(
                gain_in, floor
            )
            rout[1 + r, mid, :] = jnp.minimum(gain_out, jnp.maximum(lw - lo, 0.0)) / jnp.maximum(
                gain_out, floor
            )
        before = jnp.zeros((W, LANES), F32)
        for r in range(R):
            ri, ro = rin[1 + r, mid, :], rout[1 + r, mid, :]
            a = ae[1 + r, mid, :]
            east = a * jnp.where(
                a >= 0.0,
                jnp.minimum(rin[2 + r, mid, :], ro),
                jnp.minimum(ri, rout[2 + r, mid, :]),
            )
            a = an[1 + r, mid, :]
            north = a * jnp.where(
                a >= 0.0,
                jnp.minimum(rin[1 + r, up, :], ro),
                jnp.minimum(ri, rout[1 + r, up, :]),
            )
            ln[1 + r, mid, :] = north
            adv[g, r] = low[r] - (east - before + north - ln[1 + r, down, :])
            before = east
        return 0

    for g in range(p.tg):
        group(g)

    whole = [adv[g].reshape(R * W, LANES) for g in range(p.tg)]
    att = whole[0] * absorb[0:1, :]
    for g in range(1, p.tg):
        att = att + whole[g] * absorb[g : g + 1, :]
    light = sw[...].reshape(R * W, LANES) * jnp.exp(-optical_depth(p, att))
    warm = jnp.exp(0.063 * flat) * pltpu.roll(1.0 + 0.2 * jnp.tanh(flat), LANES - p.nz, 1)
    growth = (
        (growth_peak * tracer_interval) * dot(warm, copy_matrix(p, 2)) * light / (light + half_light)
    )
    every = jnp.concatenate(whole, axis=1)
    hi = every.astype(BF16)
    lo = (every - hi.astype(F32)).astype(BF16)

    def mm(a, b):
        return jnp.dot(a, b, preferred_element_type=F32)

    mixed = mm(hi, r_hi[...]) + mm(lo, r_hi[...]) + mm(hi, r_lo[...])
    wets = wet[...].reshape(R * W, LANES)
    for g in range(p.tg):
        new = wets * (whole[g] + growth * mixed[:, g * LANES : (g + 1) * LANES])
        store(g, new.reshape(R, W, LANES))


def ocean_first_kernel(p, *refs):
    src, z, dyn, wet, sw, d, aux, pp = (refs[: 2 * p.n],) + refs[2 * p.n :]

    @pl.when(p.is_ocean())
    def _():
        clear_pads(p, d, aux, pp)
        assemble(p, src, z, 0, d)
        assemble(p, src, z, 1, aux)
        aux_fields(p, aux, wet, sw)
        ocean_step(p, d, lambda r: aux[1 + r, PAD : PAD + p.width, :], wet, dyn, pp)


def tracer_first_kernel(p, *refs):
    src, (z, absorb, r_hi, r_lo, _, c1, wet, sw, d), scratch = refs[: 2 * p.n], refs[2 * p.n : 2 * p.n + 9], refs[2 * p.n + 9 :]

    @pl.when(jnp.logical_not(p.is_ocean()))
    def _():
        c = scratch[0]
        clear_pads(p, d)
        assemble(p, src, z, p.groups - 1, c)
        aux_fields(p, c, wet, sw)
        assemble(p, src, z, 0, d)

        def load(g, dst):
            assemble(p, src, z, g + 1, dst)

        def store(g, value):
            c1[g] = value

        tracer_step(p, d, load, wet, sw, absorb, r_hi, r_lo, store, scratch)


def load_dyn(p, dyn, d):
    clear_pads(p, d)
    for r in range(p.R):
        d[1 + r, PAD : PAD + p.width, :] = dyn[r]


def put_back(p, outs, group, value):
    for mask in range(p.n):
        outs[mask][group] = value(p.xor(mask) * p.rows)


def tracer_second_kernel(p, *refs):
    dyn, c1, wet, sw, absorb, r_hi, r_lo = refs[:7]
    outs, (d, c2), scratch = refs[7 : 7 + p.n], refs[7 + p.n : 9 + p.n], refs[9 + p.n :]
    core = slice(HALO, HALO + p.chunk)

    @pl.when(jnp.logical_not(p.is_ocean()))
    def _():
        load_dyn(p, dyn, d)

        def load(g, dst):
            for r in range(p.R):
                dst[1 + r, PAD : PAD + p.width, :] = c1[g, r]

        def store(g, value):
            c2[...] = value
            put_back(p, outs, g + 1, lambda row: c2[pl.ds(row, p.rows), core, :])

        tracer_step(p, d, load, wet, sw, absorb, r_hi, r_lo, store, scratch)
        put_back(p, outs, 0, lambda row: dyn[pl.ds(row, p.rows), core, :])


def ocean_second_kernel(p, *refs):
    dyn, c1, wet, sw, absorb = refs[:5]
    same, outs, (d, pp, heat, dyn2) = refs[5 : 5 + p.n], refs[5 + p.n : 5 + 2 * p.n], refs[5 + 2 * p.n :]
    core = slice(HALO, HALO + p.chunk)

    @pl.when(jnp.logical_not(p.is_ocean()))
    def _():
        for mask in range(p.n):
            outs[mask][...] = same[mask][...]

    @pl.when(p.is_ocean())
    def _():
        load_dyn(p, dyn, d)
        clear_pads(p, pp)
        flat = (p.R * p.width, LANES)
        att = c1[0].reshape(flat) * absorb[0:1, :]
        for g in range(1, p.tg):
            att = att + c1[g].reshape(flat) * absorb[g : g + 1, :]
        below = sw[...].reshape(flat) * jnp.exp(-optical_depth(p, att))
        kd = dot(att, sum_matrix(p)) + water_extinction
        above = below * jnp.exp(layer_depth * kd)
        heat[...] = ((above - below) / layer_depth).reshape(heat.shape)
        ocean_step(p, d, lambda r: heat[r], wet, dyn2, pp)
        put_back(p, outs, 0, lambda row: dyn2[pl.ds(row, p.rows), core, :])
        for g in range(p.tg):
            put_back(p, outs, g + 1, lambda row: c1[g, pl.ds(row, p.rows), core, :])


def unpack_kernel(p, *refs):
    src, out, t_ref = refs[: p.n], refs[p.n], refs[p.n + 1]
    step = p.per * p.nz
    for g in range(p.groups):
        count = min(step, (p.nf - g * p.per) * p.nz)
        for r in range(p.rows):
            for mask in range(p.n):
                start = pl.multiple_of(p.chunk_of(p.xor(mask)) * p.chunk, 8)
                t_ref[pl.ds(start, p.chunk), :] = src[mask][g, r]
            out[pl.ds(g * step * p.rows + r, count, stride=p.rows), :] = t_ref[...].T[:count]


def mix_kernel(p, reaction, r_hi, r_lo):
    size = p.tg * LANES
    spread = (iota((size, LANES), 0) // p.nz == iota((size, LANES), 1)).astype(F32)
    rows = lax.dot_general(
        spread, reaction[...], (((1,), (1,)), ((), ())), precision=HIGHEST, preferred_element_type=F32
    )
    full = lax.dot_general(
        rows, spread, (((1,), (1,)), ((), ())), precision=HIGHEST, preferred_element_type=F32
    )
    same = iota((size, size), 0) % p.nz == iota((size, size), 1) % p.nz
    full = jnp.where(same, full, 0.0)
    hi = full.astype(BF16)
    r_hi[...] = hi
    r_lo[...] = (full - hi.astype(F32)).astype(BF16)


def solution(mesh):
    def local(coupled_state, land_mask, bottom_level, shortwave, absorb, reaction):
        view = coupled_state[0]
        p = Plan(mesh, *view.shape)
        n, G, R, W = p.n, p.groups, p.R, p.width

        def sds(*shape, dtype=F32):
            return jax.ShapeDtypeStruct(shape, dtype)

        def call(kernel, outs, ins, scratch=(), in_specs=None, aliases=None, cost=1):
            return pl.pallas_call(
                functools.partial(kernel, p),
                out_shape=outs,
                in_specs=in_specs or [VMEM] * len(ins),
                out_specs=jax.tree.map(lambda _: VMEM, outs),
                scratch_shapes=[pltpu.VMEM(s, F32) if isinstance(s, tuple) else s for s in scratch],
                input_output_aliases=aliases or {},
                cost_estimate=pl.CostEstimate(
                    flops=cost * 10**9, bytes_accessed=cost * 10**6, transcendentals=0
                ),
                compiler_params=pltpu.CompilerParams(vmem_limit_bytes=20 * 2**20),
            )(*ins)

        def swap(value, mask):
            return lax.ppermute(value, "ty", [(i, i ^ mask) for i in range(n)])

        def swap_tracers(value, mask):
            size = p.m
            pairs = [(t * size + x, t * size + (x ^ 1)) for t in range(n) for x in range(size)]
            both = n * size
            pairs += [
                (both + t * size + x, both + (t ^ mask) * size + x)
                for t in range(n)
                for x in range(size)
            ]
            return lax.ppermute(value, ("grp", "ty", "tx"), pairs)

        def edges(value):
            size = p.m
            to = {i: (i + n * size) % (2 * n * size) for i in range(2 * n * size)}
            for tx in range(size - 1):
                for grp in range(2):
                    a = (grp * n + (n - 1 if tx % 2 == 0 else 0)) * size + tx
                    to[a], to[a + 1] = a + 1, a
            return lax.ppermute(value, ("grp", "ty", "tx"), list(to.items()))

        def across(value):
            return lax.ppermute(value, "grp", [(0, 1), (1, 0)])

        flat = view.reshape(p.nf * p.nz * p.rows, p.cols)
        packed = call(
            pack_kernel,
            [sds(SHARED, p.rows, W, LANES)] * n + [sds(G - SHARED, p.rows, W, LANES)] * n,
            [pltpu.with_memory_space_constraint(x, pltpu.HBM) for x in (flat, land_mask, bottom_level, shortwave, absorb)],
            [
                (G, p.rows, LANES + 2 * HALO, LANES),
                pltpu.VMEM(flat.shape, F32),
                pltpu.VMEM(land_mask.shape, jnp.int32),
                pltpu.VMEM(bottom_level.shape, jnp.int32),
                pltpu.VMEM(shortwave.shape, F32),
                pltpu.SMEM(absorb.shape, F32),
                pltpu.SemaphoreType.DMA((5,)),
            ],
            [HBM] * 5,
        )
        got = [packed[0]] + [swap(packed[k], k) for k in range(1, n)]
        got += [packed[n]] + [swap_tracers(packed[n + k], k) for k in range(1, n)]

        react = jnp.pad(reaction, ((0, LANES - reaction.shape[0]), (0, LANES - reaction.shape[1])))
        size = p.tg * LANES
        r_hi, r_lo = call(mix_kernel, [sds(size, size, dtype=BF16), sds(size, size, dtype=BF16)], [react])
        weights = jnp.pad(absorb, (0, p.tg * p.per - absorb.shape[0])).reshape(p.tg, p.per)
        weights = jnp.repeat(weights, p.nz, axis=1)

        z = edges(call(edge_kernel, [sds(G, R, HALO, LANES)], got + [r_hi], in_specs=[VMEM] * (2 * n) + [ANY])[0])

        padded = (R + 2, p.padded, LANES)
        block = (R, W, LANES)
        scratch = [padded, block, block] + [padded] * 5 + [block] + [padded] * 2 + [(p.tg,) + block]
        dyn1, wet_o, sw_o = call(ocean_first_kernel, [sds(*block)] * 3, got + [z], [padded] * 3)

        dyn1_t = across(dyn1)
        c1, wet_t, sw_t = call(
            tracer_first_kernel,
            [sds(p.tg, *block), sds(*block), sds(*block)],
            got + [z, weights, r_hi, r_lo, dyn1],
            [padded] + scratch,
            [VMEM] * (2 * n + 4) + [ANY],
            cost=4,
        )
        c1_o = across(c1)
        back = [sds(G, p.rows, p.chunk, LANES)] * n
        outs = call(
            tracer_second_kernel,
            back,
            [dyn1_t, c1, wet_t, sw_t, weights, r_hi, r_lo],
            [padded, block] + scratch,
            cost=4,
        )
        outs = call(
            ocean_second_kernel,
            back,
            [dyn1, c1_o, wet_o, sw_o, weights] + list(outs),
            [padded, padded, block, block],
            aliases={5 + k: k for k in range(n)},
        )
        home = [outs[0]] + [
            swap(outs[k], k) for k in range(1, n)
        ]
        out = call(unpack_kernel, [sds(p.nf * p.nz * p.rows, p.cols)], home, [(LANES, LANES)])[0]
        return out.reshape((1,) + view.shape)

    in_specs = (
        P("grp", None, None, "ty", "tx"),
        P("ty", "tx"),
        P("ty", "tx"),
        P("ty", "tx"),
        P(),
        P(),
    )
    out_specs = P("grp", None, None, "ty", "tx")
    return jax.shard_map(local, mesh=mesh, in_specs=in_specs, out_specs=out_specs, check_vma=False)
```

```python
import functools

import jax
import jax.numpy as jnp
from jax import lax
from jax.experimental import pallas as pl
from jax.experimental.pallas import tpu as pltpu
from jax.sharding import PartitionSpec as P


STEPS = 2
HALO = 2 * STEPS
LANES = 128
PAD = 8
DYN = 4
SHARED = 2

integration_interval = 0.1
tracer_interval = 0.08
coriolis = 0.8
barotropic_gradient_coefficient = 0.1
water_extinction = 0.04
layer_depth = 0.05
growth_peak = 2.0
half_light = 0.5
ratio_floor = 0.01

F32 = jnp.float32
BF16 = jnp.bfloat16
HIGHEST = lax.Precision.HIGHEST
VMEM = pl.BlockSpec(memory_space=pltpu.VMEM)
SMEM = pl.BlockSpec(memory_space=pltpu.SMEM)
ANY = pl.BlockSpec(memory_space=pl.ANY)
HBM = pl.BlockSpec(memory_space=pltpu.HBM)


def dot(a, b):
    return jnp.dot(a, b, precision=HIGHEST, preferred_element_type=F32)


def iota(shape, dim):
    return lax.broadcasted_iota(jnp.int32, shape, dim)


class Plan:
    def __init__(self, mesh, nf, nz, rows, cols):
        self.n, self.m = mesh.shape["ty"], mesh.shape["tx"]
        self.nf, self.nz, self.rows, self.cols = nf, nz, rows, cols
        assert cols == LANES and LANES % nz == 0 and LANES // nz == DYN
        assert self.n & (self.n - 1) == 0 and self.n > 1
        self.per = LANES // nz
        self.groups = -(-(nf + 1) // self.per)
        self.tg = self.groups - 1
        self.chunk = cols // self.n
        self.width = self.chunk + 2 * HALO
        assert self.width % 8 == 0 and self.chunk % 8 == 0 and self.chunk >= HALO
        self.R = self.n * rows
        self.padded = self.width + 2 * PAD
        self.depth_lane = LANES - nz
        self.sw_lane = LANES - nz // 2

    def ty(self):
        return lax.axis_index("ty")

    def is_ocean(self):
        return lax.axis_index("grp") == 0

    def chunk_of(self, ty):
        odd = lax.rem(lax.axis_index("tx"), 2)
        return jnp.where(odd == 0, ty, self.n - 1 - ty)

    def xor(self, mask):
        ty, out, bit = self.ty(), 0, 1
        while bit < self.n:
            here = lax.rem(lax.div(ty, bit), 2)
            out = out + bit * ((1 - here) if mask & bit else here)
            bit *= 2
        return out


def part(src, mask, g):
    n = len(src) // 2
    return src[mask].at[g] if g < SHARED else src[n + mask].at[g - SHARED]


def pack_kernel(p, *refs):
    given, outs, t_ref, here, sems = refs[:5], refs[5 : 5 + 2 * p.n], refs[5 + 2 * p.n], refs[6 + 2 * p.n : 11 + 2 * p.n], refs[11 + 2 * p.n]
    copies = [pltpu.make_async_copy(a, b, sems.at[i]) for i, (a, b) in enumerate(zip(given, here))]
    for copy in copies:
        copy.start()
    for copy in copies:
        copy.wait()
    view, land, bottom, sw, absorb = here
    nz, rows, step = p.nz, p.rows, p.per * p.nz
    half = nz // 2
    ocean = p.is_ocean()

    def aux(r, upper):
        depth = jnp.where(land[r : r + 1, :] == 1, bottom[r : r + 1, :], 0).astype(F32)
        return jnp.concatenate(
            [
                upper,
                jnp.broadcast_to(depth, (half, LANES)),
                jnp.broadcast_to(sw[r : r + 1, :], (half, LANES)),
            ],
            axis=0,
        )

    def field(r, g, count):
        return view[pl.ds(g * step * rows + r, count, stride=rows), :]

    def put(r, g, block):
        t_ref[g, r, HALO : HALO + LANES, :] = block.T

    def send(count):
        for mask in range(p.n):
            start = pl.multiple_of(p.chunk_of(p.xor(mask)) * p.chunk, 8)
            for g in range(count):
                for r in range(rows):
                    part(outs, mask, g)[r] = t_ref[g, r, pl.ds(start, p.width), :]

    zero = jnp.zeros((HALO, LANES), F32)
    for g in range(p.groups):
        for r in range(rows):
            t_ref[g, r, :HALO, :] = zero
            t_ref[g, r, HALO + LANES :, :] = zero

    @pl.when(jnp.logical_not(ocean))
    def _():
        for r in range(rows):
            for g in range(p.groups - 1):
                put(r, g, field(r, g, step))
            have = (p.nf - p.tg * p.per) * nz
            block = field(r, p.tg, have)
            if have < LANES - nz:
                block = jnp.concatenate([block, jnp.zeros((LANES - nz - have, LANES), F32)], axis=0)
            put(r, p.tg, aux(r, block))
        send(p.groups)

    @pl.when(ocean)
    def _():
        lower = (iota((nz, nz), 0) >= iota((nz, nz), 1)).astype(F32)
        for r in range(rows):
            put(r, 0, field(r, 0, step))
            kd = jnp.full((nz, LANES), water_extinction, F32)
            for t in range(p.nf - DYN):
                kd = kd + absorb[t] * view[pl.ds((DYN + t) * nz * rows + r, nz, stride=rows), :]
            below = sw[r : r + 1, :] * jnp.exp(-layer_depth * dot(lower, kd))
            above = below * jnp.exp(layer_depth * kd)
            forcing = (above - below) / layer_depth
            put(r, 1, aux(r, jnp.concatenate([jnp.zeros((2 * nz, LANES), F32), forcing], axis=0)))
        send(2)


def edge_kernel(p, *refs):
    src, z = refs[: 2 * p.n], refs[2 * p.n + 1]
    left = p.chunk_of(p.ty()) == 0

    def copy(lo):
        for mask in range(p.n):
            base = p.xor(mask) * p.rows
            for g in range(p.groups):
                for r in range(p.rows):
                    z[g, base + r] = part(src, mask, g)[r, lo : lo + HALO, :]

    @pl.when(left)
    def _():
        copy(HALO)

    @pl.when(jnp.logical_not(left))
    def _():
        copy(p.chunk)


def assemble(p, src, z, g, dst):
    for mask in range(p.n):
        base = p.xor(mask) * p.rows
        for r in range(p.rows):
            dst[1 + base + r, PAD : PAD + p.width, :] = part(src, mask, g)[r]
    chunk, tx = p.chunk_of(p.ty()), lax.axis_index("tx")

    @pl.when(chunk == 0)
    def _():
        dst[1 : 1 + p.R, PAD : PAD + HALO, :] = jnp.where(tx > 0, z[g], 0.0)

    @pl.when(chunk == p.n - 1)
    def _():
        dst[1 : 1 + p.R, PAD + p.width - HALO : PAD + p.width, :] = jnp.where(
            tx < p.m - 1, z[g], 0.0
        )


def aux_fields(p, aux_ref, wet_ref, sw_ref):
    level = (iota((p.width, LANES), 1) % p.nz).astype(F32)
    for r in range(p.R):
        x = aux_ref[1 + r, PAD : PAD + p.width, :]
        wet_ref[r] = (level < x[:, p.depth_lane : p.depth_lane + 1]).astype(F32)
        sw_ref[r] = jnp.broadcast_to(x[:, p.sw_lane : p.sw_lane + 1], (p.width, LANES))


def lanes_of(p, shape, dim):
    i = iota(shape, dim)
    return i // p.nz, i % p.nz


def spread(p, x, slot):
    f, _ = lanes_of(p, x.shape, 1)
    return field_sum(p, jnp.where(f == slot, x, 0.0))


def field_sum(p, x):
    shift = p.nz
    while shift < LANES:
        x = x + pltpu.roll(x, shift, 1)
        shift *= 2
    return x


def level_sum(p, x):
    _, k0 = lanes_of(p, (LANES, LANES), 0)
    _, k1 = lanes_of(p, (LANES, LANES), 1)
    ones = (k0 <= k1).astype(F32).astype(BF16)
    hi = x.astype(BF16)
    rest = x - hi.astype(F32)
    mid = rest.astype(BF16)
    lo = (rest - mid.astype(F32)).astype(BF16)
    return jnp.dot(
        jnp.concatenate([hi, mid, lo], axis=1),
        jnp.concatenate([ones] * 3, axis=0),
        preferred_element_type=F32,
    )


def optical_depth(p, attenuation):
    _, level = lanes_of(p, attenuation.shape, 1)
    plain = (water_extinction * layer_depth) * (level + 1).astype(F32)
    return layer_depth * level_sum(p, attenuation) + plain


def ocean_step(p, d, forcing, wet, out, pp):
    mid = slice(PAD, PAD + p.width)
    flat = jnp.concatenate([d[1 + r, mid, :] for r in range(p.R)], axis=0)
    f, _ = lanes_of(p, flat.shape, 1)
    weight = jnp.where(f == 2, -0.2, jnp.where(f == 3, 0.8, 0.0)) * barotropic_gradient_coefficient
    press = level_sum(p, weight * flat)
    for r in range(p.R):
        pp[1 + r, mid, :] = press[r * p.width : (r + 1) * p.width]
    f, _ = lanes_of(p, (p.width, LANES), 1)
    for r in range(p.R):
        x = d[1 + r, mid, :]
        lap = d[2 + r, mid, :] + d[r, mid, :] + d[1 + r, PAD + 1 : PAD + 1 + p.width, :]
        lap = lap + d[1 + r, PAD - 1 : PAD - 1 + p.width, :] - 4.0 * x
        grad_e = 0.5 * (pp[2 + r, mid, :] - pp[r, mid, :])
        grad_n = 0.5 * (
            pp[1 + r, PAD + 1 : PAD + 1 + p.width, :] - pp[1 + r, PAD - 1 : PAD - 1 + p.width, :]
        )
        of_u = coriolis * pltpu.roll(x, LANES - p.nz, 1) - grad_e
        of_v = -coriolis * pltpu.roll(x, p.nz, 1) - grad_n
        other = jnp.where(f == 2, forcing(r), 0.0)
        extra = jnp.where(f == 0, of_u, jnp.where(f == 1, of_v, other))
        out[r] = wet[r] * (x + integration_interval * (lap + extra))


def clear_pads(p, *refs):
    side = jnp.zeros((PAD, LANES), F32)
    for ref in refs:
        count = ref.shape[0]
        for r in range(count):
            ref[r, :PAD, :] = side
            ref[r, PAD + p.width :, :] = side
        row = jnp.zeros((p.padded, LANES), F32)
        ref[0] = row
        ref[count - 1] = row


def tracer_step(p, d, load_group, wet, sw, absorb, mix, store, scratch, lo, count):
    c, feh, fnh, va, ae, le, an, ln, low, rin, rout, fe, adv = scratch
    R, W = p.R, p.width
    mid = slice(PAD, PAD + W)
    up = slice(PAD + 1, PAD + 1 + W)
    down = slice(PAD - 1, PAD - 1 + W)
    win = slice(PAD + lo, PAD + lo + count)
    clear_pads(p, va)
    for g in range(p.tg):
        clear_pads(p, *(x.at[g] for x in (c, ae, le, an, ln, rin, rout)))

    flat = jnp.concatenate([d[1 + r, mid, :] for r in range(R)], axis=0)
    ua = spread(p, flat, 0)
    vv = spread(p, flat, 1)
    for r in range(R):
        va[1 + r, mid, :] = vv[r * W : (r + 1) * W]
    first = lax.axis_index("tx") * p.cols + p.chunk_of(p.ty()) * p.chunk - HALO
    col = first + iota((W, LANES), 0)
    inside = ((col >= 0) & (col + 1 < p.m * p.cols)).astype(F32)
    half = 0.25 * tracer_interval
    for r in range(R):
        if r + 1 < R:
            feh[r] = half * (ua[r * W : (r + 1) * W] + ua[(r + 1) * W : (r + 2) * W])
        else:
            feh[r] = jnp.zeros((W, LANES), F32)
        fnh[r] = half * (va[1 + r, mid, :] + va[1 + r, up, :]) * inside

    def faces(g, r):
        c0 = c[g, 1 + r, mid, :]
        cn = c[g, 1 + r, up, :]
        ce = c[g, 2 + r, mid, :]
        f = feh[r]
        a = jnp.abs(f) * (ce - c0)
        ae[g, 1 + r, mid, :] = a
        le[g, 1 + r, mid, :] = f * (ce + c0) - a
        f = fnh[r]
        a = jnp.abs(f) * (cn - c0)
        an[g, 1 + r, mid, :] = a
        ln[g, 1 + r, mid, :] = f * (cn + c0) - a

    def ratios(g, r):
        c0 = c[g, 1 + r, mid, :]
        cn = c[g, 1 + r, up, :]
        cs = c[g, 1 + r, down, :]
        ce = c[g, 2 + r, mid, :]
        cw = c[g, r, mid, :]
        lw = c0 - (
            le[g, 1 + r, mid, :] - le[g, r, mid, :] + ln[g, 1 + r, mid, :] - ln[g, 1 + r, down, :]
        )
        low[g, r] = lw
        high = jnp.maximum(jnp.maximum(jnp.maximum(c0, ce), jnp.maximum(cw, cn)), cs)
        least = jnp.minimum(jnp.minimum(jnp.minimum(c0, ce), jnp.minimum(cw, cn)), cs)
        e, w = ae[g, 1 + r, mid, :], ae[g, r, mid, :]
        nn, s = an[g, 1 + r, mid, :], an[g, 1 + r, down, :]
        ep, wp, np_, sp = (jnp.maximum(x, 0.0) for x in (e, w, nn, s))
        positive = (ep + wp) + (np_ + sp)
        gain_in = positive - (e + nn)
        gain_out = positive - (w + s)
        floor = ratio_floor * tracer_interval
        rin[g, 1 + r, mid, :] = jnp.minimum(gain_in, jnp.maximum(high - lw, 0.0)) / jnp.maximum(
            gain_in, floor
        )
        rout[g, 1 + r, mid, :] = jnp.minimum(gain_out, jnp.maximum(lw - least, 0.0)) / jnp.maximum(
            gain_out, floor
        )

    def limited(g, r):
        a = an[g, 1 + r, mid, :]
        north = a * jnp.where(
            a >= 0.0,
            jnp.minimum(rin[g, 1 + r, up, :], rout[g, 1 + r, mid, :]),
            jnp.minimum(rin[g, 1 + r, mid, :], rout[g, 1 + r, up, :]),
        )
        ln[g, 1 + r, mid, :] = north
        a = ae[g, 1 + r, win, :]
        east = a * jnp.where(
            a >= 0.0,
            jnp.minimum(rin[g, 2 + r, win, :], rout[g, 1 + r, win, :]),
            jnp.minimum(rin[g, 1 + r, win, :], rout[g, 2 + r, win, :]),
        )
        fe[g, r] = east
        south = ln[g, 1 + r, PAD + lo - 1 : PAD + lo - 1 + count, :]
        div = east + (ln[g, 1 + r, win, :] - south)
        if r:
            div = div - fe[g, r - 1]
        adv[g, r] = low[g, r, lo : lo + count, :] - div

    def column(r0, r1):
        shape = ((r1 - r0) * count, LANES)
        whole = [adv[g, r0:r1].reshape(shape) for g in range(p.tg)]
        att = whole[0] * absorb[0:1, :]
        for g in range(1, p.tg):
            att = att + whole[g] * absorb[g : g + 1, :]
        light = sw[r0:r1, lo : lo + count, :].reshape(shape) * jnp.exp(-optical_depth(p, att))
        x = jnp.concatenate([d[1 + r, win, :] for r in range(r0, r1)], axis=0)
        warm = jnp.exp(0.063 * x) * pltpu.roll(1.0 + 0.2 * jnp.tanh(x), LANES - p.nz, 1)
        growth = (
            (growth_peak * tracer_interval) * spread(p, warm, 2) * light / (light + half_light)
        )
        every = jnp.concatenate(whole, axis=1)
        hi = every.astype(BF16)
        rest = (every - hi.astype(F32)).astype(BF16)
        mixed = jnp.dot(
            jnp.concatenate([hi, rest, hi], axis=1), mix[...], preferred_element_type=F32
        )
        wets = wet[r0:r1, lo : lo + count, :].reshape(shape)
        for g in range(p.tg):
            new = wets * (whole[g] + growth * mixed[:, g * LANES : (g + 1) * LANES])
            store(g, r0, r1, new.reshape(r1 - r0, count, LANES))

    h = (5 * R) // 8
    for g in range(p.tg):
        load_group(g, c.at[g])
        for r in range(h + 1):
            faces(g, r)
        for r in range(h + 1):
            ratios(g, r)
        for r in range(h):
            limited(g, r)
    column(0, h)
    for g in range(p.tg):
        for r in range(h + 1, R):
            faces(g, r)
        for r in range(h + 1, R):
            ratios(g, r)
        for r in range(h, R):
            limited(g, r)
    column(h, R)


def ocean_first_kernel(p, *refs):
    src, z, dyn, wet, sw, d, aux, pp = (refs[: 2 * p.n],) + refs[2 * p.n :]

    @pl.when(p.is_ocean())
    def _():
        clear_pads(p, d, aux, pp)
        assemble(p, src, z, 0, d)
        assemble(p, src, z, 1, aux)
        aux_fields(p, aux, wet, sw)
        ocean_step(p, d, lambda r: aux[1 + r, PAD : PAD + p.width, :], wet, dyn, pp)


def tracer_first_kernel(p, *refs):
    src, (z, absorb, mix, _, c1, core, wet, sw, d, spare), scratch = (
        refs[: 2 * p.n],
        refs[2 * p.n : 2 * p.n + 10],
        refs[2 * p.n + 10 :],
    )

    @pl.when(jnp.logical_not(p.is_ocean()))
    def _():
        clear_pads(p, d)
        assemble(p, src, z, p.groups - 1, spare)
        aux_fields(p, spare, wet, sw)
        assemble(p, src, z, 0, d)

        def load(g, dst):
            assemble(p, src, z, g + 1, dst)

        def store(g, r0, r1, value):
            c1[g, r0:r1] = value
            core[g, r0:r1] = c1[g, r0:r1, HALO : HALO + p.chunk, :]

        tracer_step(p, d, load, wet, sw, absorb, mix, store, scratch, 0, p.width)


def load_dyn(p, dyn, d):
    clear_pads(p, d)
    for r in range(p.R):
        d[1 + r, PAD : PAD + p.width, :] = dyn[r]


def put_back(p, outs, group, value):
    for mask in range(p.n):
        outs[mask][group] = value(p.xor(mask) * p.rows)


def tracer_second_kernel(p, *refs):
    dyn, c1, wet, sw, absorb, mix = refs[:6]
    outs, (d, c2), scratch = refs[6 : 6 + p.n], refs[6 + p.n : 8 + p.n], refs[8 + p.n :]
    core = slice(HALO, HALO + p.chunk)

    @pl.when(jnp.logical_not(p.is_ocean()))
    def _():
        load_dyn(p, dyn, d)

        def load(g, dst):
            for r in range(p.R):
                dst[1 + r, PAD : PAD + p.width, :] = c1[g, r]

        def store(g, r0, r1, value):
            c2[g, r0:r1] = value

        tracer_step(p, d, load, wet, sw, absorb, mix, store, scratch, HALO, p.chunk)
        for g in range(p.tg):
            put_back(p, outs, g + 1, lambda row: c2[g, pl.ds(row, p.rows)])
        put_back(p, outs, 0, lambda row: dyn[pl.ds(row, p.rows), core, :])


def ocean_second_kernel(p, *refs):
    dyn, c1, wet, sw, absorb = refs[:5]
    same, outs, (d, pp, heat, dyn2) = refs[5 : 5 + p.n], refs[5 + p.n : 5 + 2 * p.n], refs[5 + 2 * p.n :]
    core = slice(HALO, HALO + p.chunk)

    @pl.when(jnp.logical_not(p.is_ocean()))
    def _():
        for mask in range(p.n):
            outs[mask][...] = same[mask][...]

    @pl.when(p.is_ocean())
    def _():
        load_dyn(p, dyn, d)
        clear_pads(p, pp)
        flat = (p.R * p.chunk, LANES)
        att = c1[0].reshape(flat) * absorb[0:1, :]
        for g in range(1, p.tg):
            att = att + c1[g].reshape(flat) * absorb[g : g + 1, :]
        below = sw[:, core, :].reshape(flat) * jnp.exp(-optical_depth(p, att))
        kd = field_sum(p, att) + water_extinction
        above = below * jnp.exp(layer_depth * kd)
        heat[...] = jnp.zeros(heat.shape, F32)
        heat[:, core, :] = ((above - below) / layer_depth).reshape(p.R, p.chunk, LANES)
        ocean_step(p, d, lambda r: heat[r], wet, dyn2, pp)
        put_back(p, outs, 0, lambda row: dyn2[pl.ds(row, p.rows), core, :])
        for g in range(p.tg):
            put_back(p, outs, g + 1, lambda row: c1[g, pl.ds(row, p.rows)])


def unpack_kernel(p, *refs):
    src, out, t_ref = refs[: p.n], refs[p.n], refs[p.n + 1]
    step = p.per * p.nz
    for g in range(p.groups):
        count = min(step, (p.nf - g * p.per) * p.nz)
        for r in range(p.rows):
            for mask in range(p.n):
                start = pl.multiple_of(p.chunk_of(p.xor(mask)) * p.chunk, 8)
                t_ref[pl.ds(start, p.chunk), :] = src[mask][g, r]
            out[pl.ds(g * step * p.rows + r, count, stride=p.rows), :] = t_ref[...].T[:count]


def mix_kernel(p, reaction_hbm, absorb_hbm, mix, weights, small, reaction, absorb, sems):
    size = p.tg * LANES
    copies = [
        pltpu.make_async_copy(reaction_hbm, reaction, sems.at[0]),
        pltpu.make_async_copy(absorb_hbm, absorb, sems.at[1]),
    ]
    for copy in copies:
        copy.start()
    for copy in copies:
        copy.wait()
    small[...] = jnp.zeros((LANES, LANES), F32)
    small[: p.nf - DYN, : p.nf - DYN] = reaction[...]
    hi = small[...].astype(BF16)
    lo = (small[...] - hi.astype(F32)).astype(BF16)
    expand = (iota((size, LANES), 0) // p.nz == iota((size, LANES), 1)).astype(F32).astype(BF16)
    same = (iota((LANES, LANES), 0) % p.nz == iota((LANES, LANES), 1) % p.nz).astype(F32)

    def wide(value):
        dims = (((1,), (1,)), ((), ()))
        rows = lax.dot_general(expand, value, dims, preferred_element_type=F32).astype(BF16)
        return lax.dot_general(rows, expand, dims, preferred_element_type=F32)

    for value, starts in ((hi, (0, size)), (lo, (2 * size,))):
        full = wide(value)
        for i in range(p.tg):
            for j in range(p.tg):
                at = slice(j * LANES, (j + 1) * LANES)
                block = (full[i * LANES : (i + 1) * LANES, at] * same).astype(BF16)
                for start in starts:
                    mix[start + i * LANES : start + (i + 1) * LANES, at] = block
    f, _ = lanes_of(p, (1, LANES), 1)
    for g in range(p.tg):
        row = jnp.zeros((1, LANES), F32)
        for k in range(p.per):
            t = g * p.per + k
            if t < p.nf - DYN:
                row = jnp.where(f == k, absorb[t], row)
        weights[g : g + 1, :] = row


def solution(mesh):
    def local(coupled_state, land_mask, bottom_level, shortwave, absorb, reaction):
        view = coupled_state[0]
        p = Plan(mesh, *view.shape)
        n, G, R, W = p.n, p.groups, p.R, p.width

        def sds(*shape, dtype=F32):
            return jax.ShapeDtypeStruct(shape, dtype)

        def call(kernel, outs, ins, scratch=(), in_specs=None, aliases=None, cost=1):
            return pl.pallas_call(
                functools.partial(kernel, p),
                out_shape=outs,
                in_specs=in_specs or [VMEM] * len(ins),
                out_specs=jax.tree.map(lambda _: VMEM, outs),
                scratch_shapes=[pltpu.VMEM(s, F32) if isinstance(s, tuple) else s for s in scratch],
                input_output_aliases=aliases or {},
                cost_estimate=pl.CostEstimate(
                    flops=cost * 10**8, bytes_accessed=cost * 10**5, transcendentals=0
                ),
                compiler_params=pltpu.CompilerParams(
                    vmem_limit_bytes=(20 if cost > 1 else 10) * 2**20,
                ),
            )(*ins)

        def swap(value, mask):
            return lax.ppermute(value, "ty", [(i, i ^ mask) for i in range(n)])

        def swap_tracers(value, mask):
            size = p.m
            pairs = [(t * size + x, t * size + (x ^ 1)) for t in range(n) for x in range(size)]
            both = n * size
            pairs += [
                (both + t * size + x, both + (t ^ mask) * size + x)
                for t in range(n)
                for x in range(size)
            ]
            return lax.ppermute(value, ("grp", "ty", "tx"), pairs)

        def edges(value):
            size = p.m
            to = {i: (i + n * size) % (2 * n * size) for i in range(2 * n * size)}
            for tx in range(size - 1):
                for grp in range(2):
                    a = (grp * n + (n - 1 if tx % 2 == 0 else 0)) * size + tx
                    to[a], to[a + 1] = a + 1, a
            return lax.ppermute(value, ("grp", "ty", "tx"), list(to.items()))

        def across(value):
            return lax.ppermute(value, "grp", [(0, 1), (1, 0)])

        flat = view.reshape(p.nf * p.nz * p.rows, p.cols)
        packed = call(
            pack_kernel,
            [sds(SHARED, p.rows, W, LANES)] * n + [sds(G - SHARED, p.rows, W, LANES)] * n,
            [pltpu.with_memory_space_constraint(x, pltpu.HBM) for x in (flat, land_mask, bottom_level, shortwave, absorb)],
            [
                (G, p.rows, LANES + 2 * HALO, LANES),
                pltpu.VMEM(flat.shape, F32),
                pltpu.VMEM(land_mask.shape, jnp.int32),
                pltpu.VMEM(bottom_level.shape, jnp.int32),
                pltpu.VMEM(shortwave.shape, F32),
                pltpu.SMEM(absorb.shape, F32),
                pltpu.SemaphoreType.DMA((5,)),
            ],
            [HBM] * 5,
        )
        got = [packed[0]] + [swap(packed[k], k) for k in range(1, n)]
        got += [packed[n]] + [swap_tracers(packed[n + k], k) for k in range(1, n)]

        size = p.tg * LANES
        mix, weights = call(
            mix_kernel,
            [sds(3 * size, size, dtype=BF16), sds(p.tg, LANES)],
            [pltpu.with_memory_space_constraint(x, pltpu.HBM) for x in (reaction, absorb)],
            [
                (LANES, LANES),
                pltpu.VMEM(reaction.shape, F32),
                pltpu.SMEM(absorb.shape, F32),
                pltpu.SemaphoreType.DMA((2,)),
            ],
            [HBM] * 2,
        )

        z = edges(call(edge_kernel, [sds(G, R, HALO, LANES)], got + [mix], in_specs=[VMEM] * (2 * n) + [ANY])[0])

        padded = (R + 2, p.padded, LANES)
        block = (R, W, LANES)

        def work(count):
            every, cut = (p.tg,) + padded, (p.tg, R, count, LANES)
            scratch = [every, block, block, padded] + [every] * 4
            return scratch + [(p.tg,) + block] + [every] * 2 + [cut] * 2

        dyn1, wet_o, sw_o = call(ocean_first_kernel, [sds(*block)] * 3, got + [z], [padded] * 3)

        dyn1_t = across(dyn1)
        c1, c1_core, wet_t, sw_t = call(
            tracer_first_kernel,
            [sds(p.tg, *block), sds(p.tg, R, p.chunk, LANES), sds(*block), sds(*block)],
            got + [z, weights, mix, dyn1],
            [padded, padded] + work(W),
            [VMEM] * (2 * n + 3) + [ANY],
            cost=4,
        )
        c1_o = across(c1_core)
        back = [sds(G, p.rows, p.chunk, LANES)] * n
        outs = call(
            tracer_second_kernel,
            back,
            [dyn1_t, c1, wet_t, sw_t, weights, mix],
            [padded, (p.tg, R, p.chunk, LANES)] + work(p.chunk),
            cost=4,
        )
        outs = call(
            ocean_second_kernel,
            back,
            [dyn1, c1_o, wet_o, sw_o, weights] + list(outs),
            [padded, padded, block, block],
            aliases={5 + k: k for k in range(n)},
        )
        home = [outs[0]] + [swap(outs[k], k) for k in range(1, n)]
        out = call(unpack_kernel, [sds(p.nf * p.nz * p.rows, p.cols)], home, [(LANES, LANES)])[0]
        return out.reshape((1,) + view.shape)

    in_specs = (
        P("grp", None, None, "ty", "tx"),
        P("ty", "tx"),
        P("ty", "tx"),
        P("ty", "tx"),
        P(),
        P(),
    )
    out_specs = P("grp", None, None, "ty", "tx")
    return jax.shard_map(local, mesh=mesh, in_specs=in_specs, out_specs=out_specs, check_vma=False)
```

```python
import functools

import jax
import jax.numpy as jnp
from jax import lax
from jax.experimental import pallas as pl
from jax.experimental.pallas import tpu as pltpu
from jax.sharding import PartitionSpec as P


STEPS = 2
HALO = 2 * STEPS
LANES = 128
PAD = 8
DYN = 4
SHARED = 2

integration_interval = 0.1
tracer_interval = 0.08
coriolis = 0.8
barotropic_gradient_coefficient = 0.1
water_extinction = 0.04
layer_depth = 0.05
growth_peak = 2.0
half_light = 0.5
ratio_floor = 0.01

F32 = jnp.float32
BF16 = jnp.bfloat16
HIGHEST = lax.Precision.HIGHEST
VMEM = pl.BlockSpec(memory_space=pltpu.VMEM)
SMEM = pl.BlockSpec(memory_space=pltpu.SMEM)
ANY = pl.BlockSpec(memory_space=pl.ANY)
HBM = pl.BlockSpec(memory_space=pltpu.HBM)


def dot(a, b):
    return jnp.dot(a, b, precision=HIGHEST, preferred_element_type=F32)


def iota(shape, dim):
    return lax.broadcasted_iota(jnp.int32, shape, dim)


class Plan:
    def __init__(self, mesh, nf, nz, rows, cols):
        self.n, self.m = mesh.shape["ty"], mesh.shape["tx"]
        self.nf, self.nz, self.rows, self.cols = nf, nz, rows, cols
        assert cols == LANES and LANES % nz == 0 and LANES // nz == DYN
        assert self.n & (self.n - 1) == 0 and self.n > 1
        self.per = LANES // nz
        self.groups = -(-(nf + 1) // self.per)
        self.tg = self.groups - 1
        self.chunk = cols // self.n
        self.width = self.chunk + 2 * HALO
        assert self.width % 8 == 0 and self.chunk % 8 == 0 and self.chunk >= HALO
        self.R = self.n * rows
        self.padded = self.width + 2 * PAD
        self.depth_lane = LANES - nz
        self.sw_lane = LANES - nz // 2

    def ty(self):
        return lax.axis_index("ty")

    def is_ocean(self):
        return lax.axis_index("grp") == 0

    def chunk_of(self, ty):
        odd = lax.rem(lax.axis_index("tx"), 2)
        return jnp.where(odd == 0, ty, self.n - 1 - ty)

    def xor(self, mask):
        ty, out, bit = self.ty(), 0, 1
        while bit < self.n:
            here = lax.rem(lax.div(ty, bit), 2)
            out = out + bit * ((1 - here) if mask & bit else here)
            bit *= 2
        return out


def part(src, mask, g):
    n = len(src) // 2
    return src[mask].at[g] if g < SHARED else src[n + mask].at[g - SHARED]


def pack_kernel(p, *refs):
    given, outs, t_ref, here, sems = refs[:5], refs[5 : 5 + 2 * p.n], refs[5 + 2 * p.n], refs[6 + 2 * p.n : 11 + 2 * p.n], refs[11 + 2 * p.n]
    copies = [pltpu.make_async_copy(a, b, sems.at[i]) for i, (a, b) in enumerate(zip(given, here))]
    for copy in copies:
        copy.start()
    for copy in copies:
        copy.wait()
    view, land, bottom, sw, absorb = here
    nz, rows, step = p.nz, p.rows, p.per * p.nz
    half = nz // 2
    ocean = p.is_ocean()

    def aux(r, upper):
        depth = jnp.where(land[r : r + 1, :] == 1, bottom[r : r + 1, :], 0).astype(F32)
        return jnp.concatenate(
            [
                upper,
                jnp.broadcast_to(depth, (half, LANES)),
                jnp.broadcast_to(sw[r : r + 1, :], (half, LANES)),
            ],
            axis=0,
        )

    def field(r, g, count):
        return view[pl.ds(g * step * rows + r, count, stride=rows), :]

    def put(r, g, block):
        t_ref[g, r, HALO : HALO + LANES, :] = block.T

    def send(count):
        for mask in range(p.n):
            start = pl.multiple_of(p.chunk_of(p.xor(mask)) * p.chunk, 8)
            for g in range(count):
                for r in range(rows):
                    part(outs, mask, g)[r] = t_ref[g, r, pl.ds(start, p.width), :]

    zero = jnp.zeros((HALO, LANES), F32)
    for g in range(p.groups):
        for r in range(rows):
            t_ref[g, r, :HALO, :] = zero
            t_ref[g, r, HALO + LANES :, :] = zero

    @pl.when(jnp.logical_not(ocean))
    def _():
        for r in range(rows):
            for g in range(p.groups - 1):
                put(r, g, field(r, g, step))
            have = (p.nf - p.tg * p.per) * nz
            block = field(r, p.tg, have)
            if have < LANES - nz:
                block = jnp.concatenate([block, jnp.zeros((LANES - nz - have, LANES), F32)], axis=0)
            put(r, p.tg, aux(r, block))
        send(p.groups)

    @pl.when(ocean)
    def _():
        lower = (iota((nz, nz), 0) >= iota((nz, nz), 1)).astype(F32)
        for r in range(rows):
            put(r, 0, field(r, 0, step))
            kd = jnp.full((nz, LANES), water_extinction, F32)
            for t in range(p.nf - DYN):
                kd = kd + absorb[t] * view[pl.ds((DYN + t) * nz * rows + r, nz, stride=rows), :]
            below = sw[r : r + 1, :] * jnp.exp(-layer_depth * dot(lower, kd))
            above = below * jnp.exp(layer_depth * kd)
            forcing = (above - below) / layer_depth
            put(r, 1, aux(r, jnp.concatenate([jnp.zeros((2 * nz, LANES), F32), forcing], axis=0)))
        send(2)


def edge_kernel(p, *refs):
    src, z = refs[: 2 * p.n], refs[2 * p.n + 1]
    left = p.chunk_of(p.ty()) == 0

    def copy(lo):
        for mask in range(p.n):
            base = p.xor(mask) * p.rows
            for g in range(p.groups):
                for r in range(p.rows):
                    z[g, base + r] = part(src, mask, g)[r, lo : lo + HALO, :]

    @pl.when(left)
    def _():
        copy(HALO)

    @pl.when(jnp.logical_not(left))
    def _():
        copy(p.chunk)


def assemble(p, src, z, groups):
    for mask in range(p.n):
        base = p.xor(mask) * p.rows
        for g, dst in groups:
            for r in range(p.rows):
                dst[1 + base + r, PAD : PAD + p.width, :] = part(src, mask, g)[r]
    chunk, tx = p.chunk_of(p.ty()), lax.axis_index("tx")

    @pl.when(chunk == 0)
    def _():
        for g, dst in groups:
            dst[1 : 1 + p.R, PAD : PAD + HALO, :] = jnp.where(tx > 0, z[g], 0.0)

    @pl.when(chunk == p.n - 1)
    def _():
        for g, dst in groups:
            dst[1 : 1 + p.R, PAD + p.width - HALO : PAD + p.width, :] = jnp.where(
                tx < p.m - 1, z[g], 0.0
            )


def aux_fields(p, aux_ref, wet_ref, sw_ref):
    level = (iota((p.width, LANES), 1) % p.nz).astype(F32)
    for r in range(p.R):
        x = aux_ref[1 + r, PAD : PAD + p.width, :]
        wet_ref[r] = (level < x[:, p.depth_lane : p.depth_lane + 1]).astype(F32)
        sw_ref[r] = jnp.broadcast_to(x[:, p.sw_lane : p.sw_lane + 1], (p.width, LANES))


def lanes_of(p, shape, dim):
    i = iota(shape, dim)
    return i // p.nz, i % p.nz


def spread(p, x, slot):
    f, _ = lanes_of(p, x.shape, 1)
    return field_sum(p, jnp.where(f == slot, x, 0.0))


def field_sum(p, x):
    shift = p.nz
    while shift < LANES:
        x = x + pltpu.roll(x, shift, 1)
        shift *= 2
    return x


def level_sum(p, x):
    _, k0 = lanes_of(p, (LANES, LANES), 0)
    _, k1 = lanes_of(p, (LANES, LANES), 1)
    ones = (k0 <= k1).astype(F32).astype(BF16)
    hi = x.astype(BF16)
    rest = x - hi.astype(F32)
    mid = rest.astype(BF16)
    lo = (rest - mid.astype(F32)).astype(BF16)
    return jnp.dot(
        jnp.concatenate([hi, mid, lo], axis=1),
        jnp.concatenate([ones] * 3, axis=0),
        preferred_element_type=F32,
    )


def optical_depth(p, attenuation):
    _, level = lanes_of(p, attenuation.shape, 1)
    plain = (water_extinction * layer_depth) * (level + 1).astype(F32)
    return layer_depth * level_sum(p, attenuation) + plain


def ocean_step(p, d, forcing, wet, out, pp):
    mid = slice(PAD, PAD + p.width)
    flat = jnp.concatenate([d[1 + r, mid, :] for r in range(p.R)], axis=0)
    f, _ = lanes_of(p, flat.shape, 1)
    weight = jnp.where(f == 2, -0.2, jnp.where(f == 3, 0.8, 0.0)) * barotropic_gradient_coefficient
    press = level_sum(p, weight * flat)
    for r in range(p.R):
        pp[1 + r, mid, :] = press[r * p.width : (r + 1) * p.width]
    f, _ = lanes_of(p, (p.width, LANES), 1)
    for r in range(p.R):
        x = d[1 + r, mid, :]
        lap = d[2 + r, mid, :] + d[r, mid, :] + d[1 + r, PAD + 1 : PAD + 1 + p.width, :]
        lap = lap + d[1 + r, PAD - 1 : PAD - 1 + p.width, :] - 4.0 * x
        grad_e = 0.5 * (pp[2 + r, mid, :] - pp[r, mid, :])
        grad_n = 0.5 * (
            pp[1 + r, PAD + 1 : PAD + 1 + p.width, :] - pp[1 + r, PAD - 1 : PAD - 1 + p.width, :]
        )
        of_u = coriolis * pltpu.roll(x, LANES - p.nz, 1) - grad_e
        of_v = -coriolis * pltpu.roll(x, p.nz, 1) - grad_n
        other = jnp.where(f == 2, forcing(r), 0.0)
        extra = jnp.where(f == 0, of_u, jnp.where(f == 1, of_v, other))
        out[r] = wet[r] * (x + integration_interval * (lap + extra))


def clear_pads(p, *refs):
    side = jnp.zeros((PAD, LANES), F32)
    for ref in refs:
        count = ref.shape[0]
        for r in range(count):
            ref[r, :PAD, :] = side
            ref[r, PAD + p.width :, :] = side
        row = jnp.zeros((p.padded, LANES), F32)
        ref[0] = row
        ref[count - 1] = row


def tracer_step(p, d, load_group, wet, sw, absorb, mix, store, scratch, lo, count):
    c, feh, fnh, va, ae, le, an, ln, low, rin, rout, fe, adv = scratch
    R, W = p.R, p.width
    mid = slice(PAD, PAD + W)
    up = slice(PAD + 1, PAD + 1 + W)
    down = slice(PAD - 1, PAD - 1 + W)
    win = slice(PAD + lo, PAD + lo + count)
    none = jnp.zeros((W, LANES), F32)
    for g in range(p.tg):
        for x in (c, ae, le):
            x[g, 0, mid, :] = none
        for x in (c, rin, rout):
            x[g, R + 1, mid, :] = none

    flat = jnp.concatenate([d[1 + r, mid, :] for r in range(R)], axis=0)
    ua = spread(p, flat, 0)
    vv = spread(p, flat, 1)
    for r in range(R):
        va[1 + r, mid, :] = vv[r * W : (r + 1) * W]
    first = lax.axis_index("tx") * p.cols + p.chunk_of(p.ty()) * p.chunk - HALO
    col = first + iota((W, LANES), 0)
    inside = ((col >= 0) & (col + 1 < p.m * p.cols)).astype(F32)
    half = 0.25 * tracer_interval
    for r in range(R):
        if r + 1 < R:
            feh[r] = half * (ua[r * W : (r + 1) * W] + ua[(r + 1) * W : (r + 2) * W])
        else:
            feh[r] = jnp.zeros((W, LANES), F32)
        fnh[r] = half * (va[1 + r, mid, :] + va[1 + r, up, :]) * inside

    def faces(g, r):
        c0 = c[g, 1 + r, mid, :]
        cn = c[g, 1 + r, up, :]
        ce = c[g, 2 + r, mid, :]
        f = feh[r]
        a = jnp.abs(f) * (ce - c0)
        ae[g, 1 + r, mid, :] = a
        le[g, 1 + r, mid, :] = f * (ce + c0) - a
        f = fnh[r]
        a = jnp.abs(f) * (cn - c0)
        an[g, 1 + r, mid, :] = a
        ln[g, 1 + r, mid, :] = f * (cn + c0) - a

    def ratios(g, r):
        c0 = c[g, 1 + r, mid, :]
        cn = c[g, 1 + r, up, :]
        cs = c[g, 1 + r, down, :]
        ce = c[g, 2 + r, mid, :]
        cw = c[g, r, mid, :]
        lw = c0 - (
            le[g, 1 + r, mid, :] - le[g, r, mid, :] + ln[g, 1 + r, mid, :] - ln[g, 1 + r, down, :]
        )
        low[g, r] = lw
        high = jnp.maximum(jnp.maximum(jnp.maximum(c0, ce), jnp.maximum(cw, cn)), cs)
        least = jnp.minimum(jnp.minimum(jnp.minimum(c0, ce), jnp.minimum(cw, cn)), cs)
        e, w = ae[g, 1 + r, mid, :], ae[g, r, mid, :]
        nn, s = an[g, 1 + r, mid, :], an[g, 1 + r, down, :]
        ep, wp, np_, sp = (jnp.maximum(x, 0.0) for x in (e, w, nn, s))
        positive = (ep + wp) + (np_ + sp)
        gain_in = positive - (e + nn)
        gain_out = positive - (w + s)
        floor = ratio_floor * tracer_interval
        rin[g, 1 + r, mid, :] = jnp.minimum(gain_in, jnp.maximum(high - lw, 0.0)) / jnp.maximum(
            gain_in, floor
        )
        rout[g, 1 + r, mid, :] = jnp.minimum(gain_out, jnp.maximum(lw - least, 0.0)) / jnp.maximum(
            gain_out, floor
        )

    def limited(g, r):
        a = an[g, 1 + r, mid, :]
        north = a * jnp.where(
            a >= 0.0,
            jnp.minimum(rin[g, 1 + r, up, :], rout[g, 1 + r, mid, :]),
            jnp.minimum(rin[g, 1 + r, mid, :], rout[g, 1 + r, up, :]),
        )
        ln[g, 1 + r, mid, :] = north
        a = ae[g, 1 + r, win, :]
        east = a * jnp.where(
            a >= 0.0,
            jnp.minimum(rin[g, 2 + r, win, :], rout[g, 1 + r, win, :]),
            jnp.minimum(rin[g, 1 + r, win, :], rout[g, 2 + r, win, :]),
        )
        fe[g, r] = east
        south = ln[g, 1 + r, PAD + lo - 1 : PAD + lo - 1 + count, :]
        div = east + (ln[g, 1 + r, win, :] - south)
        if r:
            div = div - fe[g, r - 1]
        adv[g, r] = low[g, r, lo : lo + count, :] - div

    def column(r0, r1):
        shape = ((r1 - r0) * count, LANES)
        whole = [adv[g, r0:r1].reshape(shape) for g in range(p.tg)]
        att = whole[0] * absorb[0:1, :]
        for g in range(1, p.tg):
            att = att + whole[g] * absorb[g : g + 1, :]
        light = sw[r0:r1, lo : lo + count, :].reshape(shape) * jnp.exp(-optical_depth(p, att))
        x = jnp.concatenate([d[1 + r, win, :] for r in range(r0, r1)], axis=0)
        warm = jnp.exp(0.063 * x) * pltpu.roll(1.0 + 0.2 * jnp.tanh(x), LANES - p.nz, 1)
        growth = (
            (growth_peak * tracer_interval) * spread(p, warm, 2) * light / (light + half_light)
        )
        every = jnp.concatenate(whole, axis=1)
        hi = every.astype(BF16)
        rest = (every - hi.astype(F32)).astype(BF16)
        mixed = jnp.dot(
            jnp.concatenate([hi, rest, hi], axis=1), mix[...], preferred_element_type=F32
        )
        wets = wet[r0:r1, lo : lo + count, :].reshape(shape)
        for g in range(p.tg):
            new = wets * (whole[g] + growth * mixed[:, g * LANES : (g + 1) * LANES])
            store(g, r0, r1, new.reshape(r1 - r0, count, LANES))

    h = (5 * R) // 8
    for g in range(p.tg):
        load_group(g, c.at[g])
        for r in range(h + 1):
            faces(g, r)
        for r in range(h + 1):
            ratios(g, r)
        for r in range(h):
            limited(g, r)
    column(0, h)
    for g in range(p.tg):
        for r in range(h + 1, R):
            faces(g, r)
        for r in range(h + 1, R):
            ratios(g, r)
        for r in range(h, R):
            limited(g, r)
    column(h, R)


def ocean_first_kernel(p, *refs):
    src, z, dyn, wet, sw, d, aux, pp = (refs[: 2 * p.n],) + refs[2 * p.n :]

    @pl.when(p.is_ocean())
    def _():
        clear_pads(p, d, aux, pp)
        assemble(p, src, z, [(0, d), (1, aux)])
        aux_fields(p, aux, wet, sw)
        ocean_step(p, d, lambda r: aux[1 + r, PAD : PAD + p.width, :], wet, dyn, pp)


def tracer_first_kernel(p, *refs):
    src, (z, absorb, mix, _, c1, core, wet, sw, d), scratch = (
        refs[: 2 * p.n],
        refs[2 * p.n : 2 * p.n + 9],
        refs[2 * p.n + 9 :],
    )

    @pl.when(jnp.logical_not(p.is_ocean()))
    def _():
        clear_pads(p, d)
        assemble(p, src, z, [(0, d)] + [(g + 1, scratch[0].at[g]) for g in range(p.tg)])
        aux_fields(p, scratch[0].at[p.tg - 1], wet, sw)

        def load(g, dst):
            pass

        def store(g, r0, r1, value):
            c1[g, r0:r1] = value
            core[g, r0:r1] = c1[g, r0:r1, HALO : HALO + p.chunk, :]

        tracer_step(p, d, load, wet, sw, absorb, mix, store, scratch, 0, p.width)


def load_dyn(p, dyn, d):
    clear_pads(p, d)
    for r in range(p.R):
        d[1 + r, PAD : PAD + p.width, :] = dyn[r]


def put_back(p, outs, group, value):
    for mask in range(p.n):
        outs[mask][group] = value(p.xor(mask) * p.rows)


def tracer_second_kernel(p, *refs):
    dyn, c1, wet, sw, absorb, mix = refs[:6]
    outs, (d, c2), scratch = refs[6 : 6 + p.n], refs[6 + p.n : 8 + p.n], refs[8 + p.n :]
    core = slice(HALO, HALO + p.chunk)

    @pl.when(jnp.logical_not(p.is_ocean()))
    def _():
        load_dyn(p, dyn, d)

        def load(g, dst):
            for r in range(p.R):
                dst[1 + r, PAD : PAD + p.width, :] = c1[g, r]

        def store(g, r0, r1, value):
            c2[g, r0:r1] = value

        tracer_step(p, d, load, wet, sw, absorb, mix, store, scratch, HALO, p.chunk)
        for g in range(p.tg):
            put_back(p, outs, g + 1, lambda row: c2[g, pl.ds(row, p.rows)])
        put_back(p, outs, 0, lambda row: dyn[pl.ds(row, p.rows), core, :])


def ocean_second_kernel(p, *refs):
    dyn, c1, wet, sw, absorb = refs[:5]
    same, outs, (d, pp, heat, dyn2) = refs[5 : 5 + p.n], refs[5 + p.n : 5 + 2 * p.n], refs[5 + 2 * p.n :]
    core = slice(HALO, HALO + p.chunk)

    @pl.when(jnp.logical_not(p.is_ocean()))
    def _():
        for mask in range(p.n):
            outs[mask][...] = same[mask][...]

    @pl.when(p.is_ocean())
    def _():
        load_dyn(p, dyn, d)
        clear_pads(p, pp)
        flat = (p.R * p.chunk, LANES)
        att = c1[0].reshape(flat) * absorb[0:1, :]
        for g in range(1, p.tg):
            att = att + c1[g].reshape(flat) * absorb[g : g + 1, :]
        below = sw[:, core, :].reshape(flat) * jnp.exp(-optical_depth(p, att))
        kd = field_sum(p, att) + water_extinction
        above = below * jnp.exp(layer_depth * kd)
        heat[...] = jnp.zeros(heat.shape, F32)
        heat[:, core, :] = ((above - below) / layer_depth).reshape(p.R, p.chunk, LANES)
        ocean_step(p, d, lambda r: heat[r], wet, dyn2, pp)
        put_back(p, outs, 0, lambda row: dyn2[pl.ds(row, p.rows), core, :])
        for g in range(p.tg):
            put_back(p, outs, g + 1, lambda row: c1[g, pl.ds(row, p.rows)])


def unpack_kernel(p, *refs):
    src, out, t_ref, flat, sems = refs[: p.n], refs[p.n], refs[p.n + 1], refs[p.n + 2], refs[p.n + 3]
    step = p.per * p.nz
    copies = []
    for g in range(p.groups):
        count = min(step, (p.nf - g * p.per) * p.nz)
        for r in range(p.rows):
            for mask in range(p.n):
                start = pl.multiple_of(p.chunk_of(p.xor(mask)) * p.chunk, 8)
                t_ref[g, r, pl.ds(start, p.chunk), :] = src[mask][g, r]
        for r in range(p.rows):
            flat[pl.ds(g * step * p.rows + r, count, stride=p.rows), :] = t_ref[g, r].T[:count]
        at = pl.ds(g * step * p.rows, count * p.rows)
        copy = pltpu.make_async_copy(flat.at[at], out.at[at], sems.at[g])
        copy.start()
        copies.append(copy)
    for copy in copies:
        copy.wait()


def mix_kernel(p, reaction_hbm, absorb_hbm, mix, weights, small, reaction, absorb, sems):
    size = p.tg * LANES
    copies = [
        pltpu.make_async_copy(reaction_hbm, reaction, sems.at[0]),
        pltpu.make_async_copy(absorb_hbm, absorb, sems.at[1]),
    ]
    for copy in copies:
        copy.start()
    for copy in copies:
        copy.wait()
    small[...] = jnp.zeros((LANES, LANES), F32)
    small[: p.nf - DYN, : p.nf - DYN] = reaction[...]
    hi = small[...].astype(BF16)
    lo = (small[...] - hi.astype(F32)).astype(BF16)
    expand = (iota((size, LANES), 0) // p.nz == iota((size, LANES), 1)).astype(F32).astype(BF16)
    same = (iota((LANES, LANES), 0) % p.nz == iota((LANES, LANES), 1) % p.nz).astype(F32)

    def wide(value):
        dims = (((1,), (1,)), ((), ()))
        rows = lax.dot_general(expand, value, dims, preferred_element_type=F32).astype(BF16)
        return lax.dot_general(rows, expand, dims, preferred_element_type=F32)

    for value, starts in ((hi, (0, size)), (lo, (2 * size,))):
        full = wide(value)
        for i in range(p.tg):
            for j in range(p.tg):
                at = slice(j * LANES, (j + 1) * LANES)
                block = (full[i * LANES : (i + 1) * LANES, at] * same).astype(BF16)
                for start in starts:
                    mix[start + i * LANES : start + (i + 1) * LANES, at] = block
    f, _ = lanes_of(p, (1, LANES), 1)
    for g in range(p.tg):
        row = jnp.zeros((1, LANES), F32)
        for k in range(p.per):
            t = g * p.per + k
            if t < p.nf - DYN:
                row = jnp.where(f == k, absorb[t], row)
        weights[g : g + 1, :] = row


def solution(mesh):
    def local(coupled_state, land_mask, bottom_level, shortwave, absorb, reaction):
        view = coupled_state[0]
        p = Plan(mesh, *view.shape)
        n, G, R, W = p.n, p.groups, p.R, p.width

        def sds(*shape, dtype=F32):
            return jax.ShapeDtypeStruct(shape, dtype)

        def call(kernel, outs, ins, scratch=(), in_specs=None, aliases=None, cost=1, out_spec=VMEM):
            return pl.pallas_call(
                functools.partial(kernel, p),
                out_shape=outs,
                in_specs=in_specs or [VMEM] * len(ins),
                out_specs=jax.tree.map(lambda _: out_spec, outs),
                scratch_shapes=[pltpu.VMEM(s, F32) if isinstance(s, tuple) else s for s in scratch],
                input_output_aliases=aliases or {},
                cost_estimate=pl.CostEstimate(
                    flops=cost * 10**8, bytes_accessed=cost * 10**5, transcendentals=0
                ),
                compiler_params=pltpu.CompilerParams(
                    vmem_limit_bytes=(20 if cost > 1 else 10) * 2**20,
                ),
            )(*ins)

        def swap(value, mask):
            return lax.ppermute(value, "ty", [(i, i ^ mask) for i in range(n)])

        def swap_tracers(value, mask):
            size = p.m
            pairs = [(t * size + x, t * size + (x ^ 1)) for t in range(n) for x in range(size)]
            both = n * size
            pairs += [
                (both + t * size + x, both + (t ^ mask) * size + x)
                for t in range(n)
                for x in range(size)
            ]
            return lax.ppermute(value, ("grp", "ty", "tx"), pairs)

        def edges(value):
            size = p.m
            to = {i: (i + n * size) % (2 * n * size) for i in range(2 * n * size)}
            for tx in range(size - 1):
                for grp in range(2):
                    a = (grp * n + (n - 1 if tx % 2 == 0 else 0)) * size + tx
                    to[a], to[a + 1] = a + 1, a
            return lax.ppermute(value, ("grp", "ty", "tx"), list(to.items()))

        def across(value):
            return lax.ppermute(value, "grp", [(0, 1), (1, 0)])

        flat = view.reshape(p.nf * p.nz * p.rows, p.cols)
        packed = call(
            pack_kernel,
            [sds(SHARED, p.rows, W, LANES)] * n + [sds(G - SHARED, p.rows, W, LANES)] * n,
            [pltpu.with_memory_space_constraint(x, pltpu.HBM) for x in (flat, land_mask, bottom_level, shortwave, absorb)],
            [
                (G, p.rows, LANES + 2 * HALO, LANES),
                pltpu.VMEM(flat.shape, F32),
                pltpu.VMEM(land_mask.shape, jnp.int32),
                pltpu.VMEM(bottom_level.shape, jnp.int32),
                pltpu.VMEM(shortwave.shape, F32),
                pltpu.SMEM(absorb.shape, F32),
                pltpu.SemaphoreType.DMA((5,)),
            ],
            [HBM] * 5,
        )
        got = [packed[0]] + [swap(packed[k], k) for k in range(1, n)]
        got += [packed[n]] + [swap_tracers(packed[n + k], k) for k in range(1, n)]

        size = p.tg * LANES
        mix, weights = call(
            mix_kernel,
            [sds(3 * size, size, dtype=BF16), sds(p.tg, LANES)],
            [pltpu.with_memory_space_constraint(x, pltpu.HBM) for x in (reaction, absorb)],
            [
                (LANES, LANES),
                pltpu.VMEM(reaction.shape, F32),
                pltpu.SMEM(absorb.shape, F32),
                pltpu.SemaphoreType.DMA((2,)),
            ],
            [HBM] * 2,
        )

        z = edges(call(edge_kernel, [sds(G, R, HALO, LANES)], got + [mix], in_specs=[VMEM] * (2 * n) + [ANY])[0])

        padded = (R + 2, p.padded, LANES)
        block = (R, W, LANES)

        def work(count):
            every, cut = (p.tg,) + padded, (p.tg, R, count, LANES)
            scratch = [every, block, block, padded] + [every] * 4
            return scratch + [(p.tg,) + block] + [every] * 2 + [cut] * 2

        dyn1, wet_o, sw_o = call(ocean_first_kernel, [sds(*block)] * 3, got + [z], [padded] * 3)

        dyn1_t = across(dyn1)
        c1, c1_core, wet_t, sw_t = call(
            tracer_first_kernel,
            [sds(p.tg, *block), sds(p.tg, R, p.chunk, LANES), sds(*block), sds(*block)],
            got + [z, weights, mix, dyn1],
            [padded] + work(W),
            [VMEM] * (2 * n + 3) + [ANY],
            cost=4,
        )
        c1_o = across(c1_core)
        back = [sds(G, p.rows, p.chunk, LANES)] * n
        outs = call(
            tracer_second_kernel,
            back,
            [dyn1_t, c1, wet_t, sw_t, weights, mix],
            [padded, (p.tg, R, p.chunk, LANES)] + work(p.chunk),
            cost=4,
        )
        outs = call(
            ocean_second_kernel,
            back,
            [dyn1, c1_o, wet_o, sw_o, weights] + list(outs),
            [padded, padded, block, block],
            aliases={5 + k: k for k in range(n)},
        )
        home = [outs[0]] + [swap(outs[k], k) for k in range(1, n)]
        out = call(
            unpack_kernel,
            [sds(p.nf * p.nz * p.rows, p.cols)],
            home,
            [(G, p.rows, LANES, LANES), flat.shape, pltpu.SemaphoreType.DMA((G,))],
            out_spec=HBM,
        )[0]
        return out.reshape((1,) + view.shape)

    in_specs = (
        P("grp", None, None, "ty", "tx"),
        P("ty", "tx"),
        P("ty", "tx"),
        P("ty", "tx"),
        P(),
        P(),
    )
    out_specs = P("grp", None, None, "ty", "tx")
    return jax.shard_map(local, mesh=mesh, in_specs=in_specs, out_specs=out_specs, check_vma=False)
```

```python
import functools

import jax
import jax.numpy as jnp
from jax import lax
from jax.experimental import pallas as pl
from jax.experimental.pallas import tpu as pltpu
from jax.sharding import PartitionSpec as P


STEPS = 2
HALO = 2 * STEPS
LANES = 128
PAD = 8
DYN = 4
SHARED = 2

integration_interval = 0.1
tracer_interval = 0.08
coriolis = 0.8
barotropic_gradient_coefficient = 0.1
water_extinction = 0.04
layer_depth = 0.05
growth_peak = 2.0
half_light = 0.5
ratio_floor = 0.01

F32 = jnp.float32
BF16 = jnp.bfloat16
HIGHEST = lax.Precision.HIGHEST
VMEM = pl.BlockSpec(memory_space=pltpu.VMEM)
SMEM = pl.BlockSpec(memory_space=pltpu.SMEM)
ANY = pl.BlockSpec(memory_space=pl.ANY)
HBM = pl.BlockSpec(memory_space=pltpu.HBM)


def dot(a, b):
    return jnp.dot(a, b, precision=HIGHEST, preferred_element_type=F32)


def iota(shape, dim):
    return lax.broadcasted_iota(jnp.int32, shape, dim)


class Plan:
    def __init__(self, mesh, nf, nz, rows, cols):
        self.n, self.m = mesh.shape["ty"], mesh.shape["tx"]
        self.nf, self.nz, self.rows, self.cols = nf, nz, rows, cols
        assert cols == LANES and LANES % nz == 0 and LANES // nz == DYN
        assert self.n & (self.n - 1) == 0 and self.n > 1
        self.per = LANES // nz
        self.groups = -(-(nf + 1) // self.per)
        self.tg = self.groups - 1
        self.chunk = cols // self.n
        self.width = self.chunk + 2 * HALO
        assert self.width % 8 == 0 and self.chunk % 8 == 0 and self.chunk >= HALO
        self.R = self.n * rows
        self.padded = self.width + 2 * PAD
        self.depth_lane = LANES - nz
        self.sw_lane = LANES - nz // 2

    def ty(self):
        return lax.axis_index("ty")

    def is_ocean(self):
        return lax.axis_index("grp") == 0

    def chunk_of(self, ty):
        odd = lax.rem(lax.axis_index("tx"), 2)
        return jnp.where(odd == 0, ty, self.n - 1 - ty)

    def xor(self, mask):
        ty, out, bit = self.ty(), 0, 1
        while bit < self.n:
            here = lax.rem(lax.div(ty, bit), 2)
            out = out + bit * ((1 - here) if mask & bit else here)
            bit *= 2
        return out


def part(src, mask, g):
    n = len(src) // 2
    return src[mask].at[g] if g < SHARED else src[n + mask].at[g - SHARED]


def pack_kernel(p, *refs):
    given, outs, t_ref, here, sems = refs[:5], refs[5 : 5 + 2 * p.n], refs[5 + 2 * p.n], refs[6 + 2 * p.n : 11 + 2 * p.n], refs[11 + 2 * p.n]
    copies = [pltpu.make_async_copy(a, b, sems.at[i]) for i, (a, b) in enumerate(zip(given, here))]
    for copy in copies:
        copy.start()
    for copy in copies:
        copy.wait()
    view, land, bottom, sw, absorb = here
    nz, rows, step = p.nz, p.rows, p.per * p.nz
    half = nz // 2
    ocean = p.is_ocean()

    def aux(r, upper):
        depth = jnp.where(land[r : r + 1, :] == 1, bottom[r : r + 1, :], 0).astype(F32)
        return jnp.concatenate(
            [
                upper,
                jnp.broadcast_to(depth, (half, LANES)),
                jnp.broadcast_to(sw[r : r + 1, :], (half, LANES)),
            ],
            axis=0,
        )

    def field(r, g, count):
        return view[pl.ds(g * step * rows + r, count, stride=rows), :]

    def put(r, g, block):
        t_ref[g, r, HALO : HALO + LANES, :] = block.T

    def send(count):
        for mask in range(p.n):
            start = pl.multiple_of(p.chunk_of(p.xor(mask)) * p.chunk, 8)
            for g in range(count):
                for r in range(rows):
                    part(outs, mask, g)[r] = t_ref[g, r, pl.ds(start, p.width), :]

    zero = jnp.zeros((HALO, LANES), F32)
    for g in range(p.groups):
        for r in range(rows):
            t_ref[g, r, :HALO, :] = zero
            t_ref[g, r, HALO + LANES :, :] = zero

    @pl.when(jnp.logical_not(ocean))
    def _():
        for r in range(rows):
            for g in range(p.groups - 1):
                put(r, g, field(r, g, step))
            have = (p.nf - p.tg * p.per) * nz
            block = field(r, p.tg, have)
            if have < LANES - nz:
                block = jnp.concatenate([block, jnp.zeros((LANES - nz - have, LANES), F32)], axis=0)
            put(r, p.tg, aux(r, block))
        send(p.groups)

    @pl.when(ocean)
    def _():
        lower = (iota((nz, nz), 0) >= iota((nz, nz), 1)).astype(F32)
        for r in range(rows):
            put(r, 0, field(r, 0, step))
            kd = jnp.full((nz, LANES), water_extinction, F32)
            for t in range(p.nf - DYN):
                kd = kd + absorb[t] * view[pl.ds((DYN + t) * nz * rows + r, nz, stride=rows), :]
            below = sw[r : r + 1, :] * jnp.exp(-layer_depth * dot(lower, kd))
            above = below * jnp.exp(layer_depth * kd)
            forcing = (above - below) / layer_depth
            put(r, 1, aux(r, jnp.concatenate([jnp.zeros((2 * nz, LANES), F32), forcing], axis=0)))
        send(2)


def edge_kernel(p, *refs):
    src, z = refs[: 2 * p.n], refs[2 * p.n + 1]
    left = p.chunk_of(p.ty()) == 0

    def copy(lo):
        for mask in range(p.n):
            base = p.xor(mask) * p.rows
            for g in range(p.groups):
                for r in range(p.rows):
                    z[g, base + r] = part(src, mask, g)[r, lo : lo + HALO, :]

    @pl.when(left)
    def _():
        copy(HALO)

    @pl.when(jnp.logical_not(left))
    def _():
        copy(p.chunk)


def assemble(p, src, z, groups):
    for mask in range(p.n):
        base = p.xor(mask) * p.rows
        for g, dst in groups:
            for r in range(p.rows):
                dst[1 + base + r, PAD : PAD + p.width, :] = part(src, mask, g)[r]
    chunk, tx = p.chunk_of(p.ty()), lax.axis_index("tx")

    @pl.when(chunk == 0)
    def _():
        for g, dst in groups:
            dst[1 : 1 + p.R, PAD : PAD + HALO, :] = jnp.where(tx > 0, z[g], 0.0)

    @pl.when(chunk == p.n - 1)
    def _():
        for g, dst in groups:
            dst[1 : 1 + p.R, PAD + p.width - HALO : PAD + p.width, :] = jnp.where(
                tx < p.m - 1, z[g], 0.0
            )


def aux_fields(p, aux_ref, wet_ref, sw_ref):
    level = (iota((p.width, LANES), 1) % p.nz).astype(F32)
    for r in range(p.R):
        x = aux_ref[1 + r, PAD : PAD + p.width, :]
        wet_ref[r] = (level < x[:, p.depth_lane : p.depth_lane + 1]).astype(F32)
        sw_ref[r] = jnp.broadcast_to(x[:, p.sw_lane : p.sw_lane + 1], (p.width, LANES))


def lanes_of(p, shape, dim):
    i = iota(shape, dim)
    return i // p.nz, i % p.nz


def spread(p, x, slot):
    f, _ = lanes_of(p, x.shape, 1)
    return field_sum(p, jnp.where(f == slot, x, 0.0))


def field_sum(p, x):
    shift = p.nz
    while shift < LANES:
        x = x + pltpu.roll(x, shift, 1)
        shift *= 2
    return x


def level_sum(p, x):
    _, k0 = lanes_of(p, (LANES, LANES), 0)
    _, k1 = lanes_of(p, (LANES, LANES), 1)
    ones = (k0 <= k1).astype(F32).astype(BF16)
    hi = x.astype(BF16)
    rest = x - hi.astype(F32)
    mid = rest.astype(BF16)
    lo = (rest - mid.astype(F32)).astype(BF16)
    return jnp.dot(
        jnp.concatenate([hi, mid, lo], axis=1),
        jnp.concatenate([ones] * 3, axis=0),
        preferred_element_type=F32,
    )


def optical_depth(p, attenuation):
    _, level = lanes_of(p, attenuation.shape, 1)
    plain = (water_extinction * layer_depth) * (level + 1).astype(F32)
    return layer_depth * level_sum(p, attenuation) + plain


def ocean_step(p, d, forcing, wet, out, pp):
    mid = slice(PAD, PAD + p.width)
    flat = jnp.concatenate([d[1 + r, mid, :] for r in range(p.R)], axis=0)
    f, _ = lanes_of(p, flat.shape, 1)
    weight = jnp.where(f == 2, -0.2, jnp.where(f == 3, 0.8, 0.0)) * barotropic_gradient_coefficient
    press = level_sum(p, weight * flat)
    for r in range(p.R):
        pp[1 + r, mid, :] = press[r * p.width : (r + 1) * p.width]
    f, _ = lanes_of(p, (p.width, LANES), 1)
    for r in range(p.R):
        x = d[1 + r, mid, :]
        lap = d[2 + r, mid, :] + d[r, mid, :] + d[1 + r, PAD + 1 : PAD + 1 + p.width, :]
        lap = lap + d[1 + r, PAD - 1 : PAD - 1 + p.width, :] - 4.0 * x
        grad_e = 0.5 * (pp[2 + r, mid, :] - pp[r, mid, :])
        grad_n = 0.5 * (
            pp[1 + r, PAD + 1 : PAD + 1 + p.width, :] - pp[1 + r, PAD - 1 : PAD - 1 + p.width, :]
        )
        of_u = coriolis * pltpu.roll(x, LANES - p.nz, 1) - grad_e
        of_v = -coriolis * pltpu.roll(x, p.nz, 1) - grad_n
        other = jnp.where(f == 2, forcing(r), 0.0)
        extra = jnp.where(f == 0, of_u, jnp.where(f == 1, of_v, other))
        out[r] = wet[r] * (x + integration_interval * (lap + extra))


def clear_pads(p, *refs):
    side = jnp.zeros((PAD, LANES), F32)
    for ref in refs:
        count = ref.shape[0]
        for r in range(count):
            ref[r, :PAD, :] = side
            ref[r, PAD + p.width :, :] = side
        row = jnp.zeros((p.padded, LANES), F32)
        ref[0] = row
        ref[count - 1] = row


def tracer_step(p, d, load_group, wet, sw, absorb, mix, store, scratch, lo, count):
    c, feh, fnh, va, ae, le, an, ln, low, rin, rout, fe, adv = scratch
    R, W = p.R, p.width
    mid = slice(PAD, PAD + W)
    up = slice(PAD + 1, PAD + 1 + W)
    down = slice(PAD - 1, PAD - 1 + W)
    win = slice(PAD + lo, PAD + lo + count)
    none = jnp.zeros((W, LANES), F32)
    for g in range(p.tg):
        for x in (c, ae, le):
            x[g, 0, mid, :] = none
        for x in (c, rin, rout):
            x[g, R + 1, mid, :] = none

    flat = jnp.concatenate([d[1 + r, mid, :] for r in range(R)], axis=0)
    ua = spread(p, flat, 0)
    vv = spread(p, flat, 1)
    for r in range(R):
        va[1 + r, mid, :] = vv[r * W : (r + 1) * W]
    first = lax.axis_index("tx") * p.cols + p.chunk_of(p.ty()) * p.chunk - HALO
    col = first + iota((W, LANES), 0)
    inside = ((col >= 0) & (col + 1 < p.m * p.cols)).astype(F32)
    half = 0.25 * tracer_interval
    for r in range(R):
        if r + 1 < R:
            feh[r] = half * (ua[r * W : (r + 1) * W] + ua[(r + 1) * W : (r + 2) * W])
        else:
            feh[r] = jnp.zeros((W, LANES), F32)
        fnh[r] = half * (va[1 + r, mid, :] + va[1 + r, up, :]) * inside

    def faces(g, r):
        c0 = c[g, 1 + r, mid, :]
        cn = c[g, 1 + r, up, :]
        ce = c[g, 2 + r, mid, :]
        f = feh[r]
        a = jnp.abs(f) * (ce - c0)
        ae[g, 1 + r, mid, :] = a
        le[g, 1 + r, mid, :] = f * (ce + c0) - a
        f = fnh[r]
        a = jnp.abs(f) * (cn - c0)
        an[g, 1 + r, mid, :] = a
        ln[g, 1 + r, mid, :] = f * (cn + c0) - a

    def ratios(g, r):
        c0 = c[g, 1 + r, mid, :]
        cn = c[g, 1 + r, up, :]
        cs = c[g, 1 + r, down, :]
        ce = c[g, 2 + r, mid, :]
        cw = c[g, r, mid, :]
        lw = c0 - (
            le[g, 1 + r, mid, :] - le[g, r, mid, :] + ln[g, 1 + r, mid, :] - ln[g, 1 + r, down, :]
        )
        low[g, r] = lw
        high = jnp.maximum(jnp.maximum(jnp.maximum(c0, ce), jnp.maximum(cw, cn)), cs)
        least = jnp.minimum(jnp.minimum(jnp.minimum(c0, ce), jnp.minimum(cw, cn)), cs)
        e, w = ae[g, 1 + r, mid, :], ae[g, r, mid, :]
        nn, s = an[g, 1 + r, mid, :], an[g, 1 + r, down, :]
        ep, wp, np_, sp = (jnp.maximum(x, 0.0) for x in (e, w, nn, s))
        positive = (ep + wp) + (np_ + sp)
        gain_in = positive - (e + nn)
        gain_out = positive - (w + s)
        floor = ratio_floor * tracer_interval
        rin[g, 1 + r, mid, :] = jnp.minimum(gain_in, jnp.maximum(high - lw, 0.0)) / jnp.maximum(
            gain_in, floor
        )
        rout[g, 1 + r, mid, :] = jnp.minimum(gain_out, jnp.maximum(lw - least, 0.0)) / jnp.maximum(
            gain_out, floor
        )

    def limited(g, r):
        a = an[g, 1 + r, mid, :]
        north = a * jnp.where(
            a >= 0.0,
            jnp.minimum(rin[g, 1 + r, up, :], rout[g, 1 + r, mid, :]),
            jnp.minimum(rin[g, 1 + r, mid, :], rout[g, 1 + r, up, :]),
        )
        ln[g, 1 + r, mid, :] = north
        a = ae[g, 1 + r, win, :]
        east = a * jnp.where(
            a >= 0.0,
            jnp.minimum(rin[g, 2 + r, win, :], rout[g, 1 + r, win, :]),
            jnp.minimum(rin[g, 1 + r, win, :], rout[g, 2 + r, win, :]),
        )
        fe[g, r] = east
        south = ln[g, 1 + r, PAD + lo - 1 : PAD + lo - 1 + count, :]
        div = east + (ln[g, 1 + r, win, :] - south)
        if r:
            div = div - fe[g, r - 1]
        adv[g, r] = low[g, r, lo : lo + count, :] - div

    def column(r0, r1):
        shape = ((r1 - r0) * count, LANES)
        whole = [adv[g, r0:r1].reshape(shape) for g in range(p.tg)]
        att = whole[0] * absorb[0:1, :]
        for g in range(1, p.tg):
            att = att + whole[g] * absorb[g : g + 1, :]
        light = sw[r0:r1, lo : lo + count, :].reshape(shape) * jnp.exp(-optical_depth(p, att))
        x = jnp.concatenate([d[1 + r, win, :] for r in range(r0, r1)], axis=0)
        warm = jnp.exp(0.063 * x) * pltpu.roll(1.0 + 0.2 * jnp.tanh(x), LANES - p.nz, 1)
        growth = (
            (growth_peak * tracer_interval) * spread(p, warm, 2) * light / (light + half_light)
        )
        every = jnp.concatenate(whole, axis=1)
        hi = every.astype(BF16)
        rest = (every - hi.astype(F32)).astype(BF16)
        mixed = jnp.dot(
            jnp.concatenate([hi, rest, hi], axis=1), mix[...], preferred_element_type=F32
        )
        wets = wet[r0:r1, lo : lo + count, :].reshape(shape)
        for g in range(p.tg):
            new = wets * (whole[g] + growth * mixed[:, g * LANES : (g + 1) * LANES])
            store(g, r0, r1, new.reshape(r1 - r0, count, LANES))

    h = (5 * R) // 8
    for g in range(p.tg):
        load_group(g, c.at[g])
        for r in range(h + 1):
            faces(g, r)
        for r in range(h + 1):
            ratios(g, r)
        for r in range(h):
            limited(g, r)
    column(0, h)
    for g in range(p.tg):
        for r in range(h + 1, R):
            faces(g, r)
        for r in range(h + 1, R):
            ratios(g, r)
        for r in range(h, R):
            limited(g, r)
    column(h, R)


def ocean_first_kernel(p, *refs):
    src, z, dyn, wet, sw, d, aux, pp = (refs[: 2 * p.n],) + refs[2 * p.n :]

    @pl.when(p.is_ocean())
    def _():
        clear_pads(p, d, aux, pp)
        assemble(p, src, z, [(0, d), (1, aux)])
        aux_fields(p, aux, wet, sw)
        ocean_step(p, d, lambda r: aux[1 + r, PAD : PAD + p.width, :], wet, dyn, pp)


def tracer_first_kernel(p, *refs):
    src, (z, absorb, mix, dyn, c1, first, core, wet, sw, d), scratch = (
        refs[: 2 * p.n],
        refs[2 * p.n : 2 * p.n + 10],
        refs[2 * p.n + 10 :],
    )

    @pl.when(p.is_ocean())
    def _():
        first[...] = dyn[...]

    @pl.when(jnp.logical_not(p.is_ocean()))
    def _():
        clear_pads(p, d)
        assemble(p, src, z, [(0, d)] + [(g + 1, scratch[0].at[g]) for g in range(p.tg)])
        aux_fields(p, scratch[0].at[p.tg - 1], wet, sw)

        def load(g, dst):
            pass

        def store(g, r0, r1, value):
            c1[g, r0:r1] = value
            if g:
                core[g - 1, r0:r1] = c1[g, r0:r1, HALO : HALO + p.chunk, :]
            else:
                first[r0:r1] = value

        tracer_step(p, d, load, wet, sw, absorb, mix, store, scratch, 0, p.width)


def load_dyn(p, dyn, d):
    clear_pads(p, d)
    for r in range(p.R):
        d[1 + r, PAD : PAD + p.width, :] = dyn[r]


def put_back(p, outs, group, value):
    for mask in range(p.n):
        outs[mask][group] = value(p.xor(mask) * p.rows)


def tracer_second_kernel(p, *refs):
    dyn, c1, wet, sw, absorb, mix = refs[:6]
    outs, (d, c2), scratch = refs[6 : 6 + p.n], refs[6 + p.n : 8 + p.n], refs[8 + p.n :]
    core = slice(HALO, HALO + p.chunk)

    @pl.when(jnp.logical_not(p.is_ocean()))
    def _():
        load_dyn(p, dyn, d)

        def load(g, dst):
            for r in range(p.R):
                dst[1 + r, PAD : PAD + p.width, :] = c1[g, r]

        def store(g, r0, r1, value):
            c2[g, r0:r1] = value

        tracer_step(p, d, load, wet, sw, absorb, mix, store, scratch, HALO, p.chunk)
        for g in range(p.tg):
            put_back(p, outs, g + 1, lambda row: c2[g, pl.ds(row, p.rows)])
        put_back(p, outs, 0, lambda row: dyn[pl.ds(row, p.rows), core, :])


def ocean_second_kernel(p, *refs):
    dyn, first, c1, wet, sw, absorb = refs[:6]
    same, outs, (d, pp, heat, dyn2) = refs[6 : 6 + p.n], refs[6 + p.n : 6 + 2 * p.n], refs[6 + 2 * p.n :]
    core = slice(HALO, HALO + p.chunk)

    @pl.when(jnp.logical_not(p.is_ocean()))
    def _():
        for mask in range(p.n):
            outs[mask][...] = same[mask][...]

    @pl.when(p.is_ocean())
    def _():
        load_dyn(p, dyn, d)
        clear_pads(p, pp)
        flat = (p.R * p.chunk, LANES)
        att = first[:, core, :].reshape(flat) * absorb[0:1, :]
        for g in range(1, p.tg):
            att = att + c1[g - 1].reshape(flat) * absorb[g : g + 1, :]
        below = sw[:, core, :].reshape(flat) * jnp.exp(-optical_depth(p, att))
        kd = field_sum(p, att) + water_extinction
        above = below * jnp.exp(layer_depth * kd)
        heat[...] = jnp.zeros(heat.shape, F32)
        heat[:, core, :] = ((above - below) / layer_depth).reshape(p.R, p.chunk, LANES)
        ocean_step(p, d, lambda r: heat[r], wet, dyn2, pp)
        put_back(p, outs, 0, lambda row: dyn2[pl.ds(row, p.rows), core, :])
        put_back(p, outs, 1, lambda row: first[pl.ds(row, p.rows), core, :])
        for g in range(1, p.tg):
            put_back(p, outs, g + 1, lambda row: c1[g - 1, pl.ds(row, p.rows)])


def unpack_kernel(p, *refs):
    src, out, t_ref, flat, sems = refs[: p.n], refs[p.n], refs[p.n + 1], refs[p.n + 2], refs[p.n + 3]
    step = p.per * p.nz
    copies = []
    for g in range(p.groups):
        count = min(step, (p.nf - g * p.per) * p.nz)
        for r in range(p.rows):
            for mask in range(p.n):
                start = pl.multiple_of(p.chunk_of(p.xor(mask)) * p.chunk, 8)
                t_ref[g, r, pl.ds(start, p.chunk), :] = src[mask][g, r]
        for r in range(p.rows):
            flat[pl.ds(g * step * p.rows + r, count, stride=p.rows), :] = t_ref[g, r].T[:count]
        at = pl.ds(g * step * p.rows, count * p.rows)
        copy = pltpu.make_async_copy(flat.at[at], out.at[at], sems.at[g])
        copy.start()
        copies.append(copy)
    for copy in copies:
        copy.wait()


def mix_kernel(p, reaction_hbm, absorb_hbm, mix, weights, small, reaction, absorb, sems):
    size = p.tg * LANES
    copies = [
        pltpu.make_async_copy(reaction_hbm, reaction, sems.at[0]),
        pltpu.make_async_copy(absorb_hbm, absorb, sems.at[1]),
    ]
    for copy in copies:
        copy.start()
    for copy in copies:
        copy.wait()
    small[...] = jnp.zeros((LANES, LANES), F32)
    small[: p.nf - DYN, : p.nf - DYN] = reaction[...]
    hi = small[...].astype(BF16)
    lo = (small[...] - hi.astype(F32)).astype(BF16)
    expand = (iota((size, LANES), 0) // p.nz == iota((size, LANES), 1)).astype(F32).astype(BF16)
    same = (iota((LANES, LANES), 0) % p.nz == iota((LANES, LANES), 1) % p.nz).astype(F32)

    def wide(value):
        dims = (((1,), (1,)), ((), ()))
        rows = lax.dot_general(expand, value, dims, preferred_element_type=F32).astype(BF16)
        return lax.dot_general(rows, expand, dims, preferred_element_type=F32)

    for value, starts in ((hi, (0, size)), (lo, (2 * size,))):
        full = wide(value)
        for i in range(p.tg):
            for j in range(p.tg):
                at = slice(j * LANES, (j + 1) * LANES)
                block = (full[i * LANES : (i + 1) * LANES, at] * same).astype(BF16)
                for start in starts:
                    mix[start + i * LANES : start + (i + 1) * LANES, at] = block
    f, _ = lanes_of(p, (1, LANES), 1)
    for g in range(p.tg):
        row = jnp.zeros((1, LANES), F32)
        for k in range(p.per):
            t = g * p.per + k
            if t < p.nf - DYN:
                row = jnp.where(f == k, absorb[t], row)
        weights[g : g + 1, :] = row


def solution(mesh):
    def local(coupled_state, land_mask, bottom_level, shortwave, absorb, reaction):
        view = coupled_state[0]
        p = Plan(mesh, *view.shape)
        n, G, R, W = p.n, p.groups, p.R, p.width

        def sds(*shape, dtype=F32):
            return jax.ShapeDtypeStruct(shape, dtype)

        def call(kernel, outs, ins, scratch=(), in_specs=None, aliases=None, cost=1, out_spec=VMEM):
            return pl.pallas_call(
                functools.partial(kernel, p),
                out_shape=outs,
                in_specs=in_specs or [VMEM] * len(ins),
                out_specs=jax.tree.map(lambda _: out_spec, outs),
                scratch_shapes=[pltpu.VMEM(s, F32) if isinstance(s, tuple) else s for s in scratch],
                input_output_aliases=aliases or {},
                cost_estimate=pl.CostEstimate(
                    flops=cost * 10**8, bytes_accessed=cost * 10**5, transcendentals=0
                ),
                compiler_params=pltpu.CompilerParams(
                    vmem_limit_bytes=(20 if cost > 1 else 10) * 2**20,
                ),
            )(*ins)

        def swap(value, mask):
            return lax.ppermute(value, "ty", [(i, i ^ mask) for i in range(n)])

        def swap_tracers(value, mask):
            size = p.m
            pairs = [(t * size + x, t * size + (x ^ 1)) for t in range(n) for x in range(size)]
            both = n * size
            pairs += [
                (both + t * size + x, both + (t ^ mask) * size + x)
                for t in range(n)
                for x in range(size)
            ]
            return lax.ppermute(value, ("grp", "ty", "tx"), pairs)

        def edges(value):
            size = p.m
            to = {i: (i + n * size) % (2 * n * size) for i in range(2 * n * size)}
            for tx in range(size - 1):
                for grp in range(2):
                    a = (grp * n + (n - 1 if tx % 2 == 0 else 0)) * size + tx
                    to[a], to[a + 1] = a + 1, a
            return lax.ppermute(value, ("grp", "ty", "tx"), list(to.items()))

        def across(value):
            return lax.ppermute(value, "grp", [(0, 1), (1, 0)])

        flat = view.reshape(p.nf * p.nz * p.rows, p.cols)
        packed = call(
            pack_kernel,
            [sds(SHARED, p.rows, W, LANES)] * n + [sds(G - SHARED, p.rows, W, LANES)] * n,
            [pltpu.with_memory_space_constraint(x, pltpu.HBM) for x in (flat, land_mask, bottom_level, shortwave, absorb)],
            [
                (G, p.rows, LANES + 2 * HALO, LANES),
                pltpu.VMEM(flat.shape, F32),
                pltpu.VMEM(land_mask.shape, jnp.int32),
                pltpu.VMEM(bottom_level.shape, jnp.int32),
                pltpu.VMEM(shortwave.shape, F32),
                pltpu.SMEM(absorb.shape, F32),
                pltpu.SemaphoreType.DMA((5,)),
            ],
            [HBM] * 5,
        )
        got = [packed[0]] + [swap(packed[k], k) for k in range(1, n)]
        got += [packed[n]] + [swap_tracers(packed[n + k], k) for k in range(1, n)]

        size = p.tg * LANES
        mix, weights = call(
            mix_kernel,
            [sds(3 * size, size, dtype=BF16), sds(p.tg, LANES)],
            [pltpu.with_memory_space_constraint(x, pltpu.HBM) for x in (reaction, absorb)],
            [
                (LANES, LANES),
                pltpu.VMEM(reaction.shape, F32),
                pltpu.SMEM(absorb.shape, F32),
                pltpu.SemaphoreType.DMA((2,)),
            ],
            [HBM] * 2,
        )

        z = edges(call(edge_kernel, [sds(G, R, HALO, LANES)], got + [mix], in_specs=[VMEM] * (2 * n) + [ANY])[0])

        padded = (R + 2, p.padded, LANES)
        block = (R, W, LANES)

        def work(count):
            every, cut = (p.tg,) + padded, (p.tg, R, count, LANES)
            scratch = [every, block, block, padded] + [every] * 4
            return scratch + [(p.tg,) + block] + [every] * 2 + [cut] * 2

        dyn1, wet_o, sw_o = call(ocean_first_kernel, [sds(*block)] * 3, got + [z], [padded] * 3)

        c1, first, c1_core, wet_t, sw_t = call(
            tracer_first_kernel,
            [
                sds(p.tg, *block),
                sds(*block),
                sds(p.tg - 1, R, p.chunk, LANES),
                sds(*block),
                sds(*block),
            ],
            got + [z, weights, mix, dyn1],
            [padded] + work(W),
            [VMEM] * (2 * n + 4),
            cost=4,
        )
        swapped = across(first)
        c1_o = across(c1_core)
        back = [sds(G, p.rows, p.chunk, LANES)] * n
        outs = call(
            tracer_second_kernel,
            back,
            [swapped, c1, wet_t, sw_t, weights, mix],
            [padded, (p.tg, R, p.chunk, LANES)] + work(p.chunk),
            cost=4,
        )
        outs = call(
            ocean_second_kernel,
            back,
            [dyn1, swapped, c1_o, wet_o, sw_o, weights] + list(outs),
            [padded, padded, block, block],
            aliases={6 + k: k for k in range(n)},
        )
        home = [outs[0]] + [swap(outs[k], k) for k in range(1, n)]
        out = call(
            unpack_kernel,
            [sds(p.nf * p.nz * p.rows, p.cols)],
            home,
            [(G, p.rows, LANES, LANES), flat.shape, pltpu.SemaphoreType.DMA((G,))],
            out_spec=HBM,
        )[0]
        return out.reshape((1,) + view.shape)

    in_specs = (
        P("grp", None, None, "ty", "tx"),
        P("ty", "tx"),
        P("ty", "tx"),
        P("ty", "tx"),
        P(),
        P(),
    )
    out_specs = P("grp", None, None, "ty", "tx")
    return jax.shard_map(local, mesh=mesh, in_specs=in_specs, out_specs=out_specs, check_vma=False)
```

```python
import functools

import jax
import jax.numpy as jnp
from jax import lax
from jax.experimental import pallas as pl
from jax.experimental.pallas import tpu as pltpu
from jax.sharding import PartitionSpec as P


STEPS = 2
HALO = 2 * STEPS
LANES = 128
PAD = 8
DYN = 4
SHARED = 2

integration_interval = 0.1
tracer_interval = 0.08
coriolis = 0.8
barotropic_gradient_coefficient = 0.1
water_extinction = 0.04
layer_depth = 0.05
growth_peak = 2.0
half_light = 0.5
ratio_floor = 0.01

F32 = jnp.float32
BF16 = jnp.bfloat16
HIGHEST = lax.Precision.HIGHEST
VMEM = pl.BlockSpec(memory_space=pltpu.VMEM)
SMEM = pl.BlockSpec(memory_space=pltpu.SMEM)
ANY = pl.BlockSpec(memory_space=pl.ANY)
HBM = pl.BlockSpec(memory_space=pltpu.HBM)


def dot(a, b):
    return jnp.dot(a, b, precision=HIGHEST, preferred_element_type=F32)


def iota(shape, dim):
    return lax.broadcasted_iota(jnp.int32, shape, dim)


class Plan:
    def __init__(self, mesh, nf, nz, rows, cols):
        self.n, self.m = mesh.shape["ty"], mesh.shape["tx"]
        self.nf, self.nz, self.rows, self.cols = nf, nz, rows, cols
        assert cols == LANES and LANES % nz == 0 and LANES // nz == DYN
        assert self.n & (self.n - 1) == 0 and self.n > 1
        self.per = LANES // nz
        self.groups = -(-(nf + 1) // self.per)
        self.tg = self.groups - 1
        self.chunk = cols // self.n
        self.width = self.chunk + 2 * HALO
        assert self.width % 8 == 0 and self.chunk % 8 == 0 and self.chunk >= HALO
        self.R = self.n * rows
        self.padded = self.width + 2 * PAD
        self.depth_lane = LANES - nz
        self.sw_lane = LANES - nz // 2

    def ty(self):
        return lax.axis_index("ty")

    def is_ocean(self):
        return lax.axis_index("grp") == 0

    def chunk_of(self, ty):
        odd = lax.rem(lax.axis_index("tx"), 2)
        return jnp.where(odd == 0, ty, self.n - 1 - ty)

    def xor(self, mask):
        ty, out, bit = self.ty(), 0, 1
        while bit < self.n:
            here = lax.rem(lax.div(ty, bit), 2)
            out = out + bit * ((1 - here) if mask & bit else here)
            bit *= 2
        return out


def part(src, mask, g):
    n = len(src) // 2
    return src[mask].at[g] if g < SHARED else src[n + mask].at[g - SHARED]


def pack_kernel(p, *refs):
    given, outs, t_ref, here, sems = refs[:5], refs[5 : 5 + 2 * p.n], refs[5 + 2 * p.n], refs[6 + 2 * p.n : 11 + 2 * p.n], refs[11 + 2 * p.n]
    copies = [pltpu.make_async_copy(a, b, sems.at[i]) for i, (a, b) in enumerate(zip(given, here))]
    for copy in copies:
        copy.start()
    for copy in copies:
        copy.wait()
    view, land, bottom, sw, absorb = here
    nz, rows, step = p.nz, p.rows, p.per * p.nz
    half = nz // 2
    ocean = p.is_ocean()

    def aux(r, upper):
        depth = jnp.where(land[r : r + 1, :] == 1, bottom[r : r + 1, :], 0).astype(F32)
        return jnp.concatenate(
            [
                upper,
                jnp.broadcast_to(depth, (half, LANES)),
                jnp.broadcast_to(sw[r : r + 1, :], (half, LANES)),
            ],
            axis=0,
        )

    def field(r, g, count):
        return view[pl.ds(g * step * rows + r, count, stride=rows), :]

    def put(r, g, block):
        t_ref[g, r, HALO : HALO + LANES, :] = block.T

    def send(count):
        for mask in range(p.n):
            start = pl.multiple_of(p.chunk_of(p.xor(mask)) * p.chunk, 8)
            for g in range(count):
                for r in range(rows):
                    part(outs, mask, g)[r] = t_ref[g, r, pl.ds(start, p.width), :]

    zero = jnp.zeros((HALO, LANES), F32)
    for g in range(p.groups):
        for r in range(rows):
            t_ref[g, r, :HALO, :] = zero
            t_ref[g, r, HALO + LANES :, :] = zero

    @pl.when(jnp.logical_not(ocean))
    def _():
        for r in range(rows):
            for g in range(p.groups - 1):
                put(r, g, field(r, g, step))
            have = (p.nf - p.tg * p.per) * nz
            block = field(r, p.tg, have)
            if have < LANES - nz:
                block = jnp.concatenate([block, jnp.zeros((LANES - nz - have, LANES), F32)], axis=0)
            put(r, p.tg, aux(r, block))
        send(p.groups)

    @pl.when(ocean)
    def _():
        lower = (iota((nz, nz), 0) >= iota((nz, nz), 1)).astype(F32)
        for r in range(rows):
            put(r, 0, field(r, 0, step))
            kd = jnp.full((nz, LANES), water_extinction, F32)
            for t in range(p.nf - DYN):
                kd = kd + absorb[t] * view[pl.ds((DYN + t) * nz * rows + r, nz, stride=rows), :]
            below = sw[r : r + 1, :] * jnp.exp(-layer_depth * dot(lower, kd))
            above = below * jnp.exp(layer_depth * kd)
            forcing = (above - below) / layer_depth
            put(r, 1, aux(r, jnp.concatenate([jnp.zeros((2 * nz, LANES), F32), forcing], axis=0)))
        send(2)


def edge_kernel(p, *refs):
    src, z = refs[: 2 * p.n], refs[2 * p.n + 1]
    left = p.chunk_of(p.ty()) == 0

    def copy(lo):
        for mask in range(p.n):
            base = p.xor(mask) * p.rows
            for g in range(p.groups):
                for r in range(p.rows):
                    z[g, base + r] = part(src, mask, g)[r, lo : lo + HALO, :]

    @pl.when(left)
    def _():
        copy(HALO)

    @pl.when(jnp.logical_not(left))
    def _():
        copy(p.chunk)


def assemble(p, src, z, groups):
    for mask in range(p.n):
        base = p.xor(mask) * p.rows
        for g, dst in groups:
            for r in range(p.rows):
                dst[1 + base + r, PAD : PAD + p.width, :] = part(src, mask, g)[r]
    chunk, tx = p.chunk_of(p.ty()), lax.axis_index("tx")

    @pl.when(chunk == 0)
    def _():
        for g, dst in groups:
            dst[1 : 1 + p.R, PAD : PAD + HALO, :] = jnp.where(tx > 0, z[g], 0.0)

    @pl.when(chunk == p.n - 1)
    def _():
        for g, dst in groups:
            dst[1 : 1 + p.R, PAD + p.width - HALO : PAD + p.width, :] = jnp.where(
                tx < p.m - 1, z[g], 0.0
            )


def aux_fields(p, aux_ref, wet_ref, sw_ref):
    level = (iota((p.width, LANES), 1) % p.nz).astype(F32)
    for r in range(p.R):
        x = aux_ref[1 + r, PAD : PAD + p.width, :]
        wet_ref[r] = (level < x[:, p.depth_lane : p.depth_lane + 1]).astype(F32)
        sw_ref[r] = jnp.broadcast_to(x[:, p.sw_lane : p.sw_lane + 1], (p.width, LANES))


def lanes_of(p, shape, dim):
    i = iota(shape, dim)
    return i // p.nz, i % p.nz


def spread(p, x, slot):
    f, _ = lanes_of(p, x.shape, 1)
    return field_sum(p, jnp.where(f == slot, x, 0.0))


def field_sum(p, x):
    shift = p.nz
    while shift < LANES:
        x = x + pltpu.roll(x, shift, 1)
        shift *= 2
    return x


def level_sum(p, x):
    _, k0 = lanes_of(p, (LANES, LANES), 0)
    _, k1 = lanes_of(p, (LANES, LANES), 1)
    ones = (k0 <= k1).astype(F32).astype(BF16)
    hi = x.astype(BF16)
    rest = x - hi.astype(F32)
    mid = rest.astype(BF16)
    lo = (rest - mid.astype(F32)).astype(BF16)
    return jnp.dot(
        jnp.concatenate([hi, mid, lo], axis=1),
        jnp.concatenate([ones] * 3, axis=0),
        preferred_element_type=F32,
    )


def optical_depth(p, attenuation):
    _, level = lanes_of(p, attenuation.shape, 1)
    plain = (water_extinction * layer_depth) * (level + 1).astype(F32)
    return layer_depth * level_sum(p, attenuation) + plain


def ocean_step(p, d, forcing, wet, out, pp):
    mid = slice(PAD, PAD + p.width)
    flat = jnp.concatenate([d[1 + r, mid, :] for r in range(p.R)], axis=0)
    f, _ = lanes_of(p, flat.shape, 1)
    weight = jnp.where(f == 2, -0.2, jnp.where(f == 3, 0.8, 0.0)) * barotropic_gradient_coefficient
    press = level_sum(p, weight * flat)
    for r in range(p.R):
        pp[1 + r, mid, :] = press[r * p.width : (r + 1) * p.width]
    f, _ = lanes_of(p, (p.width, LANES), 1)
    for r in range(p.R):
        x = d[1 + r, mid, :]
        lap = d[2 + r, mid, :] + d[r, mid, :] + d[1 + r, PAD + 1 : PAD + 1 + p.width, :]
        lap = lap + d[1 + r, PAD - 1 : PAD - 1 + p.width, :] - 4.0 * x
        grad_e = 0.5 * (pp[2 + r, mid, :] - pp[r, mid, :])
        grad_n = 0.5 * (
            pp[1 + r, PAD + 1 : PAD + 1 + p.width, :] - pp[1 + r, PAD - 1 : PAD - 1 + p.width, :]
        )
        of_u = coriolis * pltpu.roll(x, LANES - p.nz, 1) - grad_e
        of_v = -coriolis * pltpu.roll(x, p.nz, 1) - grad_n
        other = jnp.where(f == 2, forcing(r), 0.0)
        extra = jnp.where(f == 0, of_u, jnp.where(f == 1, of_v, other))
        out[r] = wet[r] * (x + integration_interval * (lap + extra))


def clear_pads(p, *refs):
    side = jnp.zeros((PAD, LANES), F32)
    for ref in refs:
        count = ref.shape[0]
        for r in range(count):
            ref[r, :PAD, :] = side
            ref[r, PAD + p.width :, :] = side
        row = jnp.zeros((p.padded, LANES), F32)
        ref[0] = row
        ref[count - 1] = row


def tracer_step(p, d, load_group, wet, sw, absorb, mix, store, scratch, lo, count):
    c, feh, fnh, va, ae, le, an, ln, low, rin, rout, fe, adv = scratch
    R, W = p.R, p.width
    mid = slice(PAD, PAD + W)
    up = slice(PAD + 1, PAD + 1 + W)
    down = slice(PAD - 1, PAD - 1 + W)
    win = slice(PAD + lo, PAD + lo + count)
    none = jnp.zeros((W, LANES), F32)
    for g in range(p.tg):
        for x in (c, ae, le):
            x[g, 0, mid, :] = none
        for x in (c, rin, rout):
            x[g, R + 1, mid, :] = none

    flat = jnp.concatenate([d[1 + r, mid, :] for r in range(R)], axis=0)
    ua = spread(p, flat, 0)
    vv = spread(p, flat, 1)
    for r in range(R):
        va[1 + r, mid, :] = vv[r * W : (r + 1) * W]
    first = lax.axis_index("tx") * p.cols + p.chunk_of(p.ty()) * p.chunk - HALO
    col = first + iota((W, LANES), 0)
    inside = ((col >= 0) & (col + 1 < p.m * p.cols)).astype(F32)
    half = 0.25 * tracer_interval
    for r in range(R):
        if r + 1 < R:
            feh[r] = half * (ua[r * W : (r + 1) * W] + ua[(r + 1) * W : (r + 2) * W])
        else:
            feh[r] = jnp.zeros((W, LANES), F32)
        fnh[r] = half * (va[1 + r, mid, :] + va[1 + r, up, :]) * inside

    def faces(g, r):
        c0 = c[g, 1 + r, mid, :]
        cn = c[g, 1 + r, up, :]
        ce = c[g, 2 + r, mid, :]
        f = feh[r]
        a = jnp.abs(f) * (ce - c0)
        ae[g, 1 + r, mid, :] = a
        le[g, 1 + r, mid, :] = f * (ce + c0) - a
        f = fnh[r]
        a = jnp.abs(f) * (cn - c0)
        an[g, 1 + r, mid, :] = a
        ln[g, 1 + r, mid, :] = f * (cn + c0) - a

    def ratios(g, r):
        c0 = c[g, 1 + r, mid, :]
        cn = c[g, 1 + r, up, :]
        cs = c[g, 1 + r, down, :]
        ce = c[g, 2 + r, mid, :]
        cw = c[g, r, mid, :]
        lw = c0 - (
            le[g, 1 + r, mid, :] - le[g, r, mid, :] + ln[g, 1 + r, mid, :] - ln[g, 1 + r, down, :]
        )
        low[g, r] = lw
        high = jnp.maximum(jnp.maximum(jnp.maximum(c0, ce), jnp.maximum(cw, cn)), cs)
        least = jnp.minimum(jnp.minimum(jnp.minimum(c0, ce), jnp.minimum(cw, cn)), cs)
        e, w = ae[g, 1 + r, mid, :], ae[g, r, mid, :]
        nn, s = an[g, 1 + r, mid, :], an[g, 1 + r, down, :]
        ep, wp, np_, sp = (jnp.maximum(x, 0.0) for x in (e, w, nn, s))
        positive = (ep + wp) + (np_ + sp)
        gain_in = positive - (e + nn)
        gain_out = positive - (w + s)
        floor = ratio_floor * tracer_interval
        rin[g, 1 + r, mid, :] = jnp.minimum(gain_in, jnp.maximum(high - lw, 0.0)) / jnp.maximum(
            gain_in, floor
        )
        rout[g, 1 + r, mid, :] = jnp.minimum(gain_out, jnp.maximum(lw - least, 0.0)) / jnp.maximum(
            gain_out, floor
        )

    def limited(g, r):
        a = an[g, 1 + r, mid, :]
        north = a * jnp.where(
            a >= 0.0,
            jnp.minimum(rin[g, 1 + r, up, :], rout[g, 1 + r, mid, :]),
            jnp.minimum(rin[g, 1 + r, mid, :], rout[g, 1 + r, up, :]),
        )
        ln[g, 1 + r, mid, :] = north
        a = ae[g, 1 + r, win, :]
        east = a * jnp.where(
            a >= 0.0,
            jnp.minimum(rin[g, 2 + r, win, :], rout[g, 1 + r, win, :]),
            jnp.minimum(rin[g, 1 + r, win, :], rout[g, 2 + r, win, :]),
        )
        fe[g, r] = east
        south = ln[g, 1 + r, PAD + lo - 1 : PAD + lo - 1 + count, :]
        div = east + (ln[g, 1 + r, win, :] - south)
        if r:
            div = div - fe[g, r - 1]
        adv[g, r] = low[g, r, lo : lo + count, :] - div

    def column(r0, r1):
        shape = ((r1 - r0) * count, LANES)
        whole = [adv[g, r0:r1].reshape(shape) for g in range(p.tg)]
        att = whole[0] * absorb[0:1, :]
        for g in range(1, p.tg):
            att = att + whole[g] * absorb[g : g + 1, :]
        light = sw[r0:r1, lo : lo + count, :].reshape(shape) * jnp.exp(-optical_depth(p, att))
        x = jnp.concatenate([d[1 + r, win, :] for r in range(r0, r1)], axis=0)
        warm = jnp.exp(0.063 * x) * pltpu.roll(1.0 + 0.2 * jnp.tanh(x), LANES - p.nz, 1)
        growth = (
            (growth_peak * tracer_interval) * spread(p, warm, 2) * light / (light + half_light)
        )
        every = jnp.concatenate(whole, axis=1)
        hi = every.astype(BF16)
        rest = (every - hi.astype(F32)).astype(BF16)
        mixed = jnp.dot(
            jnp.concatenate([hi, rest, hi], axis=1), mix[...], preferred_element_type=F32
        )
        wets = wet[r0:r1, lo : lo + count, :].reshape(shape)
        for g in range(p.tg):
            new = wets * (whole[g] + growth * mixed[:, g * LANES : (g + 1) * LANES])
            store(g, r0, r1, new.reshape(r1 - r0, count, LANES))

    h = R // 2
    for g in range(p.tg):
        load_group(g, c.at[g])
        for r in range(h + 1):
            faces(g, r)
        for r in range(h + 1):
            ratios(g, r)
        for r in range(h):
            limited(g, r)
    column(0, h)
    for g in range(p.tg):
        for r in range(h + 1, R):
            faces(g, r)
        for r in range(h + 1, R):
            ratios(g, r)
        for r in range(h, R):
            limited(g, r)
    column(h, R)


def ocean_first_kernel(p, *refs):
    src, z, dyn, ahead, wet, sw, d, aux, pp = (refs[: 2 * p.n],) + refs[2 * p.n :]

    @pl.when(p.is_ocean())
    def _():
        clear_pads(p, d, aux, pp)
        assemble(p, src, z, [(0, d), (1, aux)])
        aux_fields(p, aux, wet, sw)
        ocean_step(p, d, lambda r: aux[1 + r, PAD : PAD + p.width, :], wet, dyn, pp)
        load_dyn(p, dyn, d)
        ocean_step(p, d, lambda r: jnp.zeros((p.width, LANES), F32), wet, ahead, pp)


def tracer_first_kernel(p, *refs):
    src, (z, absorb, mix, dyn, c1, first, core, wet, sw, d), scratch = (
        refs[: 2 * p.n],
        refs[2 * p.n : 2 * p.n + 10],
        refs[2 * p.n + 10 :],
    )

    @pl.when(p.is_ocean())
    def _():
        first[...] = dyn[...]

    @pl.when(jnp.logical_not(p.is_ocean()))
    def _():
        clear_pads(p, d)
        assemble(p, src, z, [(0, d)] + [(g + 1, scratch[0].at[g]) for g in range(p.tg)])
        aux_fields(p, scratch[0].at[p.tg - 1], wet, sw)

        def load(g, dst):
            pass

        def store(g, r0, r1, value):
            c1[g, r0:r1] = value
            if g:
                core[g - 1, r0:r1] = c1[g, r0:r1, HALO : HALO + p.chunk, :]
            else:
                first[r0:r1] = value

        tracer_step(p, d, load, wet, sw, absorb, mix, store, scratch, 0, p.width)


def load_dyn(p, dyn, d):
    clear_pads(p, d)
    for r in range(p.R):
        d[1 + r, PAD : PAD + p.width, :] = dyn[r]


def put_back(p, outs, group, value):
    for mask in range(p.n):
        outs[mask][group] = value(p.xor(mask) * p.rows)


def tracer_second_kernel(p, *refs):
    dyn, c1, wet, sw, absorb, mix = refs[:6]
    outs, (d, c2), scratch = refs[6 : 6 + p.n], refs[6 + p.n : 8 + p.n], refs[8 + p.n :]
    core = slice(HALO, HALO + p.chunk)

    @pl.when(jnp.logical_not(p.is_ocean()))
    def _():
        load_dyn(p, dyn, d)

        def load(g, dst):
            for r in range(p.R):
                dst[1 + r, PAD : PAD + p.width, :] = c1[g, r]

        def store(g, r0, r1, value):
            c2[g, r0:r1] = value

        tracer_step(p, d, load, wet, sw, absorb, mix, store, scratch, HALO, p.chunk)
        for g in range(p.tg):
            put_back(p, outs, g + 1, lambda row: c2[g, pl.ds(row, p.rows)])
        put_back(p, outs, 0, lambda row: dyn[pl.ds(row, p.rows), core, :])


def ocean_second_kernel(p, *refs):
    ahead, first, c1, wet, sw, absorb = refs[:6]
    same, outs, (dyn2,) = refs[6 : 6 + p.n], refs[6 + p.n : 6 + 2 * p.n], refs[6 + 2 * p.n :]
    core = slice(HALO, HALO + p.chunk)

    @pl.when(jnp.logical_not(p.is_ocean()))
    def _():
        for mask in range(p.n):
            outs[mask][...] = same[mask][...]

    @pl.when(p.is_ocean())
    def _():
        flat = (p.R * p.chunk, LANES)
        att = first[:, core, :].reshape(flat) * absorb[0:1, :]
        for g in range(1, p.tg):
            att = att + c1[g - 1].reshape(flat) * absorb[g : g + 1, :]
        below = sw[:, core, :].reshape(flat) * jnp.exp(-optical_depth(p, att))
        kd = field_sum(p, att) + water_extinction
        above = below * jnp.exp(layer_depth * kd)
        f, _ = lanes_of(p, flat, 1)
        warming = jnp.where(f == 2, (integration_interval / layer_depth) * (above - below), 0.0)
        wets = wet[:, core, :].reshape(flat)
        dyn2[...] = (ahead[:, core, :].reshape(flat) + wets * warming).reshape(dyn2.shape)
        put_back(p, outs, 0, lambda row: dyn2[pl.ds(row, p.rows)])
        put_back(p, outs, 1, lambda row: first[pl.ds(row, p.rows), core, :])
        for g in range(1, p.tg):
            put_back(p, outs, g + 1, lambda row: c1[g - 1, pl.ds(row, p.rows)])


def unpack_kernel(p, *refs):
    src, out, t_ref, flat, sems = refs[: p.n], refs[p.n], refs[p.n + 1], refs[p.n + 2], refs[p.n + 3]
    step = p.per * p.nz
    copies = []
    for g in range(p.groups):
        count = min(step, (p.nf - g * p.per) * p.nz)
        for r in range(p.rows):
            for mask in range(p.n):
                start = pl.multiple_of(p.chunk_of(p.xor(mask)) * p.chunk, 8)
                t_ref[g, r, pl.ds(start, p.chunk), :] = src[mask][g, r]
        for r in range(p.rows):
            flat[pl.ds(g * step * p.rows + r, count, stride=p.rows), :] = t_ref[g, r].T[:count]
        at = pl.ds(g * step * p.rows, count * p.rows)
        copy = pltpu.make_async_copy(flat.at[at], out.at[at], sems.at[g])
        copy.start()
        copies.append(copy)
    for copy in copies:
        copy.wait()


def mix_kernel(p, reaction_hbm, absorb_hbm, mix, weights, small, reaction, absorb, sems):
    size = p.tg * LANES
    copies = [
        pltpu.make_async_copy(reaction_hbm, reaction, sems.at[0]),
        pltpu.make_async_copy(absorb_hbm, absorb, sems.at[1]),
    ]
    for copy in copies:
        copy.start()
    for copy in copies:
        copy.wait()
    small[...] = jnp.zeros((LANES, LANES), F32)
    small[: p.nf - DYN, : p.nf - DYN] = reaction[...]
    hi = small[...].astype(BF16)
    lo = (small[...] - hi.astype(F32)).astype(BF16)
    expand = (iota((size, LANES), 0) // p.nz == iota((size, LANES), 1)).astype(F32).astype(BF16)
    same = (iota((LANES, LANES), 0) % p.nz == iota((LANES, LANES), 1) % p.nz).astype(F32)

    def wide(value):
        dims = (((1,), (1,)), ((), ()))
        rows = lax.dot_general(expand, value, dims, preferred_element_type=F32).astype(BF16)
        return lax.dot_general(rows, expand, dims, preferred_element_type=F32)

    for value, starts in ((hi, (0, size)), (lo, (2 * size,))):
        full = wide(value)
        for i in range(p.tg):
            for j in range(p.tg):
                at = slice(j * LANES, (j + 1) * LANES)
                block = (full[i * LANES : (i + 1) * LANES, at] * same).astype(BF16)
                for start in starts:
                    mix[start + i * LANES : start + (i + 1) * LANES, at] = block
    f, _ = lanes_of(p, (1, LANES), 1)
    for g in range(p.tg):
        row = jnp.zeros((1, LANES), F32)
        for k in range(p.per):
            t = g * p.per + k
            if t < p.nf - DYN:
                row = jnp.where(f == k, absorb[t], row)
        weights[g : g + 1, :] = row


def solution(mesh):
    def local(coupled_state, land_mask, bottom_level, shortwave, absorb, reaction):
        view = coupled_state[0]
        p = Plan(mesh, *view.shape)
        n, G, R, W = p.n, p.groups, p.R, p.width

        def sds(*shape, dtype=F32):
            return jax.ShapeDtypeStruct(shape, dtype)

        def call(kernel, outs, ins, scratch=(), in_specs=None, aliases=None, cost=1, out_spec=VMEM):
            return pl.pallas_call(
                functools.partial(kernel, p),
                out_shape=outs,
                in_specs=in_specs or [VMEM] * len(ins),
                out_specs=jax.tree.map(lambda _: out_spec, outs),
                scratch_shapes=[pltpu.VMEM(s, F32) if isinstance(s, tuple) else s for s in scratch],
                input_output_aliases=aliases or {},
                cost_estimate=pl.CostEstimate(
                    flops=cost * 10**8, bytes_accessed=cost * 10**5, transcendentals=0
                ),
                compiler_params=pltpu.CompilerParams(
                    vmem_limit_bytes=(20 if cost > 1 else 10) * 2**20,
                ),
            )(*ins)

        def swap(value, mask):
            return lax.ppermute(value, "ty", [(i, i ^ mask) for i in range(n)])

        def swap_tracers(value, mask):
            size = p.m
            pairs = [(t * size + x, t * size + (x ^ 1)) for t in range(n) for x in range(size)]
            both = n * size
            pairs += [
                (both + t * size + x, both + (t ^ mask) * size + x)
                for t in range(n)
                for x in range(size)
            ]
            return lax.ppermute(value, ("grp", "ty", "tx"), pairs)

        def edges(value):
            size = p.m
            to = {i: (i + n * size) % (2 * n * size) for i in range(2 * n * size)}
            for tx in range(size - 1):
                for grp in range(2):
                    a = (grp * n + (n - 1 if tx % 2 == 0 else 0)) * size + tx
                    to[a], to[a + 1] = a + 1, a
            return lax.ppermute(value, ("grp", "ty", "tx"), list(to.items()))

        def across(value):
            return lax.ppermute(value, "grp", [(0, 1), (1, 0)])

        flat = view.reshape(p.nf * p.nz * p.rows, p.cols)
        packed = call(
            pack_kernel,
            [sds(SHARED, p.rows, W, LANES)] * n + [sds(G - SHARED, p.rows, W, LANES)] * n,
            [pltpu.with_memory_space_constraint(x, pltpu.HBM) for x in (flat, land_mask, bottom_level, shortwave, absorb)],
            [
                (G, p.rows, LANES + 2 * HALO, LANES),
                pltpu.VMEM(flat.shape, F32),
                pltpu.VMEM(land_mask.shape, jnp.int32),
                pltpu.VMEM(bottom_level.shape, jnp.int32),
                pltpu.VMEM(shortwave.shape, F32),
                pltpu.SMEM(absorb.shape, F32),
                pltpu.SemaphoreType.DMA((5,)),
            ],
            [HBM] * 5,
        )
        got = [packed[0]] + [swap(packed[k], k) for k in range(1, n)]
        got += [packed[n]] + [swap_tracers(packed[n + k], k) for k in range(1, n)]

        size = p.tg * LANES
        mix, weights = call(
            mix_kernel,
            [sds(3 * size, size, dtype=BF16), sds(p.tg, LANES)],
            [pltpu.with_memory_space_constraint(x, pltpu.HBM) for x in (reaction, absorb)],
            [
                (LANES, LANES),
                pltpu.VMEM(reaction.shape, F32),
                pltpu.SMEM(absorb.shape, F32),
                pltpu.SemaphoreType.DMA((2,)),
            ],
            [HBM] * 2,
        )

        z = edges(call(edge_kernel, [sds(G, R, HALO, LANES)], got + [mix], in_specs=[VMEM] * (2 * n) + [ANY])[0])

        padded = (R + 2, p.padded, LANES)
        block = (R, W, LANES)

        def work(count):
            every, cut = (p.tg,) + padded, (p.tg, R, count, LANES)
            scratch = [every, block, block, padded] + [every] * 4
            return scratch + [(p.tg,) + block] + [every] * 2 + [cut] * 2

        dyn1, ahead, wet_o, sw_o = call(
            ocean_first_kernel, [sds(*block)] * 4, got + [z], [padded] * 3
        )

        c1, first, c1_core, wet_t, sw_t = call(
            tracer_first_kernel,
            [
                sds(p.tg, *block),
                sds(*block),
                sds(p.tg - 1, R, p.chunk, LANES),
                sds(*block),
                sds(*block),
            ],
            got + [z, weights, mix, dyn1],
            [padded] + work(W),
            [VMEM] * (2 * n + 4),
            cost=4,
        )
        swapped = across(first)
        c1_o = across(c1_core)
        back = [sds(G, p.rows, p.chunk, LANES)] * n
        outs = call(
            tracer_second_kernel,
            back,
            [swapped, c1, wet_t, sw_t, weights, mix],
            [padded, (p.tg, R, p.chunk, LANES)] + work(p.chunk),
            cost=4,
        )
        outs = call(
            ocean_second_kernel,
            back,
            [ahead, swapped, c1_o, wet_o, sw_o, weights] + list(outs),
            [(R, p.chunk, LANES)],
            aliases={6 + k: k for k in range(n)},
        )
        home = [outs[0]] + [swap(outs[k], k) for k in range(1, n)]
        out = call(
            unpack_kernel,
            [sds(p.nf * p.nz * p.rows, p.cols)],
            home,
            [(G, p.rows, LANES, LANES), flat.shape, pltpu.SemaphoreType.DMA((G,))],
            out_spec=HBM,
        )[0]
        return out.reshape((1,) + view.shape)

    in_specs = (
        P("grp", None, None, "ty", "tx"),
        P("ty", "tx"),
        P("ty", "tx"),
        P("ty", "tx"),
        P(),
        P(),
    )
    out_specs = P("grp", None, None, "ty", "tx")
    return jax.shard_map(local, mesh=mesh, in_specs=in_specs, out_specs=out_specs, check_vma=False)
```
